512 devices in a mesh: region: 64 (over z, x, core), slab: 8 (over y).
Axes of the slice: x: 4, y: 8, z: 8, core: 2. Of those that a mesh axis runs over, the one named last changes fastest.
Arguments:
- features: bfloat16 [131072, 96], P(('region', 'slab')), may hold values from -6 to 6
- neighbours: int32 [131072, 27], P(('region', 'slab')), may hold values from 0 to 2304, as said below
- down_map: int32 [32768, 8], P(('region', 'slab')), may hold values from 0 to 256, as said below
- w_conv: bfloat16 [2592, 96], replicated, may hold values from -0.125 to 0.125
- w_down: bfloat16 [768, 128], replicated, may hold values from -0.21875 to 0.21875
- coarse_grad: bfloat16 [32768, 128], P(('region', 'slab')), may hold values from -6 to 6
Outputs:
- coarse: bfloat16 [32768, 128], P(('region', 'slab'))
- grad_input: float32 [131072, 96], P(('region', 'slab'))
- conv_weight_grad: float32 [2592, 96], replicated
- down_weight_grad: float32 [768, 128], replicated
The draws below stay inside these ranges and needn't reach their ends.
Inputs may be any that keep to these rules, and one draw needn't show every extreme that they name: `neighbours`: device d is the device at region index d // (slab axis size) and slab index d mod (slab axis size). Each device's live voxels are its first slots; dead slots list 9 * 256 everywhere and are named by no one. An entry k * 256 + j names slot j of the device whose region index differs by k // 3 - 1 and slab index by k mod 3 - 1; that device exists. A live voxel names itself at offset 13 (k = 4), and otherwise a live voxel or 2304. When k is not 4, j is below 64, the naming voxel lies in its device's first 64 slots, and some voxel names slot 63 of another device in every draw. 9 * 256 means no source. `down_map`: every live voxel of a device is named exactly once, by a coarse voxel slot of that device, by its slot on the device; all other entries are 256.
All inputs are finite; a program needn't handle non-finite values.
Results may differ from the reference program's by a relative error of at most 0.005.
Values may be sent and summed in bfloat16 or wider, within the bound.
A program may use at most 64 MiB of HBM per device.

```python
import jax
import jax.numpy as jnp
from jax import lax

C = 96
C_OUT = 128
OFFS = 27
DOWN_OFFS = 8
V_DEV = 256
RIM = 64
VC_DEV = 64
NV = 131072
NC = 32768
N_REGION = 64
N_SLAB = 8
DEVICES = 512


def live_counts(key):
    cube = jax.random.randint(jax.random.fold_in(key, 7), (DEVICES,), 0, 65)
    counts = RIM + (V_DEV - RIM) * cube * cube * cube // (64 * 64 * 64)
    fullest = jax.random.randint(jax.random.fold_in(key, 8), (), 0, DEVICES)
    return jnp.where(jnp.arange(DEVICES) == fullest, V_DEV, counts).astype(jnp.int32)


def draw_neighbours(key, part):
    counts = live_counts(key)
    voxel = jnp.arange(NV, dtype=jnp.int32)[:, None]
    device = voxel // V_DEV
    local_idx = voxel % V_DEV
    region = device // N_SLAB
    slab = device % N_SLAB
    offset = jnp.arange(OFFS, dtype=jnp.int32)[None, :]
    step_region = offset // 9 - 1
    step_slab = offset // 3 % 3 - 1
    device_live = counts[device]
    live = local_idx < device_live
    present = jax.random.randint(jax.random.fold_in(key, 11), (NV, OFFS), 0, 5) < 2
    centre = offset == OFFS // 2
    target_region = region + step_region
    target_slab = slab + step_slab
    inside = (target_region >= 0) & (target_region < N_REGION) & (target_slab >= 0) & (target_slab < N_SLAB)
    moving = (step_region != 0) | (step_slab != 0)
    outward_draw = jax.random.randint(jax.random.fold_in(key, 12), (NV, OFFS), 0, 4) == 0
    outward = (local_idx < RIM) & inside & moving & outward_draw
    nearby = jax.random.randint(jax.random.fold_in(key, 13), (NV, OFFS), 0, 1 << 20) % device_live
    remote_slot = jax.random.randint(jax.random.fold_in(key, 14), (NV, OFFS), 0, RIM)
    remote = (target_region * N_SLAB + target_slab) * V_DEV + remote_slot
    value = jnp.where(outward, remote, device * V_DEV + nearby)
    value = jnp.where(centre, voxel, value)
    value = jnp.where(live & (present | centre), value, NV)
    upward = region + 1 < N_REGION
    forced_offset = jnp.where(upward, 21, 3)
    forced_region = jnp.where(upward, region + 1, region - 1)
    forced_target = (forced_region * N_SLAB + slab) * V_DEV + RIM - 1
    value = jnp.where((local_idx == 0) & (offset == forced_offset), forced_target, value)
    target_dev = value // V_DEV
    code = (target_dev // N_SLAB - region + 1) * 3 + (target_dev % N_SLAB - slab + 1)
    encoded = jnp.where(value >= NV, 9 * V_DEV, code * V_DEV + value % V_DEV)
    return encoded.astype(jnp.int32)


def draw_down_map(key, part):
    counts = live_counts(key)
    base = jax.random.fold_in(key, 21)

    def device_map(device):
        order = jax.random.permutation(jax.random.fold_in(base, device), DOWN_OFFS * VC_DEV)
        source = jnp.argsort(order).astype(jnp.int32)
        return jnp.where(source < counts[device], source, V_DEV)
    maps = jax.vmap(device_map)(jnp.arange(DEVICES, dtype=jnp.int32))
    return maps.reshape(NC, DOWN_OFFS).astype(jnp.int32)


def steps_of(own_key, dims, pieces, low, high):
    def one(axis_at, parts):
        steps = jax.random.uniform(jax.random.fold_in(jax.random.fold_in(own_key, 6), axis_at), (parts,), jnp.float32, low / len(pieces), high / len(pieces))
        return jnp.repeat(jnp.exp(steps), dims[axis_at] // parts).reshape((-1,) + (1,) * (len(dims) - axis_at - 1))

    factor_of = one(*pieces[0])
    for cut in pieces[1:]:
        factor_of = factor_of * one(*cut)
    return factor_of


def normal_values(own_key, shape, scale, reach, cuts=(), kind=jnp.bfloat16):
    values = scale * jax.random.normal(own_key, shape, jnp.float32)
    if cuts:
        values = values * steps_of(own_key, shape, cuts, -0.22, 0.18)
    return jnp.clip(values, -reach, reach).astype(kind)


def setup_inputs(seed: int = 0) -> dict:
    keys = jax.random.split(jax.random.key(seed), 7)
    return {
        "features": normal_values(keys[0], (NV, C), 1.0, 6.0, ((0, 512),)),
        "neighbours": draw_neighbours(jax.random.fold_in(keys[6], 71), 0),
        "down_map": draw_down_map(jax.random.fold_in(keys[6], 71), 0),
        "w_conv": normal_values(keys[3], (OFFS * C, C), (OFFS * C) ** -0.5, 0.125),
        "w_down": normal_values(keys[4], (DOWN_OFFS * C, C_OUT), (DOWN_OFFS * C) ** -0.5, 0.21875),
        "coarse_grad": normal_values(keys[5], (NC, C_OUT), 1.0, 6.0, ((0, 512),)),
    }


def reference(features, neighbours, down_map, w_conv, w_down, coarse_grad):
    total, channels = features.shape
    offsets = neighbours.shape[1]
    taps = down_map.shape[1]
    device = (jnp.arange(total, dtype=jnp.int32) // V_DEV)[:, None]
    code = neighbours // V_DEV
    target = device + (code // 3 - 1) * N_SLAB + (code % 3 - 1)
    source = jnp.where(neighbours >= 9 * V_DEV, total, target * V_DEV + neighbours % V_DEV).astype(jnp.int32)
    coarse_dev = (jnp.arange(down_map.shape[0], dtype=jnp.int32) // VC_DEV)[:, None]
    fine = jnp.where(down_map >= V_DEV, total, coarse_dev * V_DEV + down_map).astype(jnp.int32)
    zero_row = jnp.zeros((1, channels), features.dtype)
    table = jnp.concatenate([features, zero_row], axis=0)
    pos_blocks = source.reshape(-1, V_DEV, offsets)

    def conv_block(block_pos):
        rows = table[block_pos].reshape(block_pos.shape[0], offsets * channels)
        return jnp.dot(rows, w_conv, preferred_element_type=jnp.float32)

    conv_out = lax.map(conv_block, pos_blocks).reshape(total, channels)
    hidden = (features.astype(jnp.float32) + jax.nn.silu(conv_out)).astype(jnp.bfloat16)
    hidden_pad = jnp.concatenate([hidden, jnp.zeros((1, channels), hidden.dtype)], axis=0)
    down_blocks = fine.reshape(-1, VC_DEV, taps)
    cotangent_blocks = coarse_grad.reshape(-1, VC_DEV, coarse_grad.shape[1])

    def down_block(carry, inputs):
        hidden_grad, weight_grad = carry
        block_map, block_grad = inputs
        rows = hidden_pad[block_map].reshape(block_map.shape[0], taps * channels)
        result = jnp.dot(rows, w_down, preferred_element_type=jnp.float32).astype(jnp.bfloat16)
        weight_grad = weight_grad + jnp.dot(rows.T, block_grad, preferred_element_type=jnp.float32)
        spread = jnp.dot(block_grad, w_down.T, preferred_element_type=jnp.float32).reshape(-1, channels)
        hidden_grad = hidden_grad.at[block_map.reshape(-1)].add(spread)
        return (hidden_grad, weight_grad), result

    start = (jnp.zeros((total + 1, channels), jnp.float32), jnp.zeros(w_down.shape, jnp.float32))
    (hidden_grad, down_weight_grad), coarse = lax.scan(down_block, start, (down_blocks, cotangent_blocks))
    coarse = coarse.reshape(-1, w_down.shape[1])
    hidden_grad = hidden_grad[:total]
    sigmoid_y = jax.nn.sigmoid(conv_out)
    conv_grad = (hidden_grad * sigmoid_y * (1.0 + conv_out * (1.0 - sigmoid_y))).astype(jnp.bfloat16)
    grad_blocks = conv_grad.reshape(-1, V_DEV, channels)

    def back_block(carry, inputs):
        table_grad, weight_grad = carry
        block_pos, block_grad = inputs
        rows = table[block_pos].reshape(block_pos.shape[0], offsets * channels)
        weight_grad = weight_grad + jnp.dot(rows.T, block_grad, preferred_element_type=jnp.float32)
        spread = jnp.dot(block_grad, w_conv.T, preferred_element_type=jnp.float32).reshape(-1, channels)
        table_grad = table_grad.at[block_pos.reshape(-1)].add(spread)
        return (table_grad, weight_grad), None

    start = (jnp.zeros((total + 1, channels), jnp.float32), jnp.zeros(w_conv.shape, jnp.float32))
    (table_grad, conv_weight_grad), unused = lax.scan(back_block, start, (pos_blocks, grad_blocks))
    grad_input = hidden_grad + table_grad[:total]
    return coarse, grad_input, conv_weight_grad, down_weight_grad
```

```python
import jax
import jax.numpy as jnp
from jax import lax
from jax.experimental import pallas as pl
from jax.experimental.pallas import tpu as pltpu
from jax.sharding import PartitionSpec as P
from jax.experimental import pallas as pl
from jax.experimental.pallas import tpu as pltpu

MESH = pl.DeviceIdType.MESH
HALVINGS = 7
ORDER_A = [0, 4, 7, 1, 5, 8]
ORDER_B = [4, 7, 0, 5, 8, 1]
FULL_A = [2, 6]
FULL_B = [6, 2]


def _bit_partner(region, slab, b):
    if b < 3:
        v = (slab // (1 << b)) % 2
        return v, region, slab + (1 - 2 * v) * (1 << b)
    j = b - 3
    v = (region // (1 << j)) % 2
    return v, region + (1 - 2 * v) * (1 << j), slab


def _step(region, slab, core, ba, bb):
    va, ra, sa = _bit_partner(region, slab, ba)
    vb, rb, sb = _bit_partner(region, slab, bb)
    return va + core * (vb - va), ra + core * (rb - ra), sa + core * (sb - sa)


def allreduce_kernel(x_ref, o_ref, *scratch):
    HALVES = [x_ref.shape[0] >> (k + 1) for k in range(HALVINGS)]
    recvs = scratch[:9]
    send_sem, recv_sem, free_sem = scratch[9], scratch[10], scratch[11]
    region = lax.axis_index("region")
    slab = lax.axis_index("slab")
    core = region % 2
    steps = [(core, region + 1 - 2 * core, slab)]
    for ba, bb in zip(ORDER_A, ORDER_B):
        steps.append(_step(region, slab, core, ba, bb))
    fulls = [_step(region, slab, core, ba, bb) for ba, bb in zip(FULL_A, FULL_B)]

    barrier = pltpu.get_barrier_semaphore()
    for _, r, s in steps + fulls:
        pl.semaphore_signal(barrier, inc=1, device_id=(r, s), device_id_type=MESH)
    pl.semaphore_wait(barrier, len(steps) + len(fulls))

    off = 0
    offs = []
    for k, (v, r, s) in enumerate(steps):
        size = HALVES[k]
        keep = pl.multiple_of(off + v * size, 8)
        send = pl.multiple_of(off + (1 - v) * size, 8)
        src = x_ref if k == 0 else o_ref
        copy = pltpu.make_async_remote_copy(
            src_ref=src.at[pl.ds(send, size)], dst_ref=recvs[k],
            send_sem=send_sem.at[k], recv_sem=recv_sem.at[k],
            device_id=(r, s), device_id_type=MESH)
        copy.start()
        copy.wait()
        pl.semaphore_signal(free_sem.at[k], inc=1, device_id=(r, s), device_id_type=MESH)
        o_ref[pl.ds(keep, size)] = src[pl.ds(keep, size)] + recvs[k][...]
        off = keep
        offs.append(keep)
    last = HALVES[-1]
    for i, (v, r, s) in enumerate(fulls):
        k = len(steps) + i
        copy = pltpu.make_async_remote_copy(
            src_ref=o_ref.at[pl.ds(off, last)], dst_ref=recvs[k],
            send_sem=send_sem.at[k], recv_sem=recv_sem.at[k],
            device_id=(r, s), device_id_type=MESH)
        copy.start()
        copy.wait()
        o_ref[pl.ds(off, last)] = o_ref[pl.ds(off, last)] + recvs[k][...]
    base = len(steps) + len(fulls)
    for k in reversed(range(len(steps))):
        v, r, s = steps[k]
        size = HALVES[k]
        j = base + (len(steps) - 1 - k)
        copy = pltpu.make_async_remote_copy(
            src_ref=o_ref.at[pl.ds(offs[k], size)], dst_ref=o_ref.at[pl.ds(offs[k], size)],
            send_sem=send_sem.at[j], recv_sem=recv_sem.at[j],
            device_id=(r, s), device_id_type=MESH)
        pl.semaphore_wait(free_sem.at[k], 1)
        copy.start()
        copy.wait()


def allreduce(x):
    rows = x.shape[0]
    HALVES = [rows >> (k + 1) for k in range(HALVINGS)]
    n_copies = 9 + 7
    return pl.pallas_call(
        allreduce_kernel,
        out_shape=jax.ShapeDtypeStruct((rows, 128), jnp.float32),
        in_specs=[pl.BlockSpec(memory_space=pltpu.VMEM)],
        out_specs=pl.BlockSpec(memory_space=pltpu.VMEM),
        scratch_shapes=[pltpu.VMEM((h, 128), jnp.float32) for h in HALVES]
        + [pltpu.VMEM((HALVES[-1], 128), jnp.float32)] * 2
        + [pltpu.SemaphoreType.DMA((n_copies,)), pltpu.SemaphoreType.DMA((n_copies,))]
        + [pltpu.SemaphoreType.REGULAR((HALVINGS,))],
        compiler_params=pltpu.CompilerParams(collective_id=0, has_side_effects=True),
    )(x)


def summed_everywhere(arrays):
    flat = jnp.concatenate([a.reshape(-1) for a in arrays])
    unit = 128 * 8 << HALVINGS
    rows = -(-flat.size // unit) * unit // 128
    padded = jnp.pad(flat, (0, rows * 128 - flat.size)).reshape(rows, 128)
    total = allreduce(padded).reshape(-1)
    out, at = [], 0
    for a in arrays:
        out.append(total[at:at + a.size].reshape(a.shape))
        at += a.size
    return out


def extended_2(block, sides, width):
    for axis, dim in sides:
        count = lax.axis_size(axis)
        forward = [(i, i + 1) for i in range(count - 1)]
        backward = [(target, source) for source, target in forward]
        low = lax.ppermute(
            lax.slice_in_dim(block, block.shape[dim] - width, None, axis=dim), axis, forward
        )
        high = lax.ppermute(lax.slice_in_dim(block, 0, width, axis=dim), axis, backward)
        block = jnp.concatenate([low, block, high], axis=dim)
    return block


def on_device(features, neighbours, down_map, w_conv, w_down, coarse_grad):
    voxels, channels = features.shape
    offsets = neighbours.shape[1]
    absent = neighbours >= 9 * voxels
    slot_idx = neighbours // voxels
    local_idx = neighbours - slot_idx * voxels
    zero_row = jnp.zeros((1, channels), features.dtype)
    sendable = features.reshape(1, 1, voxels * channels // 128, 128)
    extended = extended_2(sendable, (("region", 0), ("slab", 1)), 1)
    table = jnp.concatenate([extended.reshape(9 * voxels, channels), zero_row], axis=0)
    positions = jnp.where(absent, 9 * voxels, slot_idx * voxels + local_idx)
    row_block = min(voxels, 512)
    block_count = voxels // row_block
    pos_blocks = positions.reshape(block_count, row_block, offsets)

    def conv_block(block_pos):
        rows = table[block_pos].reshape(row_block, offsets * channels)
        return jnp.dot(rows, w_conv, preferred_element_type=jnp.float32)

    conv_out = lax.map(conv_block, pos_blocks).reshape(voxels, channels)
    hidden = (features.astype(jnp.float32) + jax.nn.silu(conv_out)).astype(jnp.bfloat16)
    coarse_count, taps = down_map.shape
    down_local = jnp.minimum(down_map, voxels)
    hidden_pad = jnp.concatenate([hidden, zero_row], axis=0)
    coarse_rows = hidden_pad[down_local].reshape(coarse_count, taps * channels)
    coarse = jnp.dot(coarse_rows, w_down, preferred_element_type=jnp.float32).astype(jnp.bfloat16)
    coarse_back = jnp.dot(coarse_grad, w_down.T, preferred_element_type=jnp.float32)
    hidden_grad = jnp.zeros((voxels + 1, channels), jnp.float32)
    hidden_grad = hidden_grad.at[down_local.reshape(-1)].add(coarse_back.reshape(-1, channels))[
        :voxels
    ]
    down_wgrad = lax.dot_general(
        coarse_rows, coarse_grad, (((0,), (0,)), ((), ())), preferred_element_type=jnp.float32
    )
    sigmoid_y = jax.nn.sigmoid(conv_out)
    conv_grad = (hidden_grad * sigmoid_y * (1.0 + conv_out * (1.0 - sigmoid_y))).astype(
        jnp.bfloat16
    )
    grad_blocks = conv_grad.reshape(block_count, row_block, channels)

    def back_block(carry, inputs):
        table_grad, weight_grad = carry
        block_pos, block_grad = inputs
        rows = table[block_pos].reshape(row_block, offsets * channels)
        weight_grad = weight_grad + lax.dot_general(
            rows, block_grad, (((0,), (0,)), ((), ())), preferred_element_type=jnp.float32
        )
        spread = jnp.dot(block_grad, w_conv.T, preferred_element_type=jnp.float32).reshape(
            -1, channels
        )
        table_grad = table_grad.at[block_pos.reshape(-1)].add(spread)
        return ((table_grad, weight_grad), None)

    start = (
        jnp.zeros((table.shape[0], channels), jnp.float32),
        jnp.zeros(w_conv.shape, jnp.float32),
    )
    (table_grad, conv_wgrad), unused = lax.scan(back_block, start, (pos_blocks, grad_blocks))
    conv_wgrad, down_wgrad = summed_everywhere([conv_wgrad, down_wgrad])
    sections = table_grad[: 9 * voxels].reshape(3, 3, voxels, channels)
    own_part = sections[1, 1]
    outgoing = sections.at[1, 1].set(0.0).reshape(3, 3, voxels * channels // 128, 128)
    returned = extended_2(outgoing.astype(jnp.bfloat16), (("region", 0), ("slab", 1)), 1).astype(
        outgoing.dtype
    )
    returned = returned.reshape(5, 5, voxels, channels)
    incoming = jnp.sum(returned[0::2, 0::2], axis=(0, 1))
    grad_input = hidden_grad + own_part + incoming
    return (coarse, grad_input, conv_wgrad, down_wgrad)


def solution(mesh):
    in_specs = (
        P(("region", "slab"), None),
        P(("region", "slab"), None),
        P(("region", "slab"), None),
        P(),
        P(),
        P(("region", "slab"), None),
    )
    out_specs = (P(("region", "slab"), None), P(("region", "slab"), None), P(), P())
    return jax.shard_map(
        on_device, mesh=mesh, in_specs=in_specs, out_specs=out_specs, check_vma=False
    )
```

```python
import jax
import jax.numpy as jnp
from jax import lax
from jax.experimental import pallas as pl
from jax.experimental.pallas import tpu as pltpu
from jax.sharding import PartitionSpec as P
from jax.experimental import pallas as pl
from jax.experimental.pallas import tpu as pltpu

MESH = pl.DeviceIdType.MESH
HALVINGS = 7
ORDER_A = [0, 4, 7, 1, 5, 8]
ORDER_B = [4, 7, 0, 5, 8, 1]
FULL_A = [2, 6]
FULL_B = [6, 2]


def _bit_partner(region, slab, b):
    if b < 3:
        v = (slab // (1 << b)) % 2
        return v, region, slab + (1 - 2 * v) * (1 << b)
    j = b - 3
    v = (region // (1 << j)) % 2
    return v, region + (1 - 2 * v) * (1 << j), slab


def _step(region, slab, core, ba, bb):
    va, ra, sa = _bit_partner(region, slab, ba)
    vb, rb, sb = _bit_partner(region, slab, bb)
    return va + core * (vb - va), ra + core * (rb - ra), sa + core * (sb - sa)


def allreduce_kernel(x_ref, o_ref, *scratch):
    HALVES = [x_ref.shape[0] >> (k + 1) for k in range(HALVINGS)]
    recvs = scratch[:9]
    send_sem, recv_sem, free_sem = scratch[9], scratch[10], scratch[11]
    region = lax.axis_index("region")
    slab = lax.axis_index("slab")
    core = region % 2
    steps = [(core, region + 1 - 2 * core, slab)]
    for ba, bb in zip(ORDER_A, ORDER_B):
        steps.append(_step(region, slab, core, ba, bb))
    fulls = [_step(region, slab, core, ba, bb) for ba, bb in zip(FULL_A, FULL_B)]

    barrier = pltpu.get_barrier_semaphore()
    for _, r, s in steps + fulls:
        pl.semaphore_signal(barrier, inc=1, device_id=(r, s), device_id_type=MESH)
    pl.semaphore_wait(barrier, len(steps) + len(fulls))

    off = 0
    offs = []
    for k, (v, r, s) in enumerate(steps):
        size = HALVES[k]
        keep = pl.multiple_of(off + v * size, 8)
        send = pl.multiple_of(off + (1 - v) * size, 8)
        src = x_ref if k == 0 else o_ref
        copy = pltpu.make_async_remote_copy(
            src_ref=src.at[pl.ds(send, size)], dst_ref=recvs[k],
            send_sem=send_sem.at[k], recv_sem=recv_sem.at[k],
            device_id=(r, s), device_id_type=MESH)
        copy.start()
        copy.wait()
        pl.semaphore_signal(free_sem.at[k], inc=1, device_id=(r, s), device_id_type=MESH)
        o_ref[pl.ds(keep, size)] = src[pl.ds(keep, size)] + recvs[k][...]
        off = keep
        offs.append(keep)
    last = HALVES[-1]
    for i, (v, r, s) in enumerate(fulls):
        k = len(steps) + i
        copy = pltpu.make_async_remote_copy(
            src_ref=o_ref.at[pl.ds(off, last)], dst_ref=recvs[k],
            send_sem=send_sem.at[k], recv_sem=recv_sem.at[k],
            device_id=(r, s), device_id_type=MESH)
        copy.start()
        copy.wait()
        o_ref[pl.ds(off, last)] = o_ref[pl.ds(off, last)] + recvs[k][...]
    base = len(steps) + len(fulls)
    for k in reversed(range(len(steps))):
        v, r, s = steps[k]
        size = HALVES[k]
        j = base + (len(steps) - 1 - k)
        copy = pltpu.make_async_remote_copy(
            src_ref=o_ref.at[pl.ds(offs[k], size)], dst_ref=o_ref.at[pl.ds(offs[k], size)],
            send_sem=send_sem.at[j], recv_sem=recv_sem.at[j],
            device_id=(r, s), device_id_type=MESH)
        pl.semaphore_wait(free_sem.at[k], 1)
        copy.start()
        copy.wait()


def allreduce(x):
    rows = x.shape[0]
    HALVES = [rows >> (k + 1) for k in range(HALVINGS)]
    n_copies = 9 + 7
    return pl.pallas_call(
        allreduce_kernel,
        out_shape=jax.ShapeDtypeStruct((rows, 128), jnp.float32),
        in_specs=[pl.BlockSpec(memory_space=pltpu.VMEM)],
        out_specs=pl.BlockSpec(memory_space=pltpu.VMEM),
        scratch_shapes=[pltpu.VMEM((h, 128), jnp.float32) for h in HALVES]
        + [pltpu.VMEM((HALVES[-1], 128), jnp.float32)] * 2
        + [pltpu.SemaphoreType.DMA((n_copies,)), pltpu.SemaphoreType.DMA((n_copies,))]
        + [pltpu.SemaphoreType.REGULAR((HALVINGS,))],
        compiler_params=pltpu.CompilerParams(collective_id=0, has_side_effects=True),
    )(x)


def summed_everywhere(arrays):
    flat = jnp.concatenate([a.reshape(-1) for a in arrays])
    unit = 128 * 8 << HALVINGS
    rows = -(-flat.size // unit) * unit // 128
    padded = jnp.pad(flat, (0, rows * 128 - flat.size)).reshape(rows, 128)
    total = allreduce(padded).reshape(-1)
    out, at = [], 0
    for a in arrays:
        out.append(total[at:at + a.size].reshape(a.shape))
        at += a.size
    return out


def extended_2(block, sides, width):
    for axis, dim in sides:
        count = lax.axis_size(axis)
        forward = [(i, i + 1) for i in range(count - 1)]
        backward = [(target, source) for source, target in forward]
        low = lax.ppermute(
            lax.slice_in_dim(block, block.shape[dim] - width, None, axis=dim), axis, forward
        )
        high = lax.ppermute(lax.slice_in_dim(block, 0, width, axis=dim), axis, backward)
        block = jnp.concatenate([low, block, high], axis=dim)
    return block


def _one_hot(pos_ref, o, rows):
    column = pos_ref[:, o:o + 1]
    lanes = lax.broadcasted_iota(jnp.int32, (column.shape[0], rows), 1)
    return (column == lanes).astype(jnp.bfloat16)


def conv_fwd_kernel(pos_ref, table_ref, w_ref, out_ref):
    channels = table_ref.shape[1]
    table = table_ref[...]
    total = jnp.zeros(out_ref.shape, jnp.float32)
    for o in range(pos_ref.shape[1]):
        picked = jnp.dot(_one_hot(pos_ref, o, table.shape[0]), table, preferred_element_type=jnp.float32)
        weight = w_ref[o * channels:(o + 1) * channels, :]
        total = total + jnp.dot(picked.astype(jnp.bfloat16), weight, preferred_element_type=jnp.float32)
    out_ref[...] = total


def conv_bwd_kernel(pos_ref, table_ref, grad_ref, w_ref, tgrad_ref, wgrad_ref):
    channels = table_ref.shape[1]
    table = table_ref[...]
    grad = grad_ref[...]
    back = (((0,), (0,)), ((), ()))
    total = jnp.zeros(tgrad_ref.shape, jnp.float32)
    for o in range(pos_ref.shape[1]):
        hot = _one_hot(pos_ref, o, table.shape[0])
        picked = jnp.dot(hot, table, preferred_element_type=jnp.float32).astype(jnp.bfloat16)
        wgrad_ref[o * channels:(o + 1) * channels, :] = lax.dot_general(
            picked, grad, back, preferred_element_type=jnp.float32)
        weight = w_ref[o * channels:(o + 1) * channels, :]
        spread = lax.dot_general(grad, weight, (((1,), (1,)), ((), ())), preferred_element_type=jnp.float32)
        high = spread.astype(jnp.bfloat16)
        low = (spread - high.astype(jnp.float32)).astype(jnp.bfloat16)
        total = total + lax.dot_general(hot, high, back, preferred_element_type=jnp.float32)
        total = total + lax.dot_general(hot, low, back, preferred_element_type=jnp.float32)
    tgrad_ref[...] = total


def _vmem_call(kernel, outs, *args):
    return pl.pallas_call(
        kernel,
        out_shape=outs,
        in_specs=[pl.BlockSpec(memory_space=pltpu.VMEM)] * len(args),
        out_specs=jax.tree.map(lambda _: pl.BlockSpec(memory_space=pltpu.VMEM), outs),
    )(*args)


def on_device(features, neighbours, down_map, w_conv, w_down, coarse_grad):
    voxels, channels = features.shape
    offsets = neighbours.shape[1]
    rim = 64
    absent = neighbours >= 9 * voxels
    slot_idx = neighbours // voxels
    local_idx = neighbours - slot_idx * voxels
    halo_slot = jnp.where(slot_idx < 4, slot_idx, slot_idx - 1)
    compact = jnp.where(slot_idx == 4, 8 * rim + local_idx, halo_slot * rim + local_idx)
    positions = jnp.where(absent, -1, compact).astype(jnp.int32)
    sendable = features[:rim].reshape(1, 1, rim * channels // 128, 128)
    extended = extended_2(sendable, (("region", 0), ("slab", 1)), 1).reshape(9, rim, channels)
    halo = jnp.concatenate([extended[:4], extended[5:]], axis=0).reshape(8 * rim, channels)
    table = jnp.concatenate([halo, features], axis=0)
    table_rows = table.shape[0]

    conv_out = _vmem_call(
        conv_fwd_kernel, jax.ShapeDtypeStruct((voxels, channels), jnp.float32), positions, table, w_conv)
    hidden = (features.astype(jnp.float32) + jax.nn.silu(conv_out)).astype(jnp.bfloat16)
    zero_row = jnp.zeros((1, channels), features.dtype)
    coarse_count, taps = down_map.shape
    down_local = jnp.minimum(down_map, voxels)
    hidden_pad = jnp.concatenate([hidden, zero_row], axis=0)
    coarse_rows = hidden_pad[down_local].reshape(coarse_count, taps * channels)
    coarse = jnp.dot(coarse_rows, w_down, preferred_element_type=jnp.float32).astype(jnp.bfloat16)
    coarse_back = jnp.dot(coarse_grad, w_down.T, preferred_element_type=jnp.float32)
    hidden_grad = jnp.zeros((voxels + 1, channels), jnp.float32)
    hidden_grad = hidden_grad.at[down_local.reshape(-1)].add(coarse_back.reshape(-1, channels))[
        :voxels
    ]
    down_wgrad = lax.dot_general(
        coarse_rows, coarse_grad, (((0,), (0,)), ((), ())), preferred_element_type=jnp.float32
    )
    sigmoid_y = jax.nn.sigmoid(conv_out)
    conv_grad = (hidden_grad * sigmoid_y * (1.0 + conv_out * (1.0 - sigmoid_y))).astype(
        jnp.bfloat16
    )
    table_grad, conv_wgrad = _vmem_call(
        conv_bwd_kernel,
        (jax.ShapeDtypeStruct((table_rows, channels), jnp.float32),
         jax.ShapeDtypeStruct(w_conv.shape, jnp.float32)),
        positions, table, conv_grad, w_conv)
    conv_wgrad, down_wgrad = summed_everywhere([conv_wgrad, down_wgrad])
    own_part = table_grad[8 * rim:]
    halo_grad = table_grad[: 8 * rim].reshape(8, rim, channels)
    sections = jnp.concatenate(
        [halo_grad[:4], jnp.zeros((1, rim, channels), jnp.float32), halo_grad[4:]], axis=0)
    outgoing = sections.reshape(3, 3, rim * channels // 128, 128)
    returned = extended_2(outgoing.astype(jnp.bfloat16), (("region", 0), ("slab", 1)), 1).astype(
        outgoing.dtype
    )
    returned = returned.reshape(5, 5, rim, channels)
    incoming = jnp.sum(returned[0::2, 0::2], axis=(0, 1))
    grad_input = hidden_grad + own_part
    grad_input = grad_input.at[:rim].add(incoming)
    return (coarse, grad_input, conv_wgrad, down_wgrad)


def solution(mesh):
    in_specs = (
        P(("region", "slab"), None),
        P(("region", "slab"), None),
        P(("region", "slab"), None),
        P(),
        P(),
        P(("region", "slab"), None),
    )
    out_specs = (P(("region", "slab"), None), P(("region", "slab"), None), P(), P())
    return jax.shard_map(
        on_device, mesh=mesh, in_specs=in_specs, out_specs=out_specs, check_vma=False
    )
```

```python
import jax
import jax.numpy as jnp
from jax import lax
from jax.experimental import pallas as pl
from jax.experimental.pallas import tpu as pltpu
from jax.sharding import PartitionSpec as P
from jax.experimental import pallas as pl
from jax.experimental.pallas import tpu as pltpu

MESH = pl.DeviceIdType.MESH
HALVINGS = 7
ORDER_A = [0, 4, 7, 1, 5, 8]
ORDER_B = [4, 7, 0, 5, 8, 1]
FULL_A = [2, 6]
FULL_B = [6, 2]


def _bit_partner(region, slab, b):
    if b < 3:
        v = (slab // (1 << b)) % 2
        return v, region, slab + (1 - 2 * v) * (1 << b)
    j = b - 3
    v = (region // (1 << j)) % 2
    return v, region + (1 - 2 * v) * (1 << j), slab


def _step(region, slab, core, ba, bb):
    va, ra, sa = _bit_partner(region, slab, ba)
    vb, rb, sb = _bit_partner(region, slab, bb)
    return va + core * (vb - va), ra + core * (rb - ra), sa + core * (sb - sa)


def allreduce_kernel(x_ref, o_ref, *scratch):
    HALVES = [x_ref.shape[0] >> (k + 1) for k in range(HALVINGS)]
    recvs = scratch[:9]
    send_sem, recv_sem, free_sem = scratch[9], scratch[10], scratch[11]
    region = lax.axis_index("region")
    slab = lax.axis_index("slab")
    core = region % 2
    steps = [(core, region + 1 - 2 * core, slab)]
    for ba, bb in zip(ORDER_A, ORDER_B):
        steps.append(_step(region, slab, core, ba, bb))
    fulls = [_step(region, slab, core, ba, bb) for ba, bb in zip(FULL_A, FULL_B)]

    barrier = pltpu.get_barrier_semaphore()
    for _, r, s in steps + fulls:
        pl.semaphore_signal(barrier, inc=1, device_id=(r, s), device_id_type=MESH)
    pl.semaphore_wait(barrier, len(steps) + len(fulls))

    off = 0
    offs = []
    pending = []

    def settle(copy, k, r, s):
        copy.wait_send()
        pl.semaphore_signal(free_sem.at[k], inc=1, device_id=(r, s), device_id_type=MESH)

    for k, (v, r, s) in enumerate(steps):
        size = HALVES[k]
        keep = pl.multiple_of(off + v * size, 8)
        send = pl.multiple_of(off + (1 - v) * size, 8)
        src = x_ref if k == 0 else o_ref
        copy = pltpu.make_async_remote_copy(
            src_ref=src.at[pl.ds(send, size)], dst_ref=recvs[k],
            send_sem=send_sem.at[k], recv_sem=recv_sem.at[k],
            device_id=(r, s), device_id_type=MESH)
        copy.start()
        if pending:
            settle(*pending.pop())
        copy.wait_recv()
        o_ref[pl.ds(keep, size)] = src[pl.ds(keep, size)] + recvs[k][...]
        pending.append((copy, k, r, s))
        off = keep
        offs.append(keep)
    settle(*pending.pop())
    last = HALVES[-1]
    for i, (v, r, s) in enumerate(fulls):
        k = len(steps) + i
        copy = pltpu.make_async_remote_copy(
            src_ref=o_ref.at[pl.ds(off, last)], dst_ref=recvs[k],
            send_sem=send_sem.at[k], recv_sem=recv_sem.at[k],
            device_id=(r, s), device_id_type=MESH)
        copy.start()
        copy.wait()
        o_ref[pl.ds(off, last)] = o_ref[pl.ds(off, last)] + recvs[k][...]
    base = len(steps) + len(fulls)
    sent = []
    for k in reversed(range(len(steps))):
        v, r, s = steps[k]
        size = HALVES[k]
        j = base + (len(steps) - 1 - k)
        copy = pltpu.make_async_remote_copy(
            src_ref=o_ref.at[pl.ds(offs[k], size)], dst_ref=o_ref.at[pl.ds(offs[k], size)],
            send_sem=send_sem.at[j], recv_sem=recv_sem.at[j],
            device_id=(r, s), device_id_type=MESH)
        pl.semaphore_wait(free_sem.at[k], 1)
        copy.start()
        copy.wait_recv()
        sent.append(copy)
    for copy in sent:
        copy.wait_send()


def allreduce(x):
    rows = x.shape[0]
    HALVES = [rows >> (k + 1) for k in range(HALVINGS)]
    n_copies = 9 + 7
    return pl.pallas_call(
        allreduce_kernel,
        out_shape=jax.ShapeDtypeStruct((rows, 128), jnp.float32),
        in_specs=[pl.BlockSpec(memory_space=pltpu.VMEM)],
        out_specs=pl.BlockSpec(memory_space=pltpu.VMEM),
        scratch_shapes=[pltpu.VMEM((h, 128), jnp.float32) for h in HALVES]
        + [pltpu.VMEM((HALVES[-1], 128), jnp.float32)] * 2
        + [pltpu.SemaphoreType.DMA((n_copies,)), pltpu.SemaphoreType.DMA((n_copies,))]
        + [pltpu.SemaphoreType.REGULAR((HALVINGS,))],
        compiler_params=pltpu.CompilerParams(collective_id=0, has_side_effects=True),
    )(x)


def summed_everywhere(arrays):
    flat = jnp.concatenate([a.reshape(-1) for a in arrays])
    unit = 128 * 8 << HALVINGS
    rows = -(-flat.size // unit) * unit // 128
    padded = jnp.pad(flat, (0, rows * 128 - flat.size)).reshape(rows, 128)
    total = allreduce(padded).reshape(-1)
    out, at = [], 0
    for a in arrays:
        out.append(total[at:at + a.size].reshape(a.shape))
        at += a.size
    return out


def extended_2(block, sides, width):
    for axis, dim in sides:
        count = lax.axis_size(axis)
        forward = [(i, i + 1) for i in range(count - 1)]
        backward = [(target, source) for source, target in forward]
        low = lax.ppermute(
            lax.slice_in_dim(block, block.shape[dim] - width, None, axis=dim), axis, forward
        )
        high = lax.ppermute(lax.slice_in_dim(block, 0, width, axis=dim), axis, backward)
        block = jnp.concatenate([low, block, high], axis=dim)
    return block


def _one_hot(pos_ref, o, rows):
    column = pos_ref[:, o:o + 1]
    lanes = lax.broadcasted_iota(jnp.int32, (column.shape[0], rows), 1)
    return (column == lanes).astype(jnp.bfloat16)


def conv_fwd_kernel(pos_ref, table_ref, w_ref, out_ref):
    channels = table_ref.shape[1]
    table = table_ref[...]
    total = jnp.zeros(out_ref.shape, jnp.float32)
    for o in range(pos_ref.shape[1]):
        picked = jnp.dot(_one_hot(pos_ref, o, table.shape[0]), table, preferred_element_type=jnp.float32)
        weight = w_ref[o * channels:(o + 1) * channels, :]
        total = total + jnp.dot(picked.astype(jnp.bfloat16), weight, preferred_element_type=jnp.float32)
    out_ref[...] = total


def conv_bwd_kernel(pos_ref, table_ref, grad_ref, w_ref, tgrad_ref, wgrad_ref):
    channels = table_ref.shape[1]
    table = table_ref[...]
    grad = grad_ref[...]
    back = (((0,), (0,)), ((), ()))
    total = jnp.zeros(tgrad_ref.shape, jnp.float32)
    for o in range(pos_ref.shape[1]):
        hot = _one_hot(pos_ref, o, table.shape[0])
        picked = jnp.dot(hot, table, preferred_element_type=jnp.float32).astype(jnp.bfloat16)
        wgrad_ref[o * channels:(o + 1) * channels, :] = lax.dot_general(
            picked, grad, back, preferred_element_type=jnp.float32)
        weight = w_ref[o * channels:(o + 1) * channels, :]
        spread = lax.dot_general(grad, weight, (((1,), (1,)), ((), ())), preferred_element_type=jnp.float32)
        high = spread.astype(jnp.bfloat16)
        low = (spread - high.astype(jnp.float32)).astype(jnp.bfloat16)
        total = total + lax.dot_general(hot, high, back, preferred_element_type=jnp.float32)
        total = total + lax.dot_general(hot, low, back, preferred_element_type=jnp.float32)
    tgrad_ref[...] = total


def _vmem_call(kernel, outs, *args):
    return pl.pallas_call(
        kernel,
        out_shape=outs,
        in_specs=[pl.BlockSpec(memory_space=pltpu.VMEM)] * len(args),
        out_specs=jax.tree.map(lambda _: pl.BlockSpec(memory_space=pltpu.VMEM), outs),
    )(*args)


def on_device(features, neighbours, down_map, w_conv, w_down, coarse_grad):
    voxels, channels = features.shape
    offsets = neighbours.shape[1]
    rim = 64
    absent = neighbours >= 9 * voxels
    slot_idx = neighbours // voxels
    local_idx = neighbours - slot_idx * voxels
    halo_slot = jnp.where(slot_idx < 4, slot_idx, slot_idx - 1)
    compact = jnp.where(slot_idx == 4, 8 * rim + local_idx, halo_slot * rim + local_idx)
    positions = jnp.where(absent, -1, compact).astype(jnp.int32)
    sendable = features[:rim].reshape(1, 1, rim * channels // 128, 128)
    extended = extended_2(sendable, (("region", 0), ("slab", 1)), 1).reshape(9, rim, channels)
    halo = jnp.concatenate([extended[:4], extended[5:]], axis=0).reshape(8 * rim, channels)
    table = jnp.concatenate([halo, features], axis=0)
    table_rows = table.shape[0]

    conv_out = _vmem_call(
        conv_fwd_kernel, jax.ShapeDtypeStruct((voxels, channels), jnp.float32), positions, table, w_conv)
    hidden = (features.astype(jnp.float32) + jax.nn.silu(conv_out)).astype(jnp.bfloat16)
    zero_row = jnp.zeros((1, channels), features.dtype)
    coarse_count, taps = down_map.shape
    down_local = jnp.minimum(down_map, voxels)
    hidden_pad = jnp.concatenate([hidden, zero_row], axis=0)
    coarse_rows = hidden_pad[down_local].reshape(coarse_count, taps * channels)
    coarse = jnp.dot(coarse_rows, w_down, preferred_element_type=jnp.float32).astype(jnp.bfloat16)
    coarse_back = jnp.dot(coarse_grad, w_down.T, preferred_element_type=jnp.float32)
    hidden_grad = jnp.zeros((voxels + 1, channels), jnp.float32)
    hidden_grad = hidden_grad.at[down_local.reshape(-1)].add(coarse_back.reshape(-1, channels))[
        :voxels
    ]
    down_wgrad = lax.dot_general(
        coarse_rows, coarse_grad, (((0,), (0,)), ((), ())), preferred_element_type=jnp.float32
    )
    sigmoid_y = jax.nn.sigmoid(conv_out)
    conv_grad = (hidden_grad * sigmoid_y * (1.0 + conv_out * (1.0 - sigmoid_y))).astype(
        jnp.bfloat16
    )
    table_grad, conv_wgrad = _vmem_call(
        conv_bwd_kernel,
        (jax.ShapeDtypeStruct((table_rows, channels), jnp.float32),
         jax.ShapeDtypeStruct(w_conv.shape, jnp.float32)),
        positions, table, conv_grad, w_conv)
    conv_wgrad, down_wgrad = summed_everywhere([conv_wgrad, down_wgrad])
    own_part = table_grad[8 * rim:]
    halo_grad = table_grad[: 8 * rim].reshape(8, rim, channels)
    sections = jnp.concatenate(
        [halo_grad[:4], jnp.zeros((1, rim, channels), jnp.float32), halo_grad[4:]], axis=0)
    outgoing = sections.reshape(3, 3, rim * channels // 128, 128)
    returned = extended_2(outgoing.astype(jnp.bfloat16), (("region", 0), ("slab", 1)), 1).astype(
        outgoing.dtype
    )
    returned = returned.reshape(5, 5, rim, channels)
    incoming = jnp.sum(returned[0::2, 0::2], axis=(0, 1))
    grad_input = hidden_grad + own_part
    grad_input = grad_input.at[:rim].add(incoming)
    return (coarse, grad_input, conv_wgrad, down_wgrad)


def solution(mesh):
    in_specs = (
        P(("region", "slab"), None),
        P(("region", "slab"), None),
        P(("region", "slab"), None),
        P(),
        P(),
        P(("region", "slab"), None),
    )
    out_specs = (P(("region", "slab"), None), P(("region", "slab"), None), P(), P())
    return jax.shard_map(
        on_device, mesh=mesh, in_specs=in_specs, out_specs=out_specs, check_vma=False
    )
```

```python
import jax
import jax.numpy as jnp
from jax import lax
from jax.experimental import pallas as pl
from jax.experimental.pallas import tpu as pltpu
from jax.sharding import PartitionSpec as P
from jax.experimental import pallas as pl
from jax.experimental.pallas import tpu as pltpu

MESH = pl.DeviceIdType.MESH
HALVINGS = 7
ORDER_A = [0, 4, 7, 1, 5, 8]
ORDER_B = [4, 7, 0, 5, 8, 1]
FULL_A = [2, 6]
FULL_B = [6, 2]


def _bit_partner(region, slab, b):
    if b < 3:
        v = (slab // (1 << b)) % 2
        return v, region, slab + (1 - 2 * v) * (1 << b)
    j = b - 3
    v = (region // (1 << j)) % 2
    return v, region + (1 - 2 * v) * (1 << j), slab


def _step(region, slab, core, ba, bb):
    va, ra, sa = _bit_partner(region, slab, ba)
    vb, rb, sb = _bit_partner(region, slab, bb)
    return va + core * (vb - va), ra + core * (rb - ra), sa + core * (sb - sa)


def bwd_allreduce_kernel(pos_ref, table_ref, grad_ref, w_ref, down_ref, o_ref, tgrad_ref, *scratch):
    HALVES = [o_ref.shape[0] >> (k + 1) for k in range(HALVINGS)]
    recvs = scratch[:9]
    send_sem, recv_sem, free_sem = scratch[9], scratch[10], scratch[11]
    region = lax.axis_index("region")
    slab = lax.axis_index("slab")
    core = region % 2
    steps = [(core, region + 1 - 2 * core, slab)]
    for ba, bb in zip(ORDER_A, ORDER_B):
        steps.append(_step(region, slab, core, ba, bb))
    fulls = [_step(region, slab, core, ba, bb) for ba, bb in zip(FULL_A, FULL_B)]

    barrier = pltpu.get_barrier_semaphore()
    for _, r, s in steps + fulls:
        pl.semaphore_signal(barrier, inc=1, device_id=(r, s), device_id_type=MESH)
    conv_bwd_body(pos_ref, table_ref, grad_ref, w_ref, tgrad_ref, o_ref)
    filled = w_ref.shape[0]
    o_ref[filled:filled + down_ref.shape[0]] = down_ref[...]
    o_ref[filled + down_ref.shape[0]:] = jnp.zeros(
        (o_ref.shape[0] - filled - down_ref.shape[0], o_ref.shape[1]), jnp.float32)
    pl.semaphore_wait(barrier, len(steps) + len(fulls))

    off = 0
    offs = []
    for k, (v, r, s) in enumerate(steps):
        size = HALVES[k]
        keep = pl.multiple_of(off + v * size, 8)
        send = pl.multiple_of(off + (1 - v) * size, 8)
        src = o_ref
        copy = pltpu.make_async_remote_copy(
            src_ref=src.at[pl.ds(send, size)], dst_ref=recvs[k],
            send_sem=send_sem.at[k], recv_sem=recv_sem.at[k],
            device_id=(r, s), device_id_type=MESH)
        copy.start()
        copy.wait()
        pl.semaphore_signal(free_sem.at[k], inc=1, device_id=(r, s), device_id_type=MESH)
        o_ref[pl.ds(keep, size)] = src[pl.ds(keep, size)] + recvs[k][...]
        off = keep
        offs.append(keep)
    last = HALVES[-1]
    for i, (v, r, s) in enumerate(fulls):
        k = len(steps) + i
        copy = pltpu.make_async_remote_copy(
            src_ref=o_ref.at[pl.ds(off, last)], dst_ref=recvs[k],
            send_sem=send_sem.at[k], recv_sem=recv_sem.at[k],
            device_id=(r, s), device_id_type=MESH)
        copy.start()
        copy.wait()
        o_ref[pl.ds(off, last)] = o_ref[pl.ds(off, last)] + recvs[k][...]
    base = len(steps) + len(fulls)
    for k in reversed(range(len(steps))):
        v, r, s = steps[k]
        size = HALVES[k]
        j = base + (len(steps) - 1 - k)
        copy = pltpu.make_async_remote_copy(
            src_ref=o_ref.at[pl.ds(offs[k], size)], dst_ref=o_ref.at[pl.ds(offs[k], size)],
            send_sem=send_sem.at[j], recv_sem=recv_sem.at[j],
            device_id=(r, s), device_id_type=MESH)
        pl.semaphore_wait(free_sem.at[k], 1)
        copy.start()
        copy.wait()


def bwd_allreduce(positions, table, conv_grad, w_conv, down):
    width = w_conv.shape[1]
    unit = 8 << HALVINGS
    rows = -(-(w_conv.shape[0] + down.shape[0]) // unit) * unit
    HALVES = [rows >> (k + 1) for k in range(HALVINGS)]
    n_copies = 9 + 7
    args = (positions, table, conv_grad, w_conv, down)
    return pl.pallas_call(
        bwd_allreduce_kernel,
        out_shape=(jax.ShapeDtypeStruct((rows, width), jnp.float32),
                   jax.ShapeDtypeStruct(table.shape, jnp.float32)),
        in_specs=[pl.BlockSpec(memory_space=pltpu.VMEM)] * len(args),
        out_specs=(pl.BlockSpec(memory_space=pltpu.VMEM), pl.BlockSpec(memory_space=pltpu.VMEM)),
        scratch_shapes=[pltpu.VMEM((h, width), jnp.float32) for h in HALVES]
        + [pltpu.VMEM((HALVES[-1], width), jnp.float32)] * 2
        + [pltpu.SemaphoreType.DMA((n_copies,)), pltpu.SemaphoreType.DMA((n_copies,))]
        + [pltpu.SemaphoreType.REGULAR((HALVINGS,))],
        compiler_params=pltpu.CompilerParams(collective_id=0, has_side_effects=True),
    )(*args)


def extended_2(block, sides, width):
    for axis, dim in sides:
        count = lax.axis_size(axis)
        forward = [(i, i + 1) for i in range(count - 1)]
        backward = [(target, source) for source, target in forward]
        low = lax.ppermute(
            lax.slice_in_dim(block, block.shape[dim] - width, None, axis=dim), axis, forward
        )
        high = lax.ppermute(lax.slice_in_dim(block, 0, width, axis=dim), axis, backward)
        block = jnp.concatenate([low, block, high], axis=dim)
    return block


def _one_hot(pos_ref, o, rows):
    column = pos_ref[:, o:o + 1]
    lanes = lax.broadcasted_iota(jnp.int32, (column.shape[0], rows), 1)
    return (column == lanes).astype(jnp.bfloat16)


def conv_fwd_kernel(pos_ref, table_ref, w_ref, out_ref):
    channels = table_ref.shape[1]
    table = table_ref[...]
    total = jnp.zeros(out_ref.shape, jnp.float32)
    for o in range(pos_ref.shape[1]):
        picked = jnp.dot(_one_hot(pos_ref, o, table.shape[0]), table, preferred_element_type=jnp.float32)
        weight = w_ref[o * channels:(o + 1) * channels, :]
        total = total + jnp.dot(picked.astype(jnp.bfloat16), weight, preferred_element_type=jnp.float32)
    out_ref[...] = total


def conv_bwd_body(pos_ref, table_ref, grad_ref, w_ref, tgrad_ref, wgrad_ref):
    channels = table_ref.shape[1]
    table = table_ref[...]
    grad = grad_ref[...]
    back = (((0,), (0,)), ((), ()))
    total = jnp.zeros(tgrad_ref.shape, jnp.float32)
    for o in range(pos_ref.shape[1]):
        hot = _one_hot(pos_ref, o, table.shape[0])
        picked = jnp.dot(hot, table, preferred_element_type=jnp.float32).astype(jnp.bfloat16)
        wgrad_ref[o * channels:(o + 1) * channels, :] = lax.dot_general(
            picked, grad, back, preferred_element_type=jnp.float32)
        weight = w_ref[o * channels:(o + 1) * channels, :]
        spread = lax.dot_general(grad, weight, (((1,), (1,)), ((), ())), preferred_element_type=jnp.float32)
        high = spread.astype(jnp.bfloat16)
        low = (spread - high.astype(jnp.float32)).astype(jnp.bfloat16)
        total = total + lax.dot_general(hot, high, back, preferred_element_type=jnp.float32)
        total = total + lax.dot_general(hot, low, back, preferred_element_type=jnp.float32)
    tgrad_ref[...] = total


def _vmem_call(kernel, outs, *args):
    return pl.pallas_call(
        kernel,
        out_shape=outs,
        in_specs=[pl.BlockSpec(memory_space=pltpu.VMEM)] * len(args),
        out_specs=jax.tree.map(lambda _: pl.BlockSpec(memory_space=pltpu.VMEM), outs),
    )(*args)


def on_device(features, neighbours, down_map, w_conv, w_down, coarse_grad):
    voxels, channels = features.shape
    offsets = neighbours.shape[1]
    rim = 64
    absent = neighbours >= 9 * voxels
    slot_idx = neighbours // voxels
    local_idx = neighbours - slot_idx * voxels
    halo_slot = jnp.where(slot_idx < 4, slot_idx, slot_idx - 1)
    compact = jnp.where(slot_idx == 4, 8 * rim + local_idx, halo_slot * rim + local_idx)
    positions = jnp.where(absent, -1, compact).astype(jnp.int32)
    sendable = features[:rim].reshape(1, 1, rim * channels // 128, 128)
    extended = extended_2(sendable, (("region", 0), ("slab", 1)), 1).reshape(9, rim, channels)
    halo = jnp.concatenate([extended[:4], extended[5:]], axis=0).reshape(8 * rim, channels)
    table = jnp.concatenate([halo, features], axis=0)
    table_rows = table.shape[0]

    conv_out = _vmem_call(
        conv_fwd_kernel, jax.ShapeDtypeStruct((voxels, channels), jnp.float32), positions, table, w_conv)
    hidden = (features.astype(jnp.float32) + jax.nn.silu(conv_out)).astype(jnp.bfloat16)
    zero_row = jnp.zeros((1, channels), features.dtype)
    coarse_count, taps = down_map.shape
    down_local = jnp.minimum(down_map, voxels)
    hidden_pad = jnp.concatenate([hidden, zero_row], axis=0)
    coarse_rows = hidden_pad[down_local].reshape(coarse_count, taps * channels)
    coarse = jnp.dot(coarse_rows, w_down, preferred_element_type=jnp.float32).astype(jnp.bfloat16)
    coarse_back = jnp.dot(coarse_grad, w_down.T, preferred_element_type=jnp.float32)
    hidden_grad = jnp.zeros((voxels + 1, channels), jnp.float32)
    hidden_grad = hidden_grad.at[down_local.reshape(-1)].add(coarse_back.reshape(-1, channels))[
        :voxels
    ]
    down_wgrad = lax.dot_general(
        coarse_rows, coarse_grad, (((0,), (0,)), ((), ())), preferred_element_type=jnp.float32
    )
    sigmoid_y = jax.nn.sigmoid(conv_out)
    conv_grad = (hidden_grad * sigmoid_y * (1.0 + conv_out * (1.0 - sigmoid_y))).astype(
        jnp.bfloat16
    )
    down_flat = down_wgrad.reshape(-1, channels)
    summed, table_grad = bwd_allreduce(positions, table, conv_grad, w_conv, down_flat)
    conv_wgrad = summed[: w_conv.shape[0]]
    down_wgrad = summed[w_conv.shape[0]: w_conv.shape[0] + down_flat.shape[0]].reshape(w_down.shape)
    own_part = table_grad[8 * rim:]
    halo_grad = table_grad[: 8 * rim].reshape(8, rim, channels)
    sections = jnp.concatenate(
        [halo_grad[:4], jnp.zeros((1, rim, channels), jnp.float32), halo_grad[4:]], axis=0)
    outgoing = sections.reshape(3, 3, rim * channels // 128, 128)
    returned = extended_2(outgoing.astype(jnp.bfloat16), (("region", 0), ("slab", 1)), 1).astype(
        outgoing.dtype
    )
    returned = returned.reshape(5, 5, rim, channels)
    incoming = jnp.sum(returned[0::2, 0::2], axis=(0, 1))
    grad_input = hidden_grad + own_part
    grad_input = grad_input.at[:rim].add(incoming)
    return (coarse, grad_input, conv_wgrad, down_wgrad)


def solution(mesh):
    in_specs = (
        P(("region", "slab"), None),
        P(("region", "slab"), None),
        P(("region", "slab"), None),
        P(),
        P(),
        P(("region", "slab"), None),
    )
    out_specs = (P(("region", "slab"), None), P(("region", "slab"), None), P(), P())
    return jax.shard_map(
        on_device, mesh=mesh, in_specs=in_specs, out_specs=out_specs, check_vma=False
    )
```

```python
import jax
import jax.numpy as jnp
from jax import lax
from jax.experimental import pallas as pl
from jax.experimental.pallas import tpu as pltpu
from jax.sharding import PartitionSpec as P
from jax.experimental import pallas as pl
from jax.experimental.pallas import tpu as pltpu

MESH = pl.DeviceIdType.MESH
HALVINGS = 7
ORDER_A = [0, 4, 7, 1, 5, 8]
ORDER_B = [4, 7, 0, 5, 8, 1]
FULL_A = [2, 6]
FULL_B = [6, 2]


def _bit_partner(region, slab, b):
    if b < 3:
        v = (slab // (1 << b)) % 2
        return v, region, slab + (1 - 2 * v) * (1 << b)
    j = b - 3
    v = (region // (1 << j)) % 2
    return v, region + (1 - 2 * v) * (1 << j), slab


def _step(region, slab, core, ba, bb):
    va, ra, sa = _bit_partner(region, slab, ba)
    vb, rb, sb = _bit_partner(region, slab, bb)
    return va + core * (vb - va), ra + core * (rb - ra), sa + core * (sb - sa)


def allreduce_kernel(x_ref, o_ref, *scratch):
    HALVES = [x_ref.shape[0] >> (k + 1) for k in range(HALVINGS)]
    recvs = scratch[:9]
    send_sem, recv_sem, free_sem = scratch[9], scratch[10], scratch[11]
    region = lax.axis_index("region")
    slab = lax.axis_index("slab")
    core = region % 2
    steps = [(core, region + 1 - 2 * core, slab)]
    for ba, bb in zip(ORDER_A, ORDER_B):
        steps.append(_step(region, slab, core, ba, bb))
    fulls = [_step(region, slab, core, ba, bb) for ba, bb in zip(FULL_A, FULL_B)]

    barrier = pltpu.get_barrier_semaphore()
    for _, r, s in steps + fulls:
        pl.semaphore_signal(barrier, inc=1, device_id=(r, s), device_id_type=MESH)
    pl.semaphore_wait(barrier, len(steps) + len(fulls))

    off = 0
    offs = []
    for k, (v, r, s) in enumerate(steps):
        size = HALVES[k]
        keep = pl.multiple_of(off + v * size, 8)
        send = pl.multiple_of(off + (1 - v) * size, 8)
        src = x_ref if k == 0 else o_ref
        copy = pltpu.make_async_remote_copy(
            src_ref=src.at[pl.ds(send, size)], dst_ref=recvs[k],
            send_sem=send_sem.at[k], recv_sem=recv_sem.at[k],
            device_id=(r, s), device_id_type=MESH)
        copy.start()
        copy.wait()
        pl.semaphore_signal(free_sem.at[k], inc=1, device_id=(r, s), device_id_type=MESH)
        o_ref[pl.ds(keep, size)] = src[pl.ds(keep, size)] + recvs[k][...]
        off = keep
        offs.append(keep)
    last = HALVES[-1]
    for i, (v, r, s) in enumerate(fulls):
        k = len(steps) + i
        copy = pltpu.make_async_remote_copy(
            src_ref=o_ref.at[pl.ds(off, last)], dst_ref=recvs[k],
            send_sem=send_sem.at[k], recv_sem=recv_sem.at[k],
            device_id=(r, s), device_id_type=MESH)
        copy.start()
        copy.wait()
        o_ref[pl.ds(off, last)] = o_ref[pl.ds(off, last)] + recvs[k][...]
    base = len(steps) + len(fulls)
    for k in reversed(range(len(steps))):
        v, r, s = steps[k]
        size = HALVES[k]
        j = base + (len(steps) - 1 - k)
        copy = pltpu.make_async_remote_copy(
            src_ref=o_ref.at[pl.ds(offs[k], size)], dst_ref=o_ref.at[pl.ds(offs[k], size)],
            send_sem=send_sem.at[j], recv_sem=recv_sem.at[j],
            device_id=(r, s), device_id_type=MESH)
        pl.semaphore_wait(free_sem.at[k], 1)
        copy.start()
        copy.wait()


def allreduce(x):
    rows = x.shape[0]
    HALVES = [rows >> (k + 1) for k in range(HALVINGS)]
    n_copies = 9 + 7
    return pl.pallas_call(
        allreduce_kernel,
        out_shape=jax.ShapeDtypeStruct((rows, 128), jnp.float32),
        in_specs=[pl.BlockSpec(memory_space=pltpu.VMEM)],
        out_specs=pl.BlockSpec(memory_space=pltpu.VMEM),
        scratch_shapes=[pltpu.VMEM((h, 128), jnp.float32) for h in HALVES]
        + [pltpu.VMEM((HALVES[-1], 128), jnp.float32)] * 2
        + [pltpu.SemaphoreType.DMA((n_copies,)), pltpu.SemaphoreType.DMA((n_copies,))]
        + [pltpu.SemaphoreType.REGULAR((HALVINGS,))],
        compiler_params=pltpu.CompilerParams(collective_id=0, has_side_effects=True),
    )(x)


def summed_everywhere(arrays):
    flat = jnp.concatenate([a.reshape(-1) for a in arrays])
    unit = 128 * 8 << HALVINGS
    rows = -(-flat.size // unit) * unit // 128
    padded = jnp.pad(flat, (0, rows * 128 - flat.size)).reshape(rows, 128)
    total = allreduce(padded).reshape(-1)
    out, at = [], 0
    for a in arrays:
        out.append(total[at:at + a.size].reshape(a.shape))
        at += a.size
    return out


def _exists(index, size):
    low = (index + size - 1) // size
    high = (2 * size - 3 - index) // (size - 1)
    return (low, 1, high)


def halo_kernel(src_ref, out_ref, send_sem, recv_sem):
    region = lax.axis_index("region")
    slab = lax.axis_index("slab")
    along_region = _exists(region, lax.axis_size("region"))
    along_slab = _exists(slab, lax.axis_size("slab"))
    codes = [c for c in range(9) if c != 4]
    slot = {c: i for i, c in enumerate(codes)}
    out_ref[...] = jnp.zeros(out_ref.shape, out_ref.dtype)
    barrier = pltpu.get_barrier_semaphore()
    present = {}
    for c in codes:
        present[c] = along_region[c // 3] * along_slab[c % 3]
        target = (region + c // 3 - 1, slab + c % 3 - 1)

        @pl.when(present[c] == 1)
        def _():
            pl.semaphore_signal(barrier, inc=1, device_id=target, device_id_type=MESH)
    count = (along_region[0] + 1 + along_region[2]) * (along_slab[0] + 1 + along_slab[2]) - 1
    pl.semaphore_wait(barrier, count)
    copies = {}
    for c in codes:
        target = (region + c // 3 - 1, slab + c % 3 - 1)
        copies[c] = pltpu.make_async_remote_copy(
            src_ref=src_ref.at[slot[c]], dst_ref=out_ref.at[slot[8 - c]],
            send_sem=send_sem.at[slot[c]], recv_sem=recv_sem.at[slot[8 - c]],
            device_id=target, device_id_type=MESH)

        @pl.when(present[c] == 1)
        def _():
            copies[c].start()
    for c in codes:
        @pl.when(present[c] == 1)
        def _():
            copies[8 - c].wait_recv()
            copies[c].wait_send()


def halo_exchange(src, cid):
    return pl.pallas_call(
        halo_kernel,
        out_shape=jax.ShapeDtypeStruct(src.shape, src.dtype),
        in_specs=[pl.BlockSpec(memory_space=pltpu.VMEM)],
        out_specs=pl.BlockSpec(memory_space=pltpu.VMEM),
        scratch_shapes=[pltpu.SemaphoreType.DMA((8,)), pltpu.SemaphoreType.DMA((8,))],
        compiler_params=pltpu.CompilerParams(collective_id=cid, has_side_effects=True),
    )(src)


def extended_2(block, sides, width):
    for axis, dim in sides:
        count = lax.axis_size(axis)
        forward = [(i, i + 1) for i in range(count - 1)]
        backward = [(target, source) for source, target in forward]
        low = lax.ppermute(
            lax.slice_in_dim(block, block.shape[dim] - width, None, axis=dim), axis, forward
        )
        high = lax.ppermute(lax.slice_in_dim(block, 0, width, axis=dim), axis, backward)
        block = jnp.concatenate([low, block, high], axis=dim)
    return block


def _one_hot(pos_ref, o, rows):
    column = pos_ref[:, o:o + 1]
    lanes = lax.broadcasted_iota(jnp.int32, (column.shape[0], rows), 1)
    return (column == lanes).astype(jnp.bfloat16)


def conv_fwd_kernel(pos_ref, table_ref, w_ref, out_ref):
    channels = table_ref.shape[1]
    table = table_ref[...]
    total = jnp.zeros(out_ref.shape, jnp.float32)
    for o in range(pos_ref.shape[1]):
        picked = jnp.dot(_one_hot(pos_ref, o, table.shape[0]), table, preferred_element_type=jnp.float32)
        weight = w_ref[o * channels:(o + 1) * channels, :]
        total = total + jnp.dot(picked.astype(jnp.bfloat16), weight, preferred_element_type=jnp.float32)
    out_ref[...] = total


def conv_bwd_kernel(pos_ref, table_ref, grad_ref, w_ref, tgrad_ref, wgrad_ref):
    channels = table_ref.shape[1]
    table = table_ref[...]
    grad = grad_ref[...]
    back = (((0,), (0,)), ((), ()))
    total = jnp.zeros(tgrad_ref.shape, jnp.float32)
    for o in range(pos_ref.shape[1]):
        hot = _one_hot(pos_ref, o, table.shape[0])
        picked = jnp.dot(hot, table, preferred_element_type=jnp.float32).astype(jnp.bfloat16)
        wgrad_ref[o * channels:(o + 1) * channels, :] = lax.dot_general(
            picked, grad, back, preferred_element_type=jnp.float32)
        weight = w_ref[o * channels:(o + 1) * channels, :]
        spread = lax.dot_general(grad, weight, (((1,), (1,)), ((), ())), preferred_element_type=jnp.float32)
        high = spread.astype(jnp.bfloat16)
        low = (spread - high.astype(jnp.float32)).astype(jnp.bfloat16)
        total = total + lax.dot_general(hot, high, back, preferred_element_type=jnp.float32)
        total = total + lax.dot_general(hot, low, back, preferred_element_type=jnp.float32)
    tgrad_ref[...] = total


def _vmem_call(kernel, outs, *args):
    return pl.pallas_call(
        kernel,
        out_shape=outs,
        in_specs=[pl.BlockSpec(memory_space=pltpu.VMEM)] * len(args),
        out_specs=jax.tree.map(lambda _: pl.BlockSpec(memory_space=pltpu.VMEM), outs),
    )(*args)


def on_device(features, neighbours, down_map, w_conv, w_down, coarse_grad):
    voxels, channels = features.shape
    offsets = neighbours.shape[1]
    rim = 64
    absent = neighbours >= 9 * voxels
    slot_idx = neighbours // voxels
    local_idx = neighbours - slot_idx * voxels
    halo_slot = jnp.where(slot_idx < 4, slot_idx, slot_idx - 1)
    compact = jnp.where(slot_idx == 4, 8 * rim + local_idx, halo_slot * rim + local_idx)
    positions = jnp.where(absent, -1, compact).astype(jnp.int32)
    sendable = jnp.broadcast_to(features[None, :rim], (8, rim, channels))
    halo = halo_exchange(sendable, 1).reshape(8 * rim, channels)
    table = jnp.concatenate([halo, features], axis=0)
    table_rows = table.shape[0]

    conv_out = _vmem_call(
        conv_fwd_kernel, jax.ShapeDtypeStruct((voxels, channels), jnp.float32), positions, table, w_conv)
    hidden = (features.astype(jnp.float32) + jax.nn.silu(conv_out)).astype(jnp.bfloat16)
    zero_row = jnp.zeros((1, channels), features.dtype)
    coarse_count, taps = down_map.shape
    down_local = jnp.minimum(down_map, voxels)
    hidden_pad = jnp.concatenate([hidden, zero_row], axis=0)
    coarse_rows = hidden_pad[down_local].reshape(coarse_count, taps * channels)
    coarse = jnp.dot(coarse_rows, w_down, preferred_element_type=jnp.float32).astype(jnp.bfloat16)
    coarse_back = jnp.dot(coarse_grad, w_down.T, preferred_element_type=jnp.float32)
    hidden_grad = jnp.zeros((voxels + 1, channels), jnp.float32)
    hidden_grad = hidden_grad.at[down_local.reshape(-1)].add(coarse_back.reshape(-1, channels))[
        :voxels
    ]
    down_wgrad = lax.dot_general(
        coarse_rows, coarse_grad, (((0,), (0,)), ((), ())), preferred_element_type=jnp.float32
    )
    sigmoid_y = jax.nn.sigmoid(conv_out)
    conv_grad = (hidden_grad * sigmoid_y * (1.0 + conv_out * (1.0 - sigmoid_y))).astype(
        jnp.bfloat16
    )
    table_grad, conv_wgrad = _vmem_call(
        conv_bwd_kernel,
        (jax.ShapeDtypeStruct((table_rows, channels), jnp.float32),
         jax.ShapeDtypeStruct(w_conv.shape, jnp.float32)),
        positions, table, conv_grad, w_conv)
    conv_wgrad, down_wgrad = summed_everywhere([conv_wgrad, down_wgrad])
    own_part = table_grad[8 * rim:]
    halo_grad = table_grad[: 8 * rim].reshape(8, rim, channels)
    incoming = jnp.sum(halo_exchange(halo_grad, 2), axis=0)
    grad_input = hidden_grad + own_part
    grad_input = grad_input.at[:rim].add(incoming)
    return (coarse, grad_input, conv_wgrad, down_wgrad)


def solution(mesh):
    in_specs = (
        P(("region", "slab"), None),
        P(("region", "slab"), None),
        P(("region", "slab"), None),
        P(),
        P(),
        P(("region", "slab"), None),
    )
    out_specs = (P(("region", "slab"), None), P(("region", "slab"), None), P(), P())
    return jax.shard_map(
        on_device, mesh=mesh, in_specs=in_specs, out_specs=out_specs, check_vma=False
    )
```

```python
import jax
import jax.numpy as jnp
from jax import lax
from jax.experimental import pallas as pl
from jax.experimental.pallas import tpu as pltpu
from jax.sharding import PartitionSpec as P
from jax.experimental import pallas as pl
from jax.experimental.pallas import tpu as pltpu

MESH = pl.DeviceIdType.MESH
HALVINGS = 7
ORDER_A = [0, 4, 7, 1, 5, 8]
ORDER_B = [4, 7, 0, 5, 8, 1]
FULL_A = [2, 6]
FULL_B = [6, 2]


def _bit_partner(region, slab, b):
    if b < 3:
        v = (slab // (1 << b)) % 2
        return v, region, slab + (1 - 2 * v) * (1 << b)
    j = b - 3
    v = (region // (1 << j)) % 2
    return v, region + (1 - 2 * v) * (1 << j), slab


def _step(region, slab, core, ba, bb):
    va, ra, sa = _bit_partner(region, slab, ba)
    vb, rb, sb = _bit_partner(region, slab, bb)
    return va + core * (vb - va), ra + core * (rb - ra), sa + core * (sb - sa)


def allreduce_kernel(x_ref, hsrc_ref, o_ref, hout_ref, *scratch):
    HALVES = [x_ref.shape[0] >> (k + 1) for k in range(HALVINGS)]
    recvs = scratch[:9]
    send_sem, recv_sem, free_sem = scratch[9], scratch[10], scratch[11]
    codes, present, targets, hcopies, hcount = _halo_plan(hsrc_ref, hout_ref, scratch[12], scratch[13])
    hout_ref[...] = jnp.zeros(hout_ref.shape, hout_ref.dtype)
    region = lax.axis_index("region")
    slab = lax.axis_index("slab")
    core = region % 2
    steps = [(core, region + 1 - 2 * core, slab)]
    for ba, bb in zip(ORDER_A, ORDER_B):
        steps.append(_step(region, slab, core, ba, bb))
    fulls = [_step(region, slab, core, ba, bb) for ba, bb in zip(FULL_A, FULL_B)]

    barrier = pltpu.get_barrier_semaphore()
    for _, r, s in steps + fulls:
        pl.semaphore_signal(barrier, inc=1, device_id=(r, s), device_id_type=MESH)
    _halo_signal(barrier, codes, present, targets)
    pl.semaphore_wait(barrier, len(steps) + len(fulls) + hcount)
    _halo_start(codes, present, hcopies)

    off = 0
    offs = []
    for k, (v, r, s) in enumerate(steps):
        size = HALVES[k]
        keep = pl.multiple_of(off + v * size, 8)
        send = pl.multiple_of(off + (1 - v) * size, 8)
        src = x_ref if k == 0 else o_ref
        copy = pltpu.make_async_remote_copy(
            src_ref=src.at[pl.ds(send, size)], dst_ref=recvs[k],
            send_sem=send_sem.at[k], recv_sem=recv_sem.at[k],
            device_id=(r, s), device_id_type=MESH)
        copy.start()
        copy.wait()
        pl.semaphore_signal(free_sem.at[k], inc=1, device_id=(r, s), device_id_type=MESH)
        o_ref[pl.ds(keep, size)] = src[pl.ds(keep, size)] + recvs[k][...]
        off = keep
        offs.append(keep)
    last = HALVES[-1]
    for i, (v, r, s) in enumerate(fulls):
        k = len(steps) + i
        copy = pltpu.make_async_remote_copy(
            src_ref=o_ref.at[pl.ds(off, last)], dst_ref=recvs[k],
            send_sem=send_sem.at[k], recv_sem=recv_sem.at[k],
            device_id=(r, s), device_id_type=MESH)
        copy.start()
        copy.wait()
        o_ref[pl.ds(off, last)] = o_ref[pl.ds(off, last)] + recvs[k][...]
    base = len(steps) + len(fulls)
    for k in reversed(range(len(steps))):
        v, r, s = steps[k]
        size = HALVES[k]
        j = base + (len(steps) - 1 - k)
        copy = pltpu.make_async_remote_copy(
            src_ref=o_ref.at[pl.ds(offs[k], size)], dst_ref=o_ref.at[pl.ds(offs[k], size)],
            send_sem=send_sem.at[j], recv_sem=recv_sem.at[j],
            device_id=(r, s), device_id_type=MESH)
        pl.semaphore_wait(free_sem.at[k], 1)
        copy.start()
        copy.wait()
    _halo_finish(codes, present, hcopies)


def allreduce(x, hsrc):
    rows = x.shape[0]
    HALVES = [rows >> (k + 1) for k in range(HALVINGS)]
    n_copies = 9 + 7
    return pl.pallas_call(
        allreduce_kernel,
        out_shape=(jax.ShapeDtypeStruct((rows, 128), jnp.float32),
                   jax.ShapeDtypeStruct(hsrc.shape, hsrc.dtype)),
        in_specs=[pl.BlockSpec(memory_space=pltpu.VMEM)] * 2,
        out_specs=(pl.BlockSpec(memory_space=pltpu.VMEM), pl.BlockSpec(memory_space=pltpu.VMEM)),
        scratch_shapes=[pltpu.VMEM((h, 128), jnp.float32) for h in HALVES]
        + [pltpu.VMEM((HALVES[-1], 128), jnp.float32)] * 2
        + [pltpu.SemaphoreType.DMA((n_copies,)), pltpu.SemaphoreType.DMA((n_copies,))]
        + [pltpu.SemaphoreType.REGULAR((HALVINGS,))]
        + [pltpu.SemaphoreType.DMA((8,)), pltpu.SemaphoreType.DMA((8,))],
        compiler_params=pltpu.CompilerParams(collective_id=0, has_side_effects=True),
    )(x, hsrc)


def summed_everywhere(arrays, hsrc):
    flat = jnp.concatenate([a.reshape(-1) for a in arrays])
    unit = 128 * 8 << HALVINGS
    rows = -(-flat.size // unit) * unit // 128
    padded = jnp.pad(flat, (0, rows * 128 - flat.size)).reshape(rows, 128)
    total, hout = allreduce(padded, hsrc)
    total = total.reshape(-1)
    out, at = [], 0
    for a in arrays:
        out.append(total[at:at + a.size].reshape(a.shape))
        at += a.size
    return out, hout


def _exists(index, size):
    low = (index + size - 1) // size
    high = (2 * size - 3 - index) // (size - 1)
    return (low, 1, high)


def _halo_plan(src_ref, out_ref, send_sem, recv_sem):
    region = lax.axis_index("region")
    slab = lax.axis_index("slab")
    along_region = _exists(region, lax.axis_size("region"))
    along_slab = _exists(slab, lax.axis_size("slab"))
    codes = [c for c in range(9) if c != 4]
    slot = {c: i for i, c in enumerate(codes)}
    present, targets, copies = {}, {}, {}
    for c in codes:
        present[c] = along_region[c // 3] * along_slab[c % 3]
        targets[c] = (region + c // 3 - 1, slab + c % 3 - 1)
        copies[c] = pltpu.make_async_remote_copy(
            src_ref=src_ref.at[slot[c]], dst_ref=out_ref.at[slot[8 - c]],
            send_sem=send_sem.at[slot[c]], recv_sem=recv_sem.at[slot[8 - c]],
            device_id=targets[c], device_id_type=MESH)
    count = (along_region[0] + 1 + along_region[2]) * (along_slab[0] + 1 + along_slab[2]) - 1
    return codes, present, targets, copies, count


def _halo_signal(barrier, codes, present, targets):
    for c in codes:
        @pl.when(present[c] == 1)
        def _():
            pl.semaphore_signal(barrier, inc=1, device_id=targets[c], device_id_type=MESH)


def _halo_start(codes, present, copies):
    for c in codes:
        @pl.when(present[c] == 1)
        def _():
            copies[c].start()


def _halo_finish(codes, present, copies):
    for c in codes:
        @pl.when(present[c] == 1)
        def _():
            copies[8 - c].wait_recv()
            copies[c].wait_send()


def halo_kernel(src_ref, out_ref, send_sem, recv_sem):
    codes, present, targets, copies, count = _halo_plan(src_ref, out_ref, send_sem, recv_sem)
    out_ref[...] = jnp.zeros(out_ref.shape, out_ref.dtype)
    barrier = pltpu.get_barrier_semaphore()
    _halo_signal(barrier, codes, present, targets)
    pl.semaphore_wait(barrier, count)
    _halo_start(codes, present, copies)
    _halo_finish(codes, present, copies)


def halo_exchange(src, cid):
    return pl.pallas_call(
        halo_kernel,
        out_shape=jax.ShapeDtypeStruct(src.shape, src.dtype),
        in_specs=[pl.BlockSpec(memory_space=pltpu.VMEM)],
        out_specs=pl.BlockSpec(memory_space=pltpu.VMEM),
        scratch_shapes=[pltpu.SemaphoreType.DMA((8,)), pltpu.SemaphoreType.DMA((8,))],
        compiler_params=pltpu.CompilerParams(collective_id=cid, has_side_effects=True),
    )(src)


def extended_2(block, sides, width):
    for axis, dim in sides:
        count = lax.axis_size(axis)
        forward = [(i, i + 1) for i in range(count - 1)]
        backward = [(target, source) for source, target in forward]
        low = lax.ppermute(
            lax.slice_in_dim(block, block.shape[dim] - width, None, axis=dim), axis, forward
        )
        high = lax.ppermute(lax.slice_in_dim(block, 0, width, axis=dim), axis, backward)
        block = jnp.concatenate([low, block, high], axis=dim)
    return block


def _one_hot(pos_ref, o, rows):
    column = pos_ref[:, o:o + 1]
    lanes = lax.broadcasted_iota(jnp.int32, (column.shape[0], rows), 1)
    return (column == lanes).astype(jnp.bfloat16)


def conv_fwd_kernel(pos_ref, table_ref, w_ref, out_ref):
    channels = table_ref.shape[1]
    table = table_ref[...]
    total = jnp.zeros(out_ref.shape, jnp.float32)
    for o in range(pos_ref.shape[1]):
        picked = jnp.dot(_one_hot(pos_ref, o, table.shape[0]), table, preferred_element_type=jnp.float32)
        weight = w_ref[o * channels:(o + 1) * channels, :]
        total = total + jnp.dot(picked.astype(jnp.bfloat16), weight, preferred_element_type=jnp.float32)
    out_ref[...] = total


def conv_bwd_kernel(pos_ref, table_ref, grad_ref, w_ref, tgrad_ref, wgrad_ref):
    channels = table_ref.shape[1]
    table = table_ref[...]
    grad = grad_ref[...]
    back = (((0,), (0,)), ((), ()))
    total = jnp.zeros(tgrad_ref.shape, jnp.float32)
    for o in range(pos_ref.shape[1]):
        hot = _one_hot(pos_ref, o, table.shape[0])
        picked = jnp.dot(hot, table, preferred_element_type=jnp.float32).astype(jnp.bfloat16)
        wgrad_ref[o * channels:(o + 1) * channels, :] = lax.dot_general(
            picked, grad, back, preferred_element_type=jnp.float32)
        weight = w_ref[o * channels:(o + 1) * channels, :]
        spread = lax.dot_general(grad, weight, (((1,), (1,)), ((), ())), preferred_element_type=jnp.float32)
        high = spread.astype(jnp.bfloat16)
        low = (spread - high.astype(jnp.float32)).astype(jnp.bfloat16)
        total = total + lax.dot_general(hot, high, back, preferred_element_type=jnp.float32)
        total = total + lax.dot_general(hot, low, back, preferred_element_type=jnp.float32)
    tgrad_ref[...] = total


def _vmem_call(kernel, outs, *args):
    return pl.pallas_call(
        kernel,
        out_shape=outs,
        in_specs=[pl.BlockSpec(memory_space=pltpu.VMEM)] * len(args),
        out_specs=jax.tree.map(lambda _: pl.BlockSpec(memory_space=pltpu.VMEM), outs),
    )(*args)


def on_device(features, neighbours, down_map, w_conv, w_down, coarse_grad):
    voxels, channels = features.shape
    offsets = neighbours.shape[1]
    rim = 64
    absent = neighbours >= 9 * voxels
    slot_idx = neighbours // voxels
    local_idx = neighbours - slot_idx * voxels
    halo_slot = jnp.where(slot_idx < 4, slot_idx, slot_idx - 1)
    compact = jnp.where(slot_idx == 4, 8 * rim + local_idx, halo_slot * rim + local_idx)
    positions = jnp.where(absent, -1, compact).astype(jnp.int32)
    sendable = jnp.broadcast_to(features[None, :rim], (8, rim, channels))
    halo = halo_exchange(sendable, 1).reshape(8 * rim, channels)
    table = jnp.concatenate([halo, features], axis=0)
    table_rows = table.shape[0]

    conv_out = _vmem_call(
        conv_fwd_kernel, jax.ShapeDtypeStruct((voxels, channels), jnp.float32), positions, table, w_conv)
    hidden = (features.astype(jnp.float32) + jax.nn.silu(conv_out)).astype(jnp.bfloat16)
    zero_row = jnp.zeros((1, channels), features.dtype)
    coarse_count, taps = down_map.shape
    down_local = jnp.minimum(down_map, voxels)
    hidden_pad = jnp.concatenate([hidden, zero_row], axis=0)
    coarse_rows = hidden_pad[down_local].reshape(coarse_count, taps * channels)
    coarse = jnp.dot(coarse_rows, w_down, preferred_element_type=jnp.float32).astype(jnp.bfloat16)
    coarse_back = jnp.dot(coarse_grad, w_down.T, preferred_element_type=jnp.float32)
    hidden_grad = jnp.zeros((voxels + 1, channels), jnp.float32)
    hidden_grad = hidden_grad.at[down_local.reshape(-1)].add(coarse_back.reshape(-1, channels))[
        :voxels
    ]
    down_wgrad = lax.dot_general(
        coarse_rows, coarse_grad, (((0,), (0,)), ((), ())), preferred_element_type=jnp.float32
    )
    sigmoid_y = jax.nn.sigmoid(conv_out)
    conv_grad = (hidden_grad * sigmoid_y * (1.0 + conv_out * (1.0 - sigmoid_y))).astype(
        jnp.bfloat16
    )
    table_grad, conv_wgrad = _vmem_call(
        conv_bwd_kernel,
        (jax.ShapeDtypeStruct((table_rows, channels), jnp.float32),
         jax.ShapeDtypeStruct(w_conv.shape, jnp.float32)),
        positions, table, conv_grad, w_conv)
    halo_grad = table_grad[: 8 * rim].reshape(8, rim, channels)
    (conv_wgrad, down_wgrad), returned = summed_everywhere([conv_wgrad, down_wgrad], halo_grad)
    own_part = table_grad[8 * rim:]
    incoming = jnp.sum(returned, axis=0)
    grad_input = hidden_grad + own_part
    grad_input = grad_input.at[:rim].add(incoming)
    return (coarse, grad_input, conv_wgrad, down_wgrad)


def solution(mesh):
    in_specs = (
        P(("region", "slab"), None),
        P(("region", "slab"), None),
        P(("region", "slab"), None),
        P(),
        P(),
        P(("region", "slab"), None),
    )
    out_specs = (P(("region", "slab"), None), P(("region", "slab"), None), P(), P())
    return jax.shard_map(
        on_device, mesh=mesh, in_specs=in_specs, out_specs=out_specs, check_vma=False
    )
```

```python
import jax
import jax.numpy as jnp
from jax import lax
from jax.experimental import pallas as pl
from jax.experimental.pallas import tpu as pltpu
from jax.sharding import PartitionSpec as P
from jax.experimental import pallas as pl
from jax.experimental.pallas import tpu as pltpu

MESH = pl.DeviceIdType.MESH
HALVINGS = 7
ORDER_A = [0, 4, 7, 1, 5, 8]
ORDER_B = [4, 7, 0, 5, 8, 1]
FULL_A = [2, 6]
FULL_B = [6, 2]


def _bit_partner(region, slab, b):
    if b < 3:
        v = (slab // (1 << b)) % 2
        return v, region, slab + (1 - 2 * v) * (1 << b)
    j = b - 3
    v = (region // (1 << j)) % 2
    return v, region + (1 - 2 * v) * (1 << j), slab


def _step(region, slab, core, ba, bb):
    va, ra, sa = _bit_partner(region, slab, ba)
    vb, rb, sb = _bit_partner(region, slab, bb)
    return va + core * (vb - va), ra + core * (rb - ra), sa + core * (sb - sa)


def allreduce_kernel(x_ref, hsrc_ref, o_ref, hout_ref, *scratch):
    HALVES = [x_ref.shape[0] >> (k + 1) for k in range(HALVINGS)]
    recvs = scratch[:9]
    send_sem, recv_sem, free_sem = scratch[9], scratch[10], scratch[11]
    codes, present, targets, hcopies, hcount = _halo_plan(hsrc_ref, hout_ref, scratch[12], scratch[13])
    hout_ref[...] = jnp.zeros(hout_ref.shape, hout_ref.dtype)
    region = lax.axis_index("region")
    slab = lax.axis_index("slab")
    core = region % 2
    steps = [(core, region + 1 - 2 * core, slab)]
    for ba, bb in zip(ORDER_A, ORDER_B):
        steps.append(_step(region, slab, core, ba, bb))
    fulls = [_step(region, slab, core, ba, bb) for ba, bb in zip(FULL_A, FULL_B)]

    barrier = pltpu.get_barrier_semaphore()
    for _, r, s in steps + fulls:
        pl.semaphore_signal(barrier, inc=1, device_id=(r, s), device_id_type=MESH)
    _halo_signal(barrier, codes, present, targets)
    pl.semaphore_wait(barrier, len(steps) + len(fulls) + hcount)
    _halo_start(codes, present, hcopies)

    off = 0
    offs = []
    for k, (v, r, s) in enumerate(steps):
        size = HALVES[k]
        keep = pl.multiple_of(off + v * size, 8)
        send = pl.multiple_of(off + (1 - v) * size, 8)
        src = x_ref if k == 0 else o_ref
        copy = pltpu.make_async_remote_copy(
            src_ref=src.at[pl.ds(send, size)], dst_ref=recvs[k],
            send_sem=send_sem.at[k], recv_sem=recv_sem.at[k],
            device_id=(r, s), device_id_type=MESH)
        copy.start()
        copy.wait()
        pl.semaphore_signal(free_sem.at[k], inc=1, device_id=(r, s), device_id_type=MESH)
        o_ref[pl.ds(keep, size)] = src[pl.ds(keep, size)] + recvs[k][...]
        off = keep
        offs.append(keep)
    last = HALVES[-1]
    for i, (v, r, s) in enumerate(fulls):
        k = len(steps) + i
        copy = pltpu.make_async_remote_copy(
            src_ref=o_ref.at[pl.ds(off, last)], dst_ref=recvs[k],
            send_sem=send_sem.at[k], recv_sem=recv_sem.at[k],
            device_id=(r, s), device_id_type=MESH)
        copy.start()
        copy.wait()
        o_ref[pl.ds(off, last)] = o_ref[pl.ds(off, last)] + recvs[k][...]
    base = len(steps) + len(fulls)
    for k in reversed(range(len(steps))):
        v, r, s = steps[k]
        size = HALVES[k]
        j = base + (len(steps) - 1 - k)
        copy = pltpu.make_async_remote_copy(
            src_ref=o_ref.at[pl.ds(offs[k], size)], dst_ref=o_ref.at[pl.ds(offs[k], size)],
            send_sem=send_sem.at[j], recv_sem=recv_sem.at[j],
            device_id=(r, s), device_id_type=MESH)
        pl.semaphore_wait(free_sem.at[k], 1)
        copy.start()
        copy.wait()
    _halo_finish(codes, present, hcopies)


def allreduce(x, hsrc):
    rows = x.shape[0]
    HALVES = [rows >> (k + 1) for k in range(HALVINGS)]
    n_copies = 9 + 7
    return pl.pallas_call(
        allreduce_kernel,
        out_shape=(jax.ShapeDtypeStruct((rows, 128), jnp.float32),
                   jax.ShapeDtypeStruct(hsrc.shape, hsrc.dtype)),
        in_specs=[pl.BlockSpec(memory_space=pltpu.VMEM)] * 2,
        out_specs=(pl.BlockSpec(memory_space=pltpu.VMEM), pl.BlockSpec(memory_space=pltpu.VMEM)),
        scratch_shapes=[pltpu.VMEM((h, 128), jnp.float32) for h in HALVES]
        + [pltpu.VMEM((HALVES[-1], 128), jnp.float32)] * 2
        + [pltpu.SemaphoreType.DMA((n_copies,)), pltpu.SemaphoreType.DMA((n_copies,))]
        + [pltpu.SemaphoreType.REGULAR((HALVINGS,))]
        + [pltpu.SemaphoreType.DMA((8,)), pltpu.SemaphoreType.DMA((8,))],
        compiler_params=pltpu.CompilerParams(collective_id=0, has_side_effects=True),
    )(x, hsrc)


def summed_everywhere(arrays, hsrc):
    flat = jnp.concatenate([a.reshape(-1) for a in arrays])
    unit = 128 * 8 << HALVINGS
    rows = -(-flat.size // unit) * unit // 128
    padded = jnp.pad(flat, (0, rows * 128 - flat.size)).reshape(rows, 128)
    total, hout = allreduce(padded, hsrc)
    total = total.reshape(-1)
    out, at = [], 0
    for a in arrays:
        out.append(total[at:at + a.size].reshape(a.shape))
        at += a.size
    return out, hout


def _exists(index, size):
    low = (index + size - 1) // size
    high = (2 * size - 3 - index) // (size - 1)
    return (low, 1, high)


def _halo_plan(src_ref, out_ref, send_sem, recv_sem):
    region = lax.axis_index("region")
    slab = lax.axis_index("slab")
    along_region = _exists(region, lax.axis_size("region"))
    along_slab = _exists(slab, lax.axis_size("slab"))
    codes = [c for c in range(9) if c != 4]
    slot = {c: i for i, c in enumerate(codes)}
    present, targets, copies = {}, {}, {}
    for c in codes:
        present[c] = along_region[c // 3] * along_slab[c % 3]
        targets[c] = (region + c // 3 - 1, slab + c % 3 - 1)
        copies[c] = pltpu.make_async_remote_copy(
            src_ref=src_ref.at[slot[c]], dst_ref=out_ref.at[slot[8 - c]],
            send_sem=send_sem.at[slot[c]], recv_sem=recv_sem.at[slot[8 - c]],
            device_id=targets[c], device_id_type=MESH)
    count = (along_region[0] + 1 + along_region[2]) * (along_slab[0] + 1 + along_slab[2]) - 1
    return codes, present, targets, copies, count


def _halo_signal(barrier, codes, present, targets):
    for c in codes:
        @pl.when(present[c] == 1)
        def _():
            pl.semaphore_signal(barrier, inc=1, device_id=targets[c], device_id_type=MESH)


def _halo_start(codes, present, copies):
    for c in codes:
        @pl.when(present[c] == 1)
        def _():
            copies[c].start()


def _halo_finish(codes, present, copies):
    for c in codes:
        @pl.when(present[c] == 1)
        def _():
            copies[8 - c].wait_recv()
            copies[c].wait_send()


def halo_kernel(src_ref, out_ref, send_sem, recv_sem):
    codes, present, targets, copies, count = _halo_plan(src_ref, out_ref, send_sem, recv_sem)
    out_ref[...] = jnp.zeros(out_ref.shape, out_ref.dtype)
    barrier = pltpu.get_barrier_semaphore()
    _halo_signal(barrier, codes, present, targets)
    pl.semaphore_wait(barrier, count)
    _halo_start(codes, present, copies)
    _halo_finish(codes, present, copies)


def halo_exchange(src, cid):
    return pl.pallas_call(
        halo_kernel,
        out_shape=jax.ShapeDtypeStruct(src.shape, src.dtype),
        in_specs=[pl.BlockSpec(memory_space=pltpu.VMEM)],
        out_specs=pl.BlockSpec(memory_space=pltpu.VMEM),
        scratch_shapes=[pltpu.SemaphoreType.DMA((8,)), pltpu.SemaphoreType.DMA((8,))],
        compiler_params=pltpu.CompilerParams(collective_id=cid, has_side_effects=True),
    )(src)


def extended_2(block, sides, width):
    for axis, dim in sides:
        count = lax.axis_size(axis)
        forward = [(i, i + 1) for i in range(count - 1)]
        backward = [(target, source) for source, target in forward]
        low = lax.ppermute(
            lax.slice_in_dim(block, block.shape[dim] - width, None, axis=dim), axis, forward
        )
        high = lax.ppermute(lax.slice_in_dim(block, 0, width, axis=dim), axis, backward)
        block = jnp.concatenate([low, block, high], axis=dim)
    return block


def _one_hot(pos_ref, o, rows):
    column = pos_ref[:, o:o + 1]
    lanes = lax.broadcasted_iota(jnp.int32, (column.shape[0], rows), 1)
    return (column == lanes).astype(jnp.bfloat16)


def conv_fwd_kernel(pos_ref, table_ref, w_ref, out_ref):
    channels = table_ref.shape[1]
    table = table_ref[...]
    total = jnp.zeros(out_ref.shape, jnp.float32)
    for o in range(pos_ref.shape[1]):
        picked = jnp.dot(_one_hot(pos_ref, o, table.shape[0]), table, preferred_element_type=jnp.float32)
        weight = w_ref[o * channels:(o + 1) * channels, :]
        total = total + jnp.dot(picked.astype(jnp.bfloat16), weight, preferred_element_type=jnp.float32)
    out_ref[...] = total


def conv_bwd_kernel(pos_ref, post_ref, table_ref, grad_ref, w_ref, tgrad_ref, wgrad_ref):
    channels = table_ref.shape[1]
    table = table_ref[...]
    grad = grad_ref[...]
    rows = table.shape[0]
    back = (((0,), (0,)), ((), ()))
    sublanes = lax.broadcasted_iota(jnp.int32, (rows, post_ref.shape[1]), 0)
    total = jnp.zeros((rows, 2 * channels), jnp.float32)
    for o in range(pos_ref.shape[1]):
        hot = _one_hot(pos_ref, o, rows)
        picked = jnp.dot(hot, table, preferred_element_type=jnp.float32).astype(jnp.bfloat16)
        wgrad_ref[o * channels:(o + 1) * channels, :] = lax.dot_general(
            picked, grad, back, preferred_element_type=jnp.float32)
        weight = w_ref[o * channels:(o + 1) * channels, :]
        spread = lax.dot_general(grad, weight, (((1,), (1,)), ((), ())), preferred_element_type=jnp.float32)
        high = spread.astype(jnp.bfloat16)
        low = (spread - high.astype(jnp.float32)).astype(jnp.bfloat16)
        hot_t = (sublanes == post_ref[o:o + 1, :]).astype(jnp.bfloat16)
        total = total + jnp.dot(hot_t, jnp.concatenate([high, low], axis=1),
                                preferred_element_type=jnp.float32)
    tgrad_ref[...] = total[:, :channels] + total[:, channels:]


def _vmem_call(kernel, outs, *args):
    return pl.pallas_call(
        kernel,
        out_shape=outs,
        in_specs=[pl.BlockSpec(memory_space=pltpu.VMEM)] * len(args),
        out_specs=jax.tree.map(lambda _: pl.BlockSpec(memory_space=pltpu.VMEM), outs),
    )(*args)


def on_device(features, neighbours, down_map, w_conv, w_down, coarse_grad):
    voxels, channels = features.shape
    offsets = neighbours.shape[1]
    rim = 64
    absent = neighbours >= 9 * voxels
    slot_idx = neighbours // voxels
    local_idx = neighbours - slot_idx * voxels
    halo_slot = jnp.where(slot_idx < 4, slot_idx, slot_idx - 1)
    compact = jnp.where(slot_idx == 4, 8 * rim + local_idx, halo_slot * rim + local_idx)
    positions = jnp.where(absent, -1, compact).astype(jnp.int32)
    sendable = jnp.broadcast_to(features[None, :rim], (8, rim, channels))
    halo = halo_exchange(sendable, 1).reshape(8 * rim, channels)
    table = jnp.concatenate([halo, features], axis=0)
    table_rows = table.shape[0]

    conv_out = _vmem_call(
        conv_fwd_kernel, jax.ShapeDtypeStruct((voxels, channels), jnp.float32), positions, table, w_conv)
    hidden = (features.astype(jnp.float32) + jax.nn.silu(conv_out)).astype(jnp.bfloat16)
    zero_row = jnp.zeros((1, channels), features.dtype)
    coarse_count, taps = down_map.shape
    down_local = jnp.minimum(down_map, voxels)
    hidden_pad = jnp.concatenate([hidden, zero_row], axis=0)
    coarse_rows = hidden_pad[down_local].reshape(coarse_count, taps * channels)
    coarse = jnp.dot(coarse_rows, w_down, preferred_element_type=jnp.float32).astype(jnp.bfloat16)
    coarse_back = jnp.dot(coarse_grad, w_down.T, preferred_element_type=jnp.float32)
    hidden_grad = jnp.zeros((voxels + 1, channels), jnp.float32)
    hidden_grad = hidden_grad.at[down_local.reshape(-1)].add(coarse_back.reshape(-1, channels))[
        :voxels
    ]
    down_wgrad = lax.dot_general(
        coarse_rows, coarse_grad, (((0,), (0,)), ((), ())), preferred_element_type=jnp.float32
    )
    sigmoid_y = jax.nn.sigmoid(conv_out)
    conv_grad = (hidden_grad * sigmoid_y * (1.0 + conv_out * (1.0 - sigmoid_y))).astype(
        jnp.bfloat16
    )
    table_grad, conv_wgrad = _vmem_call(
        conv_bwd_kernel,
        (jax.ShapeDtypeStruct((table_rows, channels), jnp.float32),
         jax.ShapeDtypeStruct(w_conv.shape, jnp.float32)),
        positions, positions.T, table, conv_grad, w_conv)
    halo_grad = table_grad[: 8 * rim].reshape(8, rim, channels)
    (conv_wgrad, down_wgrad), returned = summed_everywhere([conv_wgrad, down_wgrad], halo_grad)
    own_part = table_grad[8 * rim:]
    incoming = jnp.sum(returned, axis=0)
    grad_input = hidden_grad + own_part
    grad_input = grad_input.at[:rim].add(incoming)
    return (coarse, grad_input, conv_wgrad, down_wgrad)


def solution(mesh):
    in_specs = (
        P(("region", "slab"), None),
        P(("region", "slab"), None),
        P(("region", "slab"), None),
        P(),
        P(),
        P(("region", "slab"), None),
    )
    out_specs = (P(("region", "slab"), None), P(("region", "slab"), None), P(), P())
    return jax.shard_map(
        on_device, mesh=mesh, in_specs=in_specs, out_specs=out_specs, check_vma=False
    )
```

```python
import jax
import jax.numpy as jnp
from jax import lax
from jax.experimental import pallas as pl
from jax.experimental.pallas import tpu as pltpu
from jax.sharding import PartitionSpec as P
from jax.experimental import pallas as pl
from jax.experimental.pallas import tpu as pltpu

MESH = pl.DeviceIdType.MESH
HALVINGS = 7
ORDER_A = [0, 4, 7, 1, 5, 8]
ORDER_B = [4, 7, 0, 5, 8, 1]
FULL_A = [2, 6]
FULL_B = [6, 2]


def _bit_partner(region, slab, b):
    if b < 3:
        v = (slab // (1 << b)) % 2
        return v, region, slab + (1 - 2 * v) * (1 << b)
    j = b - 3
    v = (region // (1 << j)) % 2
    return v, region + (1 - 2 * v) * (1 << j), slab


def _step(region, slab, core, ba, bb):
    va, ra, sa = _bit_partner(region, slab, ba)
    vb, rb, sb = _bit_partner(region, slab, bb)
    return va + core * (vb - va), ra + core * (rb - ra), sa + core * (sb - sa)


def allreduce_kernel(x_ref, hsrc_ref, o_ref, hout_ref, *scratch):
    HALVES = [x_ref.shape[0] >> (k + 1) for k in range(HALVINGS)]
    recvs = scratch[:9]
    send_sem, recv_sem, free_sem = scratch[9], scratch[10], scratch[11]
    codes, present, targets, hcopies, hcount = _halo_plan(hsrc_ref, hout_ref, scratch[12], scratch[13])
    hout_ref[...] = jnp.zeros(hout_ref.shape, hout_ref.dtype)
    region = lax.axis_index("region")
    slab = lax.axis_index("slab")
    core = region % 2
    steps = [(core, region + 1 - 2 * core, slab)]
    for ba, bb in zip(ORDER_A, ORDER_B):
        steps.append(_step(region, slab, core, ba, bb))
    fulls = [_step(region, slab, core, ba, bb) for ba, bb in zip(FULL_A, FULL_B)]

    barrier = pltpu.get_barrier_semaphore()
    for _, r, s in steps + fulls:
        pl.semaphore_signal(barrier, inc=1, device_id=(r, s), device_id_type=MESH)
    _halo_signal(barrier, codes, present, targets)
    pl.semaphore_wait(barrier, len(steps) + len(fulls) + hcount)
    _halo_start(codes, present, hcopies)

    off = 0
    offs = []
    for k, (v, r, s) in enumerate(steps):
        size = HALVES[k]
        keep = pl.multiple_of(off + v * size, 8)
        send = pl.multiple_of(off + (1 - v) * size, 8)
        src = x_ref if k == 0 else o_ref
        copy = pltpu.make_async_remote_copy(
            src_ref=src.at[pl.ds(send, size)], dst_ref=recvs[k],
            send_sem=send_sem.at[k], recv_sem=recv_sem.at[k],
            device_id=(r, s), device_id_type=MESH)
        copy.start()
        copy.wait()
        pl.semaphore_signal(free_sem.at[k], inc=1, device_id=(r, s), device_id_type=MESH)
        o_ref[pl.ds(keep, size)] = src[pl.ds(keep, size)] + recvs[k][...]
        off = keep
        offs.append(keep)
    last = HALVES[-1]
    for i, (v, r, s) in enumerate(fulls):
        k = len(steps) + i
        copy = pltpu.make_async_remote_copy(
            src_ref=o_ref.at[pl.ds(off, last)], dst_ref=recvs[k],
            send_sem=send_sem.at[k], recv_sem=recv_sem.at[k],
            device_id=(r, s), device_id_type=MESH)
        copy.start()
        copy.wait()
        o_ref[pl.ds(off, last)] = o_ref[pl.ds(off, last)] + recvs[k][...]
    base = len(steps) + len(fulls)
    for k in reversed(range(len(steps))):
        v, r, s = steps[k]
        size = HALVES[k]
        j = base + (len(steps) - 1 - k)
        copy = pltpu.make_async_remote_copy(
            src_ref=o_ref.at[pl.ds(offs[k], size)], dst_ref=o_ref.at[pl.ds(offs[k], size)],
            send_sem=send_sem.at[j], recv_sem=recv_sem.at[j],
            device_id=(r, s), device_id_type=MESH)
        pl.semaphore_wait(free_sem.at[k], 1)
        copy.start()
        copy.wait()
    _halo_finish(codes, present, hcopies)


def allreduce(x, hsrc):
    rows = x.shape[0]
    HALVES = [rows >> (k + 1) for k in range(HALVINGS)]
    n_copies = 9 + 7
    return pl.pallas_call(
        allreduce_kernel,
        out_shape=(jax.ShapeDtypeStruct((rows, 128), jnp.float32),
                   jax.ShapeDtypeStruct(hsrc.shape, hsrc.dtype)),
        in_specs=[pl.BlockSpec(memory_space=pltpu.VMEM)] * 2,
        out_specs=(pl.BlockSpec(memory_space=pltpu.VMEM), pl.BlockSpec(memory_space=pltpu.VMEM)),
        scratch_shapes=[pltpu.VMEM((h, 128), jnp.float32) for h in HALVES]
        + [pltpu.VMEM((HALVES[-1], 128), jnp.float32)] * 2
        + [pltpu.SemaphoreType.DMA((n_copies,)), pltpu.SemaphoreType.DMA((n_copies,))]
        + [pltpu.SemaphoreType.REGULAR((HALVINGS,))]
        + [pltpu.SemaphoreType.DMA((8,)), pltpu.SemaphoreType.DMA((8,))],
        compiler_params=pltpu.CompilerParams(collective_id=0, has_side_effects=True),
    )(x, hsrc)


def summed_everywhere(arrays, hsrc):
    flat = jnp.concatenate([a.reshape(-1) for a in arrays])
    unit = 128 * 8 << HALVINGS
    rows = -(-flat.size // unit) * unit // 128
    padded = jnp.pad(flat, (0, rows * 128 - flat.size)).reshape(rows, 128)
    total, hout = allreduce(padded, hsrc)
    total = total.reshape(-1)
    out, at = [], 0
    for a in arrays:
        out.append(total[at:at + a.size].reshape(a.shape))
        at += a.size
    return out, hout


def _exists(index, size):
    low = (index + size - 1) // size
    high = (2 * size - 3 - index) // (size - 1)
    return (low, 1, high)


def _halo_plan(src_ref, out_ref, send_sem, recv_sem):
    region = lax.axis_index("region")
    slab = lax.axis_index("slab")
    along_region = _exists(region, lax.axis_size("region"))
    along_slab = _exists(slab, lax.axis_size("slab"))
    codes = [c for c in range(9) if c != 4]
    slot = {c: i for i, c in enumerate(codes)}
    present, targets, copies = {}, {}, {}
    for c in codes:
        present[c] = along_region[c // 3] * along_slab[c % 3]
        targets[c] = (region + c // 3 - 1, slab + c % 3 - 1)
        copies[c] = pltpu.make_async_remote_copy(
            src_ref=src_ref.at[slot[c]], dst_ref=out_ref.at[slot[8 - c]],
            send_sem=send_sem.at[slot[c]], recv_sem=recv_sem.at[slot[8 - c]],
            device_id=targets[c], device_id_type=MESH)
    count = (along_region[0] + 1 + along_region[2]) * (along_slab[0] + 1 + along_slab[2]) - 1
    return codes, present, targets, copies, count


def _halo_signal(barrier, codes, present, targets):
    for c in codes:
        @pl.when(present[c] == 1)
        def _():
            pl.semaphore_signal(barrier, inc=1, device_id=targets[c], device_id_type=MESH)


def _halo_start(codes, present, copies):
    for c in codes:
        @pl.when(present[c] == 1)
        def _():
            copies[c].start()


def _halo_finish(codes, present, copies):
    for c in codes:
        @pl.when(present[c] == 1)
        def _():
            copies[8 - c].wait_recv()
            copies[c].wait_send()


def halo_kernel(src_ref, out_ref, send_sem, recv_sem):
    codes, present, targets, copies, count = _halo_plan(src_ref, out_ref, send_sem, recv_sem)
    out_ref[...] = jnp.zeros(out_ref.shape, out_ref.dtype)
    barrier = pltpu.get_barrier_semaphore()
    _halo_signal(barrier, codes, present, targets)
    pl.semaphore_wait(barrier, count)
    _halo_start(codes, present, copies)
    _halo_finish(codes, present, copies)


def halo_exchange(src, cid):
    return pl.pallas_call(
        halo_kernel,
        out_shape=jax.ShapeDtypeStruct(src.shape, src.dtype),
        in_specs=[pl.BlockSpec(memory_space=pltpu.VMEM)],
        out_specs=pl.BlockSpec(memory_space=pltpu.VMEM),
        scratch_shapes=[pltpu.SemaphoreType.DMA((8,)), pltpu.SemaphoreType.DMA((8,))],
        compiler_params=pltpu.CompilerParams(collective_id=cid, has_side_effects=True),
    )(src)


def extended_2(block, sides, width):
    for axis, dim in sides:
        count = lax.axis_size(axis)
        forward = [(i, i + 1) for i in range(count - 1)]
        backward = [(target, source) for source, target in forward]
        low = lax.ppermute(
            lax.slice_in_dim(block, block.shape[dim] - width, None, axis=dim), axis, forward
        )
        high = lax.ppermute(lax.slice_in_dim(block, 0, width, axis=dim), axis, backward)
        block = jnp.concatenate([low, block, high], axis=dim)
    return block


def _one_hot(pos_ref, o, rows):
    column = pos_ref[:, o:o + 1]
    lanes = lax.broadcasted_iota(jnp.int32, (column.shape[0], rows), 1)
    return (column == lanes).astype(jnp.bfloat16)


def conv_fwd_kernel(pos_ref, table_ref, w_ref, out_ref):
    channels = table_ref.shape[1]
    table = table_ref[...]
    total = jnp.zeros(out_ref.shape, jnp.float32)
    for o in range(pos_ref.shape[1]):
        picked = jnp.dot(_one_hot(pos_ref, o, table.shape[0]), table, preferred_element_type=jnp.float32)
        weight = w_ref[o * channels:(o + 1) * channels, :]
        total = total + jnp.dot(picked.astype(jnp.bfloat16), weight, preferred_element_type=jnp.float32)
    out_ref[...] = total


def conv_bwd_kernel(post_ref, tablet_ref, grad_ref, w_ref, tgrad_ref, wgrad_ref):
    channels = tablet_ref.shape[0]
    table_t = tablet_ref[...]
    grad = grad_ref[...]
    rows = table_t.shape[1]
    sublanes = lax.broadcasted_iota(jnp.int32, (rows, post_ref.shape[1]), 0)
    total = jnp.zeros((rows, 2 * channels), jnp.float32)
    for o in range(post_ref.shape[0]):
        hot_t = (sublanes == post_ref[o:o + 1, :]).astype(jnp.bfloat16)
        picked_t = jnp.dot(table_t, hot_t, preferred_element_type=jnp.float32).astype(jnp.bfloat16)
        wgrad_ref[o * channels:(o + 1) * channels, :] = jnp.dot(
            picked_t, grad, preferred_element_type=jnp.float32)
        weight = w_ref[o * channels:(o + 1) * channels, :]
        spread = lax.dot_general(grad, weight, (((1,), (1,)), ((), ())), preferred_element_type=jnp.float32)
        high = spread.astype(jnp.bfloat16)
        low = (spread - high.astype(jnp.float32)).astype(jnp.bfloat16)
        total = total + jnp.dot(hot_t, jnp.concatenate([high, low], axis=1),
                                preferred_element_type=jnp.float32)
    tgrad_ref[...] = total[:, :channels] + total[:, channels:]


def _vmem_call(kernel, outs, *args):
    return pl.pallas_call(
        kernel,
        out_shape=outs,
        in_specs=[pl.BlockSpec(memory_space=pltpu.VMEM)] * len(args),
        out_specs=jax.tree.map(lambda _: pl.BlockSpec(memory_space=pltpu.VMEM), outs),
    )(*args)


def on_device(features, neighbours, down_map, w_conv, w_down, coarse_grad):
    voxels, channels = features.shape
    offsets = neighbours.shape[1]
    rim = 64
    absent = neighbours >= 9 * voxels
    slot_idx = neighbours // voxels
    local_idx = neighbours - slot_idx * voxels
    halo_slot = jnp.where(slot_idx < 4, slot_idx, slot_idx - 1)
    compact = jnp.where(slot_idx == 4, 8 * rim + local_idx, halo_slot * rim + local_idx)
    positions = jnp.where(absent, -1, compact).astype(jnp.int32)
    sendable = jnp.broadcast_to(features[None, :rim], (8, rim, channels))
    halo = halo_exchange(sendable, 1).reshape(8 * rim, channels)
    table = jnp.concatenate([halo, features], axis=0)
    table_rows = table.shape[0]

    conv_out = _vmem_call(
        conv_fwd_kernel, jax.ShapeDtypeStruct((voxels, channels), jnp.float32), positions, table, w_conv)
    hidden = (features.astype(jnp.float32) + jax.nn.silu(conv_out)).astype(jnp.bfloat16)
    zero_row = jnp.zeros((1, channels), features.dtype)
    coarse_count, taps = down_map.shape
    down_local = jnp.minimum(down_map, voxels)
    hidden_pad = jnp.concatenate([hidden, zero_row], axis=0)
    coarse_rows = hidden_pad[down_local].reshape(coarse_count, taps * channels)
    coarse = jnp.dot(coarse_rows, w_down, preferred_element_type=jnp.float32).astype(jnp.bfloat16)
    coarse_back = jnp.dot(coarse_grad, w_down.T, preferred_element_type=jnp.float32)
    hidden_grad = jnp.zeros((voxels + 1, channels), jnp.float32)
    hidden_grad = hidden_grad.at[down_local.reshape(-1)].add(coarse_back.reshape(-1, channels))[
        :voxels
    ]
    down_wgrad = lax.dot_general(
        coarse_rows, coarse_grad, (((0,), (0,)), ((), ())), preferred_element_type=jnp.float32
    )
    sigmoid_y = jax.nn.sigmoid(conv_out)
    conv_grad = (hidden_grad * sigmoid_y * (1.0 + conv_out * (1.0 - sigmoid_y))).astype(
        jnp.bfloat16
    )
    table_grad, conv_wgrad = _vmem_call(
        conv_bwd_kernel,
        (jax.ShapeDtypeStruct((table_rows, channels), jnp.float32),
         jax.ShapeDtypeStruct(w_conv.shape, jnp.float32)),
        positions.T, table.T, conv_grad, w_conv)
    halo_grad = table_grad[: 8 * rim].reshape(8, rim, channels)
    (conv_wgrad, down_wgrad), returned = summed_everywhere([conv_wgrad, down_wgrad], halo_grad)
    own_part = table_grad[8 * rim:]
    incoming = jnp.sum(returned, axis=0)
    grad_input = hidden_grad + own_part
    grad_input = grad_input.at[:rim].add(incoming)
    return (coarse, grad_input, conv_wgrad, down_wgrad)


def solution(mesh):
    in_specs = (
        P(("region", "slab"), None),
        P(("region", "slab"), None),
        P(("region", "slab"), None),
        P(),
        P(),
        P(("region", "slab"), None),
    )
    out_specs = (P(("region", "slab"), None), P(("region", "slab"), None), P(), P())
    return jax.shard_map(
        on_device, mesh=mesh, in_specs=in_specs, out_specs=out_specs, check_vma=False
    )
```

```python
import jax
import jax.numpy as jnp
from jax import lax
from jax.experimental import pallas as pl
from jax.experimental.pallas import tpu as pltpu
from jax.sharding import PartitionSpec as P
from jax.experimental import pallas as pl
from jax.experimental.pallas import tpu as pltpu

MESH = pl.DeviceIdType.MESH
HALVINGS = 7
ORDER_A = [0, 4, 7, 1, 5, 8]
ORDER_B = [4, 7, 0, 5, 8, 1]
FULL_A = [2, 6]
FULL_B = [6, 2]


def _bit_partner(region, slab, b):
    if b < 3:
        v = (slab // (1 << b)) % 2
        return v, region, slab + (1 - 2 * v) * (1 << b)
    j = b - 3
    v = (region // (1 << j)) % 2
    return v, region + (1 - 2 * v) * (1 << j), slab


def _step(region, slab, core, ba, bb):
    va, ra, sa = _bit_partner(region, slab, ba)
    vb, rb, sb = _bit_partner(region, slab, bb)
    return va + core * (vb - va), ra + core * (rb - ra), sa + core * (sb - sa)


def allreduce_kernel(x_ref, hsrc_ref, o_ref, hout_ref, *scratch):
    HALVES = [x_ref.shape[0] >> (k + 1) for k in range(HALVINGS)]
    recvs = scratch[:9]
    send_sem, recv_sem, free_sem = scratch[9], scratch[10], scratch[11]
    codes, present, targets, hcopies, hcount = _halo_plan(hsrc_ref, hout_ref, scratch[12], scratch[13])
    hout_ref[...] = jnp.zeros(hout_ref.shape, hout_ref.dtype)
    region = lax.axis_index("region")
    slab = lax.axis_index("slab")
    core = region % 2
    steps = [(core, region + 1 - 2 * core, slab)]
    for ba, bb in zip(ORDER_A, ORDER_B):
        steps.append(_step(region, slab, core, ba, bb))
    fulls = [_step(region, slab, core, ba, bb) for ba, bb in zip(FULL_A, FULL_B)]

    barrier = pltpu.get_barrier_semaphore()
    for _, r, s in steps + fulls:
        pl.semaphore_signal(barrier, inc=1, device_id=(r, s), device_id_type=MESH)
    _halo_signal(barrier, codes, present, targets)
    pl.semaphore_wait(barrier, len(steps) + len(fulls) + hcount)
    _halo_start(codes, present, hcopies)

    off = 0
    offs = []
    for k, (v, r, s) in enumerate(steps):
        size = HALVES[k]
        keep = pl.multiple_of(off + v * size, 8)
        send = pl.multiple_of(off + (1 - v) * size, 8)
        src = x_ref if k == 0 else o_ref
        copy = pltpu.make_async_remote_copy(
            src_ref=src.at[pl.ds(send, size)], dst_ref=recvs[k],
            send_sem=send_sem.at[k], recv_sem=recv_sem.at[k],
            device_id=(r, s), device_id_type=MESH)
        copy.start()
        copy.wait()
        pl.semaphore_signal(free_sem.at[k], inc=1, device_id=(r, s), device_id_type=MESH)
        o_ref[pl.ds(keep, size)] = src[pl.ds(keep, size)] + recvs[k][...]
        off = keep
        offs.append(keep)
    last = HALVES[-1]
    for i, (v, r, s) in enumerate(fulls):
        k = len(steps) + i
        copy = pltpu.make_async_remote_copy(
            src_ref=o_ref.at[pl.ds(off, last)], dst_ref=recvs[k],
            send_sem=send_sem.at[k], recv_sem=recv_sem.at[k],
            device_id=(r, s), device_id_type=MESH)
        copy.start()
        copy.wait()
        o_ref[pl.ds(off, last)] = o_ref[pl.ds(off, last)] + recvs[k][...]
    base = len(steps) + len(fulls)
    for k in reversed(range(len(steps))):
        v, r, s = steps[k]
        size = HALVES[k]
        j = base + (len(steps) - 1 - k)
        copy = pltpu.make_async_remote_copy(
            src_ref=o_ref.at[pl.ds(offs[k], size)], dst_ref=o_ref.at[pl.ds(offs[k], size)],
            send_sem=send_sem.at[j], recv_sem=recv_sem.at[j],
            device_id=(r, s), device_id_type=MESH)
        pl.semaphore_wait(free_sem.at[k], 1)
        copy.start()
        copy.wait()
    _halo_finish(codes, present, hcopies)


def allreduce(x, hsrc):
    rows = x.shape[0]
    HALVES = [rows >> (k + 1) for k in range(HALVINGS)]
    n_copies = 9 + 7
    return pl.pallas_call(
        allreduce_kernel,
        out_shape=(jax.ShapeDtypeStruct((rows, 128), jnp.float32),
                   jax.ShapeDtypeStruct(hsrc.shape, hsrc.dtype)),
        in_specs=[pl.BlockSpec(memory_space=pltpu.VMEM)] * 2,
        out_specs=(pl.BlockSpec(memory_space=pltpu.VMEM), pl.BlockSpec(memory_space=pltpu.VMEM)),
        scratch_shapes=[pltpu.VMEM((h, 128), jnp.float32) for h in HALVES]
        + [pltpu.VMEM((HALVES[-1], 128), jnp.float32)] * 2
        + [pltpu.SemaphoreType.DMA((n_copies,)), pltpu.SemaphoreType.DMA((n_copies,))]
        + [pltpu.SemaphoreType.REGULAR((HALVINGS,))]
        + [pltpu.SemaphoreType.DMA((8,)), pltpu.SemaphoreType.DMA((8,))],
        compiler_params=pltpu.CompilerParams(collective_id=0, has_side_effects=True),
    )(x, hsrc)


def summed_everywhere(arrays, hsrc):
    flat = jnp.concatenate([a.reshape(-1) for a in arrays])
    unit = 128 * 8 << HALVINGS
    rows = -(-flat.size // unit) * unit // 128
    padded = jnp.pad(flat, (0, rows * 128 - flat.size)).reshape(rows, 128)
    total, hout = allreduce(padded, hsrc)
    total = total.reshape(-1)
    out, at = [], 0
    for a in arrays:
        out.append(total[at:at + a.size].reshape(a.shape))
        at += a.size
    return out, hout


def _exists(index, size):
    low = (index + size - 1) // size
    high = (2 * size - 3 - index) // (size - 1)
    return (low, 1, high)


def _halo_plan(src_ref, out_ref, send_sem, recv_sem):
    region = lax.axis_index("region")
    slab = lax.axis_index("slab")
    along_region = _exists(region, lax.axis_size("region"))
    along_slab = _exists(slab, lax.axis_size("slab"))
    codes = [c for c in range(9) if c != 4]
    slot = {c: i for i, c in enumerate(codes)}
    present, targets, copies = {}, {}, {}
    for c in codes:
        present[c] = along_region[c // 3] * along_slab[c % 3]
        targets[c] = (region + c // 3 - 1, slab + c % 3 - 1)
        copies[c] = pltpu.make_async_remote_copy(
            src_ref=src_ref.at[slot[c]], dst_ref=out_ref.at[slot[8 - c]],
            send_sem=send_sem.at[slot[c]], recv_sem=recv_sem.at[slot[8 - c]],
            device_id=targets[c], device_id_type=MESH)
    count = (along_region[0] + 1 + along_region[2]) * (along_slab[0] + 1 + along_slab[2]) - 1
    return codes, present, targets, copies, count


def _halo_signal(barrier, codes, present, targets):
    for c in codes:
        @pl.when(present[c] == 1)
        def _():
            pl.semaphore_signal(barrier, inc=1, device_id=targets[c], device_id_type=MESH)


def _halo_start(codes, present, copies):
    for c in codes:
        @pl.when(present[c] == 1)
        def _():
            copies[c].start()


def _halo_finish(codes, present, copies):
    for c in codes:
        @pl.when(present[c] == 1)
        def _():
            copies[8 - c].wait_recv()
            copies[c].wait_send()


def halo_kernel(src_ref, out_ref, send_sem, recv_sem):
    codes, present, targets, copies, count = _halo_plan(src_ref, out_ref, send_sem, recv_sem)
    out_ref[...] = jnp.zeros(out_ref.shape, out_ref.dtype)
    barrier = pltpu.get_barrier_semaphore()
    _halo_signal(barrier, codes, present, targets)
    pl.semaphore_wait(barrier, count)
    _halo_start(codes, present, copies)
    _halo_finish(codes, present, copies)


def halo_exchange(src, cid):
    return pl.pallas_call(
        halo_kernel,
        out_shape=jax.ShapeDtypeStruct(src.shape, src.dtype),
        in_specs=[pl.BlockSpec(memory_space=pltpu.VMEM)],
        out_specs=pl.BlockSpec(memory_space=pltpu.VMEM),
        scratch_shapes=[pltpu.SemaphoreType.DMA((8,)), pltpu.SemaphoreType.DMA((8,))],
        compiler_params=pltpu.CompilerParams(collective_id=cid, has_side_effects=True),
    )(src)


def extended_2(block, sides, width):
    for axis, dim in sides:
        count = lax.axis_size(axis)
        forward = [(i, i + 1) for i in range(count - 1)]
        backward = [(target, source) for source, target in forward]
        low = lax.ppermute(
            lax.slice_in_dim(block, block.shape[dim] - width, None, axis=dim), axis, forward
        )
        high = lax.ppermute(lax.slice_in_dim(block, 0, width, axis=dim), axis, backward)
        block = jnp.concatenate([low, block, high], axis=dim)
    return block


def _one_hot(pos_ref, o, rows):
    column = pos_ref[:, o:o + 1]
    lanes = lax.broadcasted_iota(jnp.int32, (column.shape[0], rows), 1)
    return (column == lanes).astype(jnp.bfloat16)


def conv_fwd_kernel(pos_ref, table_ref, w_ref, out_ref):
    channels = table_ref.shape[1]
    table = table_ref[...]
    total = jnp.zeros(out_ref.shape, jnp.float32)
    for o in range(pos_ref.shape[1]):
        picked = jnp.dot(_one_hot(pos_ref, o, table.shape[0]), table, preferred_element_type=jnp.float32)
        weight = w_ref[o * channels:(o + 1) * channels, :]
        total = total + jnp.dot(picked.astype(jnp.bfloat16), weight, preferred_element_type=jnp.float32)
    out_ref[...] = total


def conv_bwd_kernel(post_ref, tablet_ref, grad_ref, w_ref, tgrad_ref, wgrad_ref):
    channels = tablet_ref.shape[0]
    table_t = tablet_ref[...]
    grad = grad_ref[...]
    rows = table_t.shape[1]
    sublanes = lax.broadcasted_iota(jnp.int32, (rows, post_ref.shape[1]), 0)
    total = jnp.zeros((rows, 2 * channels), jnp.float32)
    for o in range(post_ref.shape[0]):
        hot_t = (sublanes == post_ref[o:o + 1, :]).astype(jnp.bfloat16)
        picked_t = jnp.dot(table_t, hot_t, preferred_element_type=jnp.float32).astype(jnp.bfloat16)
        wgrad_ref[o * channels:(o + 1) * channels, :] = jnp.dot(
            picked_t, grad, preferred_element_type=jnp.float32)
        weight = w_ref[o * channels:(o + 1) * channels, :]
        spread = lax.dot_general(grad, weight, (((1,), (1,)), ((), ())), preferred_element_type=jnp.float32)
        high = spread.astype(jnp.bfloat16)
        low = (spread - high.astype(jnp.float32)).astype(jnp.bfloat16)
        total = total + jnp.dot(hot_t, jnp.concatenate([high, low], axis=1),
                                preferred_element_type=jnp.float32)
    tgrad_ref[...] = total[:, :channels] + total[:, channels:]


def down_kernel(down_ref, downt_ref, hidden_ref, hiddent_ref, w_ref, cgrad_ref,
                coarse_ref, hgrad_ref, wgrad_ref):
    channels = hidden_ref.shape[1]
    voxels = hidden_ref.shape[0]
    coarse_count = down_ref.shape[0]
    hidden = hidden_ref[...]
    hidden_t = hiddent_ref[...]
    cgrad = cgrad_ref[...]
    lanes = lax.broadcasted_iota(jnp.int32, (coarse_count, voxels), 1)
    sublanes = lax.broadcasted_iota(jnp.int32, (voxels, coarse_count), 0)
    coarse = jnp.zeros(coarse_ref.shape, jnp.float32)
    spread_total = jnp.zeros((voxels, 2 * channels), jnp.float32)
    for t in range(down_ref.shape[1]):
        hot = (lanes == down_ref[:, t:t + 1]).astype(jnp.bfloat16)
        hot_t = (sublanes == downt_ref[t:t + 1, :]).astype(jnp.bfloat16)
        weight = w_ref[t * channels:(t + 1) * channels, :]
        picked = jnp.dot(hot, hidden, preferred_element_type=jnp.float32).astype(jnp.bfloat16)
        coarse = coarse + jnp.dot(picked, weight, preferred_element_type=jnp.float32)
        picked_t = jnp.dot(hidden_t, hot_t, preferred_element_type=jnp.float32).astype(jnp.bfloat16)
        wgrad_ref[t * channels:(t + 1) * channels, :] = jnp.dot(
            picked_t, cgrad, preferred_element_type=jnp.float32)
        back = lax.dot_general(cgrad, weight, (((1,), (1,)), ((), ())), preferred_element_type=jnp.float32)
        high = back.astype(jnp.bfloat16)
        low = (back - high.astype(jnp.float32)).astype(jnp.bfloat16)
        spread_total = spread_total + jnp.dot(
            hot_t, jnp.concatenate([high, low], axis=1), preferred_element_type=jnp.float32)
    coarse_ref[...] = coarse.astype(coarse_ref.dtype)
    hgrad_ref[...] = spread_total[:, :channels] + spread_total[:, channels:]


def _vmem_call(kernel, outs, *args):
    return pl.pallas_call(
        kernel,
        out_shape=outs,
        in_specs=[pl.BlockSpec(memory_space=pltpu.VMEM)] * len(args),
        out_specs=jax.tree.map(lambda _: pl.BlockSpec(memory_space=pltpu.VMEM), outs),
    )(*args)


def on_device(features, neighbours, down_map, w_conv, w_down, coarse_grad):
    voxels, channels = features.shape
    offsets = neighbours.shape[1]
    rim = 64
    absent = neighbours >= 9 * voxels
    slot_idx = neighbours // voxels
    local_idx = neighbours - slot_idx * voxels
    halo_slot = jnp.where(slot_idx < 4, slot_idx, slot_idx - 1)
    compact = jnp.where(slot_idx == 4, 8 * rim + local_idx, halo_slot * rim + local_idx)
    positions = jnp.where(absent, -1, compact).astype(jnp.int32)
    sendable = jnp.broadcast_to(features[None, :rim], (8, rim, channels))
    halo = halo_exchange(sendable, 1).reshape(8 * rim, channels)
    table = jnp.concatenate([halo, features], axis=0)
    table_rows = table.shape[0]

    conv_out = _vmem_call(
        conv_fwd_kernel, jax.ShapeDtypeStruct((voxels, channels), jnp.float32), positions, table, w_conv)
    hidden = (features.astype(jnp.float32) + jax.nn.silu(conv_out)).astype(jnp.bfloat16)
    coarse, hidden_grad, down_wgrad = _vmem_call(
        down_kernel,
        (jax.ShapeDtypeStruct((down_map.shape[0], w_down.shape[1]), jnp.bfloat16),
         jax.ShapeDtypeStruct((voxels, channels), jnp.float32),
         jax.ShapeDtypeStruct(w_down.shape, jnp.float32)),
        down_map, down_map.T, hidden, hidden.T, w_down, coarse_grad)
    sigmoid_y = jax.nn.sigmoid(conv_out)
    conv_grad = (hidden_grad * sigmoid_y * (1.0 + conv_out * (1.0 - sigmoid_y))).astype(
        jnp.bfloat16
    )
    table_grad, conv_wgrad = _vmem_call(
        conv_bwd_kernel,
        (jax.ShapeDtypeStruct((table_rows, channels), jnp.float32),
         jax.ShapeDtypeStruct(w_conv.shape, jnp.float32)),
        positions.T, table.T, conv_grad, w_conv)
    halo_grad = table_grad[: 8 * rim].reshape(8, rim, channels)
    (conv_wgrad, down_wgrad), returned = summed_everywhere([conv_wgrad, down_wgrad], halo_grad)
    own_part = table_grad[8 * rim:]
    incoming = jnp.sum(returned, axis=0)
    grad_input = hidden_grad + own_part
    grad_input = grad_input.at[:rim].add(incoming)
    return (coarse, grad_input, conv_wgrad, down_wgrad)


def solution(mesh):
    in_specs = (
        P(("region", "slab"), None),
        P(("region", "slab"), None),
        P(("region", "slab"), None),
        P(),
        P(),
        P(("region", "slab"), None),
    )
    out_specs = (P(("region", "slab"), None), P(("region", "slab"), None), P(), P())
    return jax.shard_map(
        on_device, mesh=mesh, in_specs=in_specs, out_specs=out_specs, check_vma=False
    )
```

```python
import jax
import jax.numpy as jnp
from jax import lax
from jax.experimental import pallas as pl
from jax.experimental.pallas import tpu as pltpu
from jax.sharding import PartitionSpec as P
from jax.experimental import pallas as pl
from jax.experimental.pallas import tpu as pltpu

MESH = pl.DeviceIdType.MESH
HALVINGS = 7
ORDER_A = [0, 4, 7, 1, 5, 8]
ORDER_B = [4, 7, 0, 5, 8, 1]
FULL_A = [2, 6]
FULL_B = [6, 2]


def _bit_partner(region, slab, b):
    if b < 3:
        v = (slab // (1 << b)) % 2
        return v, region, slab + (1 - 2 * v) * (1 << b)
    j = b - 3
    v = (region // (1 << j)) % 2
    return v, region + (1 - 2 * v) * (1 << j), slab


def _step(region, slab, core, ba, bb):
    va, ra, sa = _bit_partner(region, slab, ba)
    vb, rb, sb = _bit_partner(region, slab, bb)
    return va + core * (vb - va), ra + core * (rb - ra), sa + core * (sb - sa)


def allreduce_kernel(x_ref, hsrc_ref, o_ref, hout_ref, *scratch):
    HALVES = [x_ref.shape[0] >> (k + 1) for k in range(HALVINGS)]
    recvs = scratch[:9]
    send_sem, recv_sem, free_sem = scratch[9], scratch[10], scratch[11]
    codes, present, targets, hcopies, hcount = _halo_plan(hsrc_ref, hout_ref, scratch[12], scratch[13])
    hout_ref[...] = jnp.zeros(hout_ref.shape, hout_ref.dtype)
    region = lax.axis_index("region")
    slab = lax.axis_index("slab")
    core = region % 2
    steps = [(core, region + 1 - 2 * core, slab)]
    for ba, bb in zip(ORDER_A, ORDER_B):
        steps.append(_step(region, slab, core, ba, bb))
    fulls = [_step(region, slab, core, ba, bb) for ba, bb in zip(FULL_A, FULL_B)]

    barrier = pltpu.get_barrier_semaphore()
    for _, r, s in steps + fulls:
        pl.semaphore_signal(barrier, inc=1, device_id=(r, s), device_id_type=MESH)
    _halo_signal(barrier, codes, present, targets)
    pl.semaphore_wait(barrier, len(steps) + len(fulls) + hcount)
    _halo_start(codes, present, hcopies)

    off = 0
    offs = []
    for k, (v, r, s) in enumerate(steps):
        size = HALVES[k]
        keep = pl.multiple_of(off + v * size, 8)
        send = pl.multiple_of(off + (1 - v) * size, 8)
        src = x_ref if k == 0 else o_ref
        copy = pltpu.make_async_remote_copy(
            src_ref=src.at[pl.ds(send, size)], dst_ref=recvs[k],
            send_sem=send_sem.at[k], recv_sem=recv_sem.at[k],
            device_id=(r, s), device_id_type=MESH)
        copy.start()
        copy.wait()
        pl.semaphore_signal(free_sem.at[k], inc=1, device_id=(r, s), device_id_type=MESH)
        o_ref[pl.ds(keep, size)] = src[pl.ds(keep, size)] + recvs[k][...]
        off = keep
        offs.append(keep)
    last = HALVES[-1]
    for i, (v, r, s) in enumerate(fulls):
        k = len(steps) + i
        copy = pltpu.make_async_remote_copy(
            src_ref=o_ref.at[pl.ds(off, last)], dst_ref=recvs[k],
            send_sem=send_sem.at[k], recv_sem=recv_sem.at[k],
            device_id=(r, s), device_id_type=MESH)
        copy.start()
        copy.wait()
        o_ref[pl.ds(off, last)] = o_ref[pl.ds(off, last)] + recvs[k][...]
    base = len(steps) + len(fulls)
    for k in reversed(range(len(steps))):
        v, r, s = steps[k]
        size = HALVES[k]
        j = base + (len(steps) - 1 - k)
        copy = pltpu.make_async_remote_copy(
            src_ref=o_ref.at[pl.ds(offs[k], size)], dst_ref=o_ref.at[pl.ds(offs[k], size)],
            send_sem=send_sem.at[j], recv_sem=recv_sem.at[j],
            device_id=(r, s), device_id_type=MESH)
        pl.semaphore_wait(free_sem.at[k], 1)
        copy.start()
        copy.wait()
    _halo_finish(codes, present, hcopies)


def allreduce(x, hsrc):
    rows = x.shape[0]
    HALVES = [rows >> (k + 1) for k in range(HALVINGS)]
    n_copies = 9 + 7
    return pl.pallas_call(
        allreduce_kernel,
        out_shape=(jax.ShapeDtypeStruct((rows, 128), jnp.float32),
                   jax.ShapeDtypeStruct(hsrc.shape, hsrc.dtype)),
        in_specs=[pl.BlockSpec(memory_space=pltpu.VMEM)] * 2,
        out_specs=(pl.BlockSpec(memory_space=pltpu.VMEM), pl.BlockSpec(memory_space=pltpu.VMEM)),
        scratch_shapes=[pltpu.VMEM((h, 128), jnp.float32) for h in HALVES]
        + [pltpu.VMEM((HALVES[-1], 128), jnp.float32)] * 2
        + [pltpu.SemaphoreType.DMA((n_copies,)), pltpu.SemaphoreType.DMA((n_copies,))]
        + [pltpu.SemaphoreType.REGULAR((HALVINGS,))]
        + [pltpu.SemaphoreType.DMA((8,)), pltpu.SemaphoreType.DMA((8,))],
        compiler_params=pltpu.CompilerParams(collective_id=0, has_side_effects=True),
    )(x, hsrc)


def summed_everywhere(arrays, hsrc):
    flat = jnp.concatenate([a.reshape(-1) for a in arrays])
    unit = 128 * 8 << HALVINGS
    rows = -(-flat.size // unit) * unit // 128
    padded = jnp.pad(flat, (0, rows * 128 - flat.size)).reshape(rows, 128)
    total, hout = allreduce(padded, hsrc)
    total = total.reshape(-1)
    out, at = [], 0
    for a in arrays:
        out.append(total[at:at + a.size].reshape(a.shape))
        at += a.size
    return out, hout


def _exists(index, size):
    low = (index + size - 1) // size
    high = (2 * size - 3 - index) // (size - 1)
    return (low, 1, high)


def _halo_plan(src_ref, out_ref, send_sem, recv_sem):
    region = lax.axis_index("region")
    slab = lax.axis_index("slab")
    along_region = _exists(region, lax.axis_size("region"))
    along_slab = _exists(slab, lax.axis_size("slab"))
    codes = [c for c in range(9) if c != 4]
    slot = {c: i for i, c in enumerate(codes)}
    present, targets, copies = {}, {}, {}
    for c in codes:
        present[c] = along_region[c // 3] * along_slab[c % 3]
        targets[c] = (region + c // 3 - 1, slab + c % 3 - 1)
        copies[c] = pltpu.make_async_remote_copy(
            src_ref=src_ref.at[slot[c]], dst_ref=out_ref.at[slot[8 - c]],
            send_sem=send_sem.at[slot[c]], recv_sem=recv_sem.at[slot[8 - c]],
            device_id=targets[c], device_id_type=MESH)
    count = (along_region[0] + 1 + along_region[2]) * (along_slab[0] + 1 + along_slab[2]) - 1
    return codes, present, targets, copies, count


def _halo_signal(barrier, codes, present, targets):
    for c in codes:
        @pl.when(present[c] == 1)
        def _():
            pl.semaphore_signal(barrier, inc=1, device_id=targets[c], device_id_type=MESH)


def _halo_start(codes, present, copies):
    for c in codes:
        @pl.when(present[c] == 1)
        def _():
            copies[c].start()


def _halo_finish(codes, present, copies):
    for c in codes:
        @pl.when(present[c] == 1)
        def _():
            copies[8 - c].wait_recv()
            copies[c].wait_send()


def halo_kernel(src_ref, out_ref, send_sem, recv_sem):
    codes, present, targets, copies, count = _halo_plan(src_ref, out_ref, send_sem, recv_sem)
    out_ref[...] = jnp.zeros(out_ref.shape, out_ref.dtype)
    barrier = pltpu.get_barrier_semaphore()
    _halo_signal(barrier, codes, present, targets)
    pl.semaphore_wait(barrier, count)
    _halo_start(codes, present, copies)
    _halo_finish(codes, present, copies)


def halo_exchange(src, cid):
    return pl.pallas_call(
        halo_kernel,
        out_shape=jax.ShapeDtypeStruct(src.shape, src.dtype),
        in_specs=[pl.BlockSpec(memory_space=pltpu.VMEM)],
        out_specs=pl.BlockSpec(memory_space=pltpu.VMEM),
        scratch_shapes=[pltpu.SemaphoreType.DMA((8,)), pltpu.SemaphoreType.DMA((8,))],
        compiler_params=pltpu.CompilerParams(collective_id=cid, has_side_effects=True),
    )(src)


def extended_2(block, sides, width):
    for axis, dim in sides:
        count = lax.axis_size(axis)
        forward = [(i, i + 1) for i in range(count - 1)]
        backward = [(target, source) for source, target in forward]
        low = lax.ppermute(
            lax.slice_in_dim(block, block.shape[dim] - width, None, axis=dim), axis, forward
        )
        high = lax.ppermute(lax.slice_in_dim(block, 0, width, axis=dim), axis, backward)
        block = jnp.concatenate([low, block, high], axis=dim)
    return block


def _one_hot(pos_ref, o, rows):
    column = pos_ref[:, o:o + 1]
    lanes = lax.broadcasted_iota(jnp.int32, (column.shape[0], rows), 1)
    return (column == lanes).astype(jnp.bfloat16)


def conv_fwd_kernel(pos_ref, table_ref, w_ref, out_ref):
    channels = table_ref.shape[1]
    table = table_ref[...]
    total = jnp.zeros(out_ref.shape, jnp.float32)
    for o in range(pos_ref.shape[1]):
        picked = jnp.dot(_one_hot(pos_ref, o, table.shape[0]), table, preferred_element_type=jnp.float32)
        weight = w_ref[o * channels:(o + 1) * channels, :]
        total = total + jnp.dot(picked.astype(jnp.bfloat16), weight, preferred_element_type=jnp.float32)
    out_ref[...] = total


def conv_fwd_halo_kernel(pos_ref, own_ref, src_ref, w_ref, out_ref, hout_ref, send_sem, recv_sem):
    channels = own_ref.shape[1]
    voxels = own_ref.shape[0]
    halo_rows = hout_ref.shape[0] * hout_ref.shape[1]
    codes, present, targets, copies, count = _halo_plan(src_ref, hout_ref, send_sem, recv_sem)
    hout_ref[...] = jnp.zeros(hout_ref.shape, hout_ref.dtype)
    barrier = pltpu.get_barrier_semaphore()
    _halo_signal(barrier, codes, present, targets)
    pl.semaphore_wait(barrier, count)
    _halo_start(codes, present, copies)
    own = own_ref[...]
    own_lanes = lax.broadcasted_iota(jnp.int32, (pos_ref.shape[0], voxels), 1) + halo_rows
    total = jnp.zeros(out_ref.shape, jnp.float32)
    for o in range(pos_ref.shape[1]):
        hot = (pos_ref[:, o:o + 1] == own_lanes).astype(jnp.bfloat16)
        picked = jnp.dot(hot, own, preferred_element_type=jnp.float32)
        weight = w_ref[o * channels:(o + 1) * channels, :]
        total = total + jnp.dot(picked.astype(jnp.bfloat16), weight, preferred_element_type=jnp.float32)
    _halo_finish(codes, present, copies)
    halo = hout_ref[...].reshape(halo_rows, channels)
    for o in range(pos_ref.shape[1]):
        picked = jnp.dot(_one_hot(pos_ref, o, halo_rows), halo, preferred_element_type=jnp.float32)
        weight = w_ref[o * channels:(o + 1) * channels, :]
        total = total + jnp.dot(picked.astype(jnp.bfloat16), weight, preferred_element_type=jnp.float32)
    out_ref[...] = total


def conv_bwd_kernel(post_ref, tablet_ref, grad_ref, w_ref, tgrad_ref, wgrad_ref):
    channels = tablet_ref.shape[0]
    table_t = tablet_ref[...]
    grad = grad_ref[...]
    rows = table_t.shape[1]
    sublanes = lax.broadcasted_iota(jnp.int32, (rows, post_ref.shape[1]), 0)
    total = jnp.zeros((rows, 2 * channels), jnp.float32)
    for o in range(post_ref.shape[0]):
        hot_t = (sublanes == post_ref[o:o + 1, :]).astype(jnp.bfloat16)
        picked_t = jnp.dot(table_t, hot_t, preferred_element_type=jnp.float32).astype(jnp.bfloat16)
        wgrad_ref[o * channels:(o + 1) * channels, :] = jnp.dot(
            picked_t, grad, preferred_element_type=jnp.float32)
        weight = w_ref[o * channels:(o + 1) * channels, :]
        spread = lax.dot_general(grad, weight, (((1,), (1,)), ((), ())), preferred_element_type=jnp.float32)
        high = spread.astype(jnp.bfloat16)
        low = (spread - high.astype(jnp.float32)).astype(jnp.bfloat16)
        total = total + jnp.dot(hot_t, jnp.concatenate([high, low], axis=1),
                                preferred_element_type=jnp.float32)
    tgrad_ref[...] = total[:, :channels] + total[:, channels:]


def _vmem_call(kernel, outs, *args):
    return pl.pallas_call(
        kernel,
        out_shape=outs,
        in_specs=[pl.BlockSpec(memory_space=pltpu.VMEM)] * len(args),
        out_specs=jax.tree.map(lambda _: pl.BlockSpec(memory_space=pltpu.VMEM), outs),
    )(*args)


def on_device(features, neighbours, down_map, w_conv, w_down, coarse_grad):
    voxels, channels = features.shape
    offsets = neighbours.shape[1]
    rim = 64
    absent = neighbours >= 9 * voxels
    slot_idx = neighbours // voxels
    local_idx = neighbours - slot_idx * voxels
    halo_slot = jnp.where(slot_idx < 4, slot_idx, slot_idx - 1)
    compact = jnp.where(slot_idx == 4, 8 * rim + local_idx, halo_slot * rim + local_idx)
    positions = jnp.where(absent, -1, compact).astype(jnp.int32)
    sendable = jnp.broadcast_to(features[None, :rim], (8, rim, channels))
    conv_out, halo = pl.pallas_call(
        conv_fwd_halo_kernel,
        out_shape=(jax.ShapeDtypeStruct((voxels, channels), jnp.float32),
                   jax.ShapeDtypeStruct(sendable.shape, sendable.dtype)),
        in_specs=[pl.BlockSpec(memory_space=pltpu.VMEM)] * 4,
        out_specs=(pl.BlockSpec(memory_space=pltpu.VMEM), pl.BlockSpec(memory_space=pltpu.VMEM)),
        scratch_shapes=[pltpu.SemaphoreType.DMA((8,)), pltpu.SemaphoreType.DMA((8,))],
        compiler_params=pltpu.CompilerParams(collective_id=1, has_side_effects=True),
    )(positions, features, sendable, w_conv)
    table = jnp.concatenate([halo.reshape(8 * rim, channels), features], axis=0)
    table_rows = table.shape[0]
    hidden = (features.astype(jnp.float32) + jax.nn.silu(conv_out)).astype(jnp.bfloat16)
    zero_row = jnp.zeros((1, channels), features.dtype)
    coarse_count, taps = down_map.shape
    down_local = jnp.minimum(down_map, voxels)
    hidden_pad = jnp.concatenate([hidden, zero_row], axis=0)
    coarse_rows = hidden_pad[down_local].reshape(coarse_count, taps * channels)
    coarse = jnp.dot(coarse_rows, w_down, preferred_element_type=jnp.float32).astype(jnp.bfloat16)
    coarse_back = jnp.dot(coarse_grad, w_down.T, preferred_element_type=jnp.float32)
    hidden_grad = jnp.zeros((voxels + 1, channels), jnp.float32)
    hidden_grad = hidden_grad.at[down_local.reshape(-1)].add(coarse_back.reshape(-1, channels))[
        :voxels
    ]
    down_wgrad = lax.dot_general(
        coarse_rows, coarse_grad, (((0,), (0,)), ((), ())), preferred_element_type=jnp.float32
    )
    sigmoid_y = jax.nn.sigmoid(conv_out)
    conv_grad = (hidden_grad * sigmoid_y * (1.0 + conv_out * (1.0 - sigmoid_y))).astype(
        jnp.bfloat16
    )
    table_grad, conv_wgrad = _vmem_call(
        conv_bwd_kernel,
        (jax.ShapeDtypeStruct((table_rows, channels), jnp.float32),
         jax.ShapeDtypeStruct(w_conv.shape, jnp.float32)),
        positions.T, table.T, conv_grad, w_conv)
    halo_grad = table_grad[: 8 * rim].reshape(8, rim, channels)
    (conv_wgrad, down_wgrad), returned = summed_everywhere([conv_wgrad, down_wgrad], halo_grad)
    own_part = table_grad[8 * rim:]
    incoming = jnp.sum(returned, axis=0)
    grad_input = hidden_grad + own_part
    grad_input = grad_input.at[:rim].add(incoming)
    return (coarse, grad_input, conv_wgrad, down_wgrad)


def solution(mesh):
    in_specs = (
        P(("region", "slab"), None),
        P(("region", "slab"), None),
        P(("region", "slab"), None),
        P(),
        P(),
        P(("region", "slab"), None),
    )
    out_specs = (P(("region", "slab"), None), P(("region", "slab"), None), P(), P())
    return jax.shard_map(
        on_device, mesh=mesh, in_specs=in_specs, out_specs=out_specs, check_vma=False
    )
```

```python
import jax
import jax.numpy as jnp
from jax import lax
from jax.experimental import pallas as pl
from jax.experimental.pallas import tpu as pltpu
from jax.sharding import PartitionSpec as P
from jax.experimental import pallas as pl
from jax.experimental.pallas import tpu as pltpu

MESH = pl.DeviceIdType.MESH
HALVINGS = 7
ORDER_A = [0, 4, 7, 1, 5, 8]
ORDER_B = [4, 7, 0, 5, 8, 1]
FULL_A = [2, 6]
FULL_B = [6, 2]


def _bit_partner(region, slab, b):
    if b < 3:
        v = (slab // (1 << b)) % 2
        return v, region, slab + (1 - 2 * v) * (1 << b)
    j = b - 3
    v = (region // (1 << j)) % 2
    return v, region + (1 - 2 * v) * (1 << j), slab


def _step(region, slab, core, ba, bb):
    va, ra, sa = _bit_partner(region, slab, ba)
    vb, rb, sb = _bit_partner(region, slab, bb)
    return va + core * (vb - va), ra + core * (rb - ra), sa + core * (sb - sa)


def allreduce_kernel(x_ref, hsrc_ref, o_ref, hout_ref, *scratch):
    HALVES = [x_ref.shape[0] >> (k + 1) for k in range(HALVINGS)]
    recvs = scratch[:9]
    send_sem, recv_sem, free_sem = scratch[9], scratch[10], scratch[11]
    codes, present, targets, hcopies, hcount = _halo_plan(hsrc_ref, hout_ref, scratch[12], scratch[13])
    hout_ref[...] = jnp.zeros(hout_ref.shape, hout_ref.dtype)
    region = lax.axis_index("region")
    slab = lax.axis_index("slab")
    core = region % 2
    steps = [(core, region + 1 - 2 * core, slab)]
    for ba, bb in zip(ORDER_A, ORDER_B):
        steps.append(_step(region, slab, core, ba, bb))
    fulls = [_step(region, slab, core, ba, bb) for ba, bb in zip(FULL_A, FULL_B)]

    barrier = pltpu.get_barrier_semaphore()
    for _, r, s in steps + fulls:
        pl.semaphore_signal(barrier, inc=1, device_id=(r, s), device_id_type=MESH)
    _halo_signal(barrier, codes, present, targets)
    pl.semaphore_wait(barrier, len(steps) + len(fulls) + hcount)
    _halo_start(codes, present, hcopies)

    off = 0
    offs = []
    for k, (v, r, s) in enumerate(steps):
        size = HALVES[k]
        keep = pl.multiple_of(off + v * size, 8)
        send = pl.multiple_of(off + (1 - v) * size, 8)
        src = x_ref if k == 0 else o_ref
        copy = pltpu.make_async_remote_copy(
            src_ref=src.at[pl.ds(send, size)], dst_ref=recvs[k],
            send_sem=send_sem.at[k], recv_sem=recv_sem.at[k],
            device_id=(r, s), device_id_type=MESH)
        copy.start()
        copy.wait()
        pl.semaphore_signal(free_sem.at[k], inc=1, device_id=(r, s), device_id_type=MESH)
        o_ref[pl.ds(keep, size)] = src[pl.ds(keep, size)] + recvs[k][...]
        off = keep
        offs.append(keep)
    last = HALVES[-1]
    for i, (v, r, s) in enumerate(fulls):
        k = len(steps) + i
        copy = pltpu.make_async_remote_copy(
            src_ref=o_ref.at[pl.ds(off, last)], dst_ref=recvs[k],
            send_sem=send_sem.at[k], recv_sem=recv_sem.at[k],
            device_id=(r, s), device_id_type=MESH)
        copy.start()
        copy.wait()
        o_ref[pl.ds(off, last)] = o_ref[pl.ds(off, last)] + recvs[k][...]
    base = len(steps) + len(fulls)
    for k in reversed(range(len(steps))):
        v, r, s = steps[k]
        size = HALVES[k]
        j = base + (len(steps) - 1 - k)
        copy = pltpu.make_async_remote_copy(
            src_ref=o_ref.at[pl.ds(offs[k], size)], dst_ref=o_ref.at[pl.ds(offs[k], size)],
            send_sem=send_sem.at[j], recv_sem=recv_sem.at[j],
            device_id=(r, s), device_id_type=MESH)
        pl.semaphore_wait(free_sem.at[k], 1)
        copy.start()
        copy.wait()
    _halo_finish(codes, present, hcopies)


def allreduce(x, hsrc):
    rows = x.shape[0]
    HALVES = [rows >> (k + 1) for k in range(HALVINGS)]
    n_copies = 9 + 7
    return pl.pallas_call(
        allreduce_kernel,
        out_shape=(jax.ShapeDtypeStruct((rows, x.shape[1]), jnp.float32),
                   jax.ShapeDtypeStruct(hsrc.shape, hsrc.dtype)),
        in_specs=[pl.BlockSpec(memory_space=pltpu.VMEM)] * 2,
        out_specs=(pl.BlockSpec(memory_space=pltpu.VMEM), pl.BlockSpec(memory_space=pltpu.VMEM)),
        scratch_shapes=[pltpu.VMEM((h, x.shape[1]), jnp.float32) for h in HALVES]
        + [pltpu.VMEM((HALVES[-1], x.shape[1]), jnp.float32)] * 2
        + [pltpu.SemaphoreType.DMA((n_copies,)), pltpu.SemaphoreType.DMA((n_copies,))]
        + [pltpu.SemaphoreType.REGULAR((HALVINGS,))]
        + [pltpu.SemaphoreType.DMA((8,)), pltpu.SemaphoreType.DMA((8,))],
        compiler_params=pltpu.CompilerParams(collective_id=0, has_side_effects=True),
    )(x, hsrc)


def summed_everywhere(arrays, hsrc):
    width = arrays[0].shape[1]
    parts = [a.reshape(-1, width) for a in arrays]
    unit = 8 << HALVINGS
    used = sum(p.shape[0] for p in parts)
    rows = -(-used // unit) * unit
    padded = jnp.concatenate(parts + [jnp.zeros((rows - used, width), jnp.float32)], axis=0)
    total, hout = allreduce(padded, hsrc)
    out, at = [], 0
    for a, p in zip(arrays, parts):
        out.append(total[at:at + p.shape[0]].reshape(a.shape))
        at += p.shape[0]
    return out, hout

def _exists(index, size):
    low = (index + size - 1) // size
    high = (2 * size - 3 - index) // (size - 1)
    return (low, 1, high)


def _halo_plan(src_ref, out_ref, send_sem, recv_sem):
    region = lax.axis_index("region")
    slab = lax.axis_index("slab")
    along_region = _exists(region, lax.axis_size("region"))
    along_slab = _exists(slab, lax.axis_size("slab"))
    codes = [c for c in range(9) if c != 4]
    slot = {c: i for i, c in enumerate(codes)}
    present, targets, copies = {}, {}, {}
    for c in codes:
        present[c] = along_region[c // 3] * along_slab[c % 3]
        targets[c] = (region + c // 3 - 1, slab + c % 3 - 1)
        copies[c] = pltpu.make_async_remote_copy(
            src_ref=src_ref.at[slot[c]], dst_ref=out_ref.at[slot[8 - c]],
            send_sem=send_sem.at[slot[c]], recv_sem=recv_sem.at[slot[8 - c]],
            device_id=targets[c], device_id_type=MESH)
    count = (along_region[0] + 1 + along_region[2]) * (along_slab[0] + 1 + along_slab[2]) - 1
    return codes, present, targets, copies, count


def _halo_signal(barrier, codes, present, targets):
    for c in codes:
        @pl.when(present[c] == 1)
        def _():
            pl.semaphore_signal(barrier, inc=1, device_id=targets[c], device_id_type=MESH)


def _halo_start(codes, present, copies):
    for c in codes:
        @pl.when(present[c] == 1)
        def _():
            copies[c].start()


def _halo_finish(codes, present, copies):
    for c in codes:
        @pl.when(present[c] == 1)
        def _():
            copies[8 - c].wait_recv()
            copies[c].wait_send()


def halo_kernel(src_ref, out_ref, send_sem, recv_sem):
    codes, present, targets, copies, count = _halo_plan(src_ref, out_ref, send_sem, recv_sem)
    out_ref[...] = jnp.zeros(out_ref.shape, out_ref.dtype)
    barrier = pltpu.get_barrier_semaphore()
    _halo_signal(barrier, codes, present, targets)
    pl.semaphore_wait(barrier, count)
    _halo_start(codes, present, copies)
    _halo_finish(codes, present, copies)


def halo_exchange(src, cid):
    return pl.pallas_call(
        halo_kernel,
        out_shape=jax.ShapeDtypeStruct(src.shape, src.dtype),
        in_specs=[pl.BlockSpec(memory_space=pltpu.VMEM)],
        out_specs=pl.BlockSpec(memory_space=pltpu.VMEM),
        scratch_shapes=[pltpu.SemaphoreType.DMA((8,)), pltpu.SemaphoreType.DMA((8,))],
        compiler_params=pltpu.CompilerParams(collective_id=cid, has_side_effects=True),
    )(src)


def extended_2(block, sides, width):
    for axis, dim in sides:
        count = lax.axis_size(axis)
        forward = [(i, i + 1) for i in range(count - 1)]
        backward = [(target, source) for source, target in forward]
        low = lax.ppermute(
            lax.slice_in_dim(block, block.shape[dim] - width, None, axis=dim), axis, forward
        )
        high = lax.ppermute(lax.slice_in_dim(block, 0, width, axis=dim), axis, backward)
        block = jnp.concatenate([low, block, high], axis=dim)
    return block


def _one_hot(pos_ref, o, rows):
    column = pos_ref[:, o:o + 1]
    lanes = lax.broadcasted_iota(jnp.int32, (column.shape[0], rows), 1)
    return (column == lanes).astype(jnp.bfloat16)


def conv_fwd_kernel(pos_ref, table_ref, w_ref, out_ref):
    channels = table_ref.shape[1]
    table = table_ref[...]
    total = jnp.zeros(out_ref.shape, jnp.float32)
    for o in range(pos_ref.shape[1]):
        picked = jnp.dot(_one_hot(pos_ref, o, table.shape[0]), table, preferred_element_type=jnp.float32)
        weight = w_ref[o * channels:(o + 1) * channels, :]
        total = total + jnp.dot(picked.astype(jnp.bfloat16), weight, preferred_element_type=jnp.float32)
    out_ref[...] = total


def conv_fwd_halo_kernel(pos_ref, own_ref, src_ref, w_ref, out_ref, hout_ref, send_sem, recv_sem):
    channels = own_ref.shape[1]
    voxels = own_ref.shape[0]
    halo_rows = hout_ref.shape[0] * hout_ref.shape[1]
    codes, present, targets, copies, count = _halo_plan(src_ref, hout_ref, send_sem, recv_sem)
    hout_ref[...] = jnp.zeros(hout_ref.shape, hout_ref.dtype)
    barrier = pltpu.get_barrier_semaphore()
    _halo_signal(barrier, codes, present, targets)
    pl.semaphore_wait(barrier, count)
    _halo_start(codes, present, copies)
    own = own_ref[...]
    own_lanes = lax.broadcasted_iota(jnp.int32, (pos_ref.shape[0], voxels), 1) + halo_rows
    total = jnp.zeros(out_ref.shape, jnp.float32)
    for o in range(pos_ref.shape[1]):
        hot = (pos_ref[:, o:o + 1] == own_lanes).astype(jnp.bfloat16)
        picked = jnp.dot(hot, own, preferred_element_type=jnp.float32)
        weight = w_ref[o * channels:(o + 1) * channels, :]
        total = total + jnp.dot(picked.astype(jnp.bfloat16), weight, preferred_element_type=jnp.float32)
    _halo_finish(codes, present, copies)
    halo = hout_ref[...].reshape(halo_rows, channels)
    for o in range(pos_ref.shape[1]):
        picked = jnp.dot(_one_hot(pos_ref, o, halo_rows), halo, preferred_element_type=jnp.float32)
        weight = w_ref[o * channels:(o + 1) * channels, :]
        total = total + jnp.dot(picked.astype(jnp.bfloat16), weight, preferred_element_type=jnp.float32)
    out_ref[...] = total


def conv_bwd_kernel(post_ref, tablet_ref, grad_ref, w_ref, tgrad_ref, wgrad_ref):
    channels = tablet_ref.shape[0]
    table_t = tablet_ref[...]
    grad = grad_ref[...]
    rows = table_t.shape[1]
    sublanes = lax.broadcasted_iota(jnp.int32, (rows, post_ref.shape[1]), 0)
    total = jnp.zeros((rows, 2 * channels), jnp.float32)
    for o in range(post_ref.shape[0]):
        hot_t = (sublanes == post_ref[o:o + 1, :]).astype(jnp.bfloat16)
        picked_t = jnp.dot(table_t, hot_t, preferred_element_type=jnp.float32).astype(jnp.bfloat16)
        wgrad_ref[o * channels:(o + 1) * channels, :] = jnp.dot(
            picked_t, grad, preferred_element_type=jnp.float32)
        weight = w_ref[o * channels:(o + 1) * channels, :]
        spread = lax.dot_general(grad, weight, (((1,), (1,)), ((), ())), preferred_element_type=jnp.float32)
        high = spread.astype(jnp.bfloat16)
        low = (spread - high.astype(jnp.float32)).astype(jnp.bfloat16)
        total = total + jnp.dot(hot_t, jnp.concatenate([high, low], axis=1),
                                preferred_element_type=jnp.float32)
    tgrad_ref[...] = total[:, :channels] + total[:, channels:]


def _vmem_call(kernel, outs, *args):
    return pl.pallas_call(
        kernel,
        out_shape=outs,
        in_specs=[pl.BlockSpec(memory_space=pltpu.VMEM)] * len(args),
        out_specs=jax.tree.map(lambda _: pl.BlockSpec(memory_space=pltpu.VMEM), outs),
    )(*args)


def on_device(features, neighbours, down_map, w_conv, w_down, coarse_grad):
    voxels, channels = features.shape
    offsets = neighbours.shape[1]
    rim = 64
    absent = neighbours >= 9 * voxels
    slot_idx = neighbours // voxels
    local_idx = neighbours - slot_idx * voxels
    halo_slot = jnp.where(slot_idx < 4, slot_idx, slot_idx - 1)
    compact = jnp.where(slot_idx == 4, 8 * rim + local_idx, halo_slot * rim + local_idx)
    positions = jnp.where(absent, -1, compact).astype(jnp.int32)
    sendable = jnp.broadcast_to(features[None, :rim], (8, rim, channels))
    conv_out, halo = pl.pallas_call(
        conv_fwd_halo_kernel,
        out_shape=(jax.ShapeDtypeStruct((voxels, channels), jnp.float32),
                   jax.ShapeDtypeStruct(sendable.shape, sendable.dtype)),
        in_specs=[pl.BlockSpec(memory_space=pltpu.VMEM)] * 4,
        out_specs=(pl.BlockSpec(memory_space=pltpu.VMEM), pl.BlockSpec(memory_space=pltpu.VMEM)),
        scratch_shapes=[pltpu.SemaphoreType.DMA((8,)), pltpu.SemaphoreType.DMA((8,))],
        compiler_params=pltpu.CompilerParams(collective_id=1, has_side_effects=True),
    )(positions, features, sendable, w_conv)
    table = jnp.concatenate([halo.reshape(8 * rim, channels), features], axis=0)
    table_rows = table.shape[0]
    hidden = (features.astype(jnp.float32) + jax.nn.silu(conv_out)).astype(jnp.bfloat16)
    zero_row = jnp.zeros((1, channels), features.dtype)
    coarse_count, taps = down_map.shape
    down_local = jnp.minimum(down_map, voxels)
    hidden_pad = jnp.concatenate([hidden, zero_row], axis=0)
    coarse_rows = hidden_pad[down_local].reshape(coarse_count, taps * channels)
    coarse = jnp.dot(coarse_rows, w_down, preferred_element_type=jnp.float32).astype(jnp.bfloat16)
    coarse_back = jnp.dot(coarse_grad, w_down.T, preferred_element_type=jnp.float32)
    hidden_grad = jnp.zeros((voxels + 1, channels), jnp.float32)
    hidden_grad = hidden_grad.at[down_local.reshape(-1)].add(coarse_back.reshape(-1, channels))[
        :voxels
    ]
    down_wgrad = lax.dot_general(
        coarse_rows, coarse_grad, (((0,), (0,)), ((), ())), preferred_element_type=jnp.float32
    )
    sigmoid_y = jax.nn.sigmoid(conv_out)
    conv_grad = (hidden_grad * sigmoid_y * (1.0 + conv_out * (1.0 - sigmoid_y))).astype(
        jnp.bfloat16
    )
    table_grad, conv_wgrad = _vmem_call(
        conv_bwd_kernel,
        (jax.ShapeDtypeStruct((table_rows, channels), jnp.float32),
         jax.ShapeDtypeStruct(w_conv.shape, jnp.float32)),
        positions.T, table.T, conv_grad, w_conv)
    halo_grad = table_grad[: 8 * rim].reshape(8, rim, channels)
    (conv_wgrad, down_wgrad), returned = summed_everywhere([conv_wgrad, down_wgrad], halo_grad)
    own_part = table_grad[8 * rim:]
    incoming = jnp.sum(returned, axis=0)
    grad_input = hidden_grad + own_part
    grad_input = grad_input.at[:rim].add(incoming)
    return (coarse, grad_input, conv_wgrad, down_wgrad)


def solution(mesh):
    in_specs = (
        P(("region", "slab"), None),
        P(("region", "slab"), None),
        P(("region", "slab"), None),
        P(),
        P(),
        P(("region", "slab"), None),
    )
    out_specs = (P(("region", "slab"), None), P(("region", "slab"), None), P(), P())
    return jax.shard_map(
        on_device, mesh=mesh, in_specs=in_specs, out_specs=out_specs, check_vma=False
    )
```

```python
import jax
import jax.numpy as jnp
from jax import lax
from jax.experimental import pallas as pl
from jax.experimental.pallas import tpu as pltpu
from jax.sharding import PartitionSpec as P
from jax.experimental import pallas as pl
from jax.experimental.pallas import tpu as pltpu

MESH = pl.DeviceIdType.MESH
HALVINGS = 7
ORDER_A = [0, 4, 7, 1, 5, 8]
ORDER_B = [4, 7, 0, 5, 8, 1]
FULL_A = [2, 6]
FULL_B = [6, 2]


def _bit_partner(region, slab, b):
    if b < 3:
        v = (slab // (1 << b)) % 2
        return v, region, slab + (1 - 2 * v) * (1 << b)
    j = b - 3
    v = (region // (1 << j)) % 2
    return v, region + (1 - 2 * v) * (1 << j), slab


def _step(region, slab, core, ba, bb):
    va, ra, sa = _bit_partner(region, slab, ba)
    vb, rb, sb = _bit_partner(region, slab, bb)
    return va + core * (vb - va), ra + core * (rb - ra), sa + core * (sb - sa)


def allreduce_kernel(x_ref, post_ref, grad_ref, w_ref, o_ref, hsrc_ref, own_ref, hout_ref, *scratch):
    HALVES = [x_ref.shape[0] >> (k + 1) for k in range(HALVINGS)]
    recvs = scratch[:9]
    send_sem, recv_sem, free_sem = scratch[9], scratch[10], scratch[11]
    codes, present, targets, hcopies, hcount = _halo_plan(hsrc_ref, hout_ref, scratch[12], scratch[13])
    hout_ref[...] = jnp.zeros(hout_ref.shape, hout_ref.dtype)
    region = lax.axis_index("region")
    slab = lax.axis_index("slab")
    core = region % 2
    steps = [(core, region + 1 - 2 * core, slab)]
    for ba, bb in zip(ORDER_A, ORDER_B):
        steps.append(_step(region, slab, core, ba, bb))
    fulls = [_step(region, slab, core, ba, bb) for ba, bb in zip(FULL_A, FULL_B)]

    barrier = pltpu.get_barrier_semaphore()
    for _, r, s in steps + fulls:
        pl.semaphore_signal(barrier, inc=1, device_id=(r, s), device_id_type=MESH)
    _halo_signal(barrier, codes, present, targets)
    conv_scatter_body(post_ref, grad_ref, w_ref, hsrc_ref, own_ref)
    pl.semaphore_wait(barrier, len(steps) + len(fulls) + hcount)
    _halo_start(codes, present, hcopies)

    off = 0
    offs = []
    for k, (v, r, s) in enumerate(steps):
        size = HALVES[k]
        keep = pl.multiple_of(off + v * size, 8)
        send = pl.multiple_of(off + (1 - v) * size, 8)
        src = x_ref if k == 0 else o_ref
        copy = pltpu.make_async_remote_copy(
            src_ref=src.at[pl.ds(send, size)], dst_ref=recvs[k],
            send_sem=send_sem.at[k], recv_sem=recv_sem.at[k],
            device_id=(r, s), device_id_type=MESH)
        copy.start()
        copy.wait()
        pl.semaphore_signal(free_sem.at[k], inc=1, device_id=(r, s), device_id_type=MESH)
        o_ref[pl.ds(keep, size)] = src[pl.ds(keep, size)] + recvs[k][...]
        off = keep
        offs.append(keep)
    last = HALVES[-1]
    for i, (v, r, s) in enumerate(fulls):
        k = len(steps) + i
        copy = pltpu.make_async_remote_copy(
            src_ref=o_ref.at[pl.ds(off, last)], dst_ref=recvs[k],
            send_sem=send_sem.at[k], recv_sem=recv_sem.at[k],
            device_id=(r, s), device_id_type=MESH)
        copy.start()
        copy.wait()
        o_ref[pl.ds(off, last)] = o_ref[pl.ds(off, last)] + recvs[k][...]
    base = len(steps) + len(fulls)
    for k in reversed(range(len(steps))):
        v, r, s = steps[k]
        size = HALVES[k]
        j = base + (len(steps) - 1 - k)
        copy = pltpu.make_async_remote_copy(
            src_ref=o_ref.at[pl.ds(offs[k], size)], dst_ref=o_ref.at[pl.ds(offs[k], size)],
            send_sem=send_sem.at[j], recv_sem=recv_sem.at[j],
            device_id=(r, s), device_id_type=MESH)
        pl.semaphore_wait(free_sem.at[k], 1)
        copy.start()
        copy.wait()
    _halo_finish(codes, present, hcopies)


def allreduce(x, post, grad, w, hshape, own_rows):
    rows = x.shape[0]
    HALVES = [rows >> (k + 1) for k in range(HALVINGS)]
    n_copies = 9 + 7
    return pl.pallas_call(
        allreduce_kernel,
        out_shape=(jax.ShapeDtypeStruct((rows, 128), jnp.float32),
                   jax.ShapeDtypeStruct(hshape, jnp.float32),
                   jax.ShapeDtypeStruct((own_rows, hshape[2]), jnp.float32),
                   jax.ShapeDtypeStruct(hshape, jnp.float32)),
        in_specs=[pl.BlockSpec(memory_space=pltpu.VMEM)] * 4,
        out_specs=tuple(pl.BlockSpec(memory_space=pltpu.VMEM) for _ in range(4)),
        scratch_shapes=[pltpu.VMEM((h, 128), jnp.float32) for h in HALVES]
        + [pltpu.VMEM((HALVES[-1], 128), jnp.float32)] * 2
        + [pltpu.SemaphoreType.DMA((n_copies,)), pltpu.SemaphoreType.DMA((n_copies,))]
        + [pltpu.SemaphoreType.REGULAR((HALVINGS,))]
        + [pltpu.SemaphoreType.DMA((8,)), pltpu.SemaphoreType.DMA((8,))],
        compiler_params=pltpu.CompilerParams(collective_id=0, has_side_effects=True),
    )(x, post, grad, w)


def summed_everywhere(arrays, post, grad, w, hshape, own_rows):
    flat = jnp.concatenate([a.reshape(-1) for a in arrays])
    unit = 128 * 8 << HALVINGS
    rows = -(-flat.size // unit) * unit // 128
    padded = jnp.pad(flat, (0, rows * 128 - flat.size)).reshape(rows, 128)
    total, _, own, hout = allreduce(padded, post, grad, w, hshape, own_rows)
    total = total.reshape(-1)
    out, at = [], 0
    for a in arrays:
        out.append(total[at:at + a.size].reshape(a.shape))
        at += a.size
    return out, own, hout


def _exists(index, size):
    low = (index + size - 1) // size
    high = (2 * size - 3 - index) // (size - 1)
    return (low, 1, high)


def _halo_plan(src_ref, out_ref, send_sem, recv_sem):
    region = lax.axis_index("region")
    slab = lax.axis_index("slab")
    along_region = _exists(region, lax.axis_size("region"))
    along_slab = _exists(slab, lax.axis_size("slab"))
    codes = [c for c in range(9) if c != 4]
    slot = {c: i for i, c in enumerate(codes)}
    present, targets, copies = {}, {}, {}
    for c in codes:
        present[c] = along_region[c // 3] * along_slab[c % 3]
        targets[c] = (region + c // 3 - 1, slab + c % 3 - 1)
        copies[c] = pltpu.make_async_remote_copy(
            src_ref=src_ref.at[slot[c]], dst_ref=out_ref.at[slot[8 - c]],
            send_sem=send_sem.at[slot[c]], recv_sem=recv_sem.at[slot[8 - c]],
            device_id=targets[c], device_id_type=MESH)
    count = (along_region[0] + 1 + along_region[2]) * (along_slab[0] + 1 + along_slab[2]) - 1
    return codes, present, targets, copies, count


def _halo_signal(barrier, codes, present, targets):
    for c in codes:
        @pl.when(present[c] == 1)
        def _():
            pl.semaphore_signal(barrier, inc=1, device_id=targets[c], device_id_type=MESH)


def _halo_start(codes, present, copies):
    for c in codes:
        @pl.when(present[c] == 1)
        def _():
            copies[c].start()


def _halo_finish(codes, present, copies):
    for c in codes:
        @pl.when(present[c] == 1)
        def _():
            copies[8 - c].wait_recv()
            copies[c].wait_send()


def halo_kernel(src_ref, out_ref, send_sem, recv_sem):
    codes, present, targets, copies, count = _halo_plan(src_ref, out_ref, send_sem, recv_sem)
    out_ref[...] = jnp.zeros(out_ref.shape, out_ref.dtype)
    barrier = pltpu.get_barrier_semaphore()
    _halo_signal(barrier, codes, present, targets)
    pl.semaphore_wait(barrier, count)
    _halo_start(codes, present, copies)
    _halo_finish(codes, present, copies)


def halo_exchange(src, cid):
    return pl.pallas_call(
        halo_kernel,
        out_shape=jax.ShapeDtypeStruct(src.shape, src.dtype),
        in_specs=[pl.BlockSpec(memory_space=pltpu.VMEM)],
        out_specs=pl.BlockSpec(memory_space=pltpu.VMEM),
        scratch_shapes=[pltpu.SemaphoreType.DMA((8,)), pltpu.SemaphoreType.DMA((8,))],
        compiler_params=pltpu.CompilerParams(collective_id=cid, has_side_effects=True),
    )(src)


def extended_2(block, sides, width):
    for axis, dim in sides:
        count = lax.axis_size(axis)
        forward = [(i, i + 1) for i in range(count - 1)]
        backward = [(target, source) for source, target in forward]
        low = lax.ppermute(
            lax.slice_in_dim(block, block.shape[dim] - width, None, axis=dim), axis, forward
        )
        high = lax.ppermute(lax.slice_in_dim(block, 0, width, axis=dim), axis, backward)
        block = jnp.concatenate([low, block, high], axis=dim)
    return block


def _one_hot(pos_ref, o, rows):
    column = pos_ref[:, o:o + 1]
    lanes = lax.broadcasted_iota(jnp.int32, (column.shape[0], rows), 1)
    return (column == lanes).astype(jnp.bfloat16)


def conv_fwd_kernel(pos_ref, table_ref, w_ref, out_ref):
    channels = table_ref.shape[1]
    table = table_ref[...]
    total = jnp.zeros(out_ref.shape, jnp.float32)
    for o in range(pos_ref.shape[1]):
        picked = jnp.dot(_one_hot(pos_ref, o, table.shape[0]), table, preferred_element_type=jnp.float32)
        weight = w_ref[o * channels:(o + 1) * channels, :]
        total = total + jnp.dot(picked.astype(jnp.bfloat16), weight, preferred_element_type=jnp.float32)
    out_ref[...] = total


def conv_fwd_halo_kernel(pos_ref, own_ref, src_ref, w_ref, out_ref, hout_ref, send_sem, recv_sem):
    channels = own_ref.shape[1]
    voxels = own_ref.shape[0]
    halo_rows = hout_ref.shape[0] * hout_ref.shape[1]
    codes, present, targets, copies, count = _halo_plan(src_ref, hout_ref, send_sem, recv_sem)
    hout_ref[...] = jnp.zeros(hout_ref.shape, hout_ref.dtype)
    barrier = pltpu.get_barrier_semaphore()
    _halo_signal(barrier, codes, present, targets)
    pl.semaphore_wait(barrier, count)
    _halo_start(codes, present, copies)
    own = own_ref[...]
    own_lanes = lax.broadcasted_iota(jnp.int32, (pos_ref.shape[0], voxels), 1) + halo_rows
    total = jnp.zeros(out_ref.shape, jnp.float32)
    for o in range(pos_ref.shape[1]):
        hot = (pos_ref[:, o:o + 1] == own_lanes).astype(jnp.bfloat16)
        picked = jnp.dot(hot, own, preferred_element_type=jnp.float32)
        weight = w_ref[o * channels:(o + 1) * channels, :]
        total = total + jnp.dot(picked.astype(jnp.bfloat16), weight, preferred_element_type=jnp.float32)
    _halo_finish(codes, present, copies)
    halo = hout_ref[...].reshape(halo_rows, channels)
    for o in range(pos_ref.shape[1]):
        picked = jnp.dot(_one_hot(pos_ref, o, halo_rows), halo, preferred_element_type=jnp.float32)
        weight = w_ref[o * channels:(o + 1) * channels, :]
        total = total + jnp.dot(picked.astype(jnp.bfloat16), weight, preferred_element_type=jnp.float32)
    out_ref[...] = total


def conv_wgrad_kernel(post_ref, tablet_ref, grad_ref, wgrad_ref):
    channels = tablet_ref.shape[0]
    table_t = tablet_ref[...]
    grad = grad_ref[...]
    rows = table_t.shape[1]
    sublanes = lax.broadcasted_iota(jnp.int32, (rows, post_ref.shape[1]), 0)
    for o in range(post_ref.shape[0]):
        hot_t = (sublanes == post_ref[o:o + 1, :]).astype(jnp.bfloat16)
        picked_t = jnp.dot(table_t, hot_t, preferred_element_type=jnp.float32).astype(jnp.bfloat16)
        wgrad_ref[o * channels:(o + 1) * channels, :] = jnp.dot(
            picked_t, grad, preferred_element_type=jnp.float32)


def conv_scatter_body(post_ref, grad_ref, w_ref, halo_ref, own_ref):
    channels = grad_ref.shape[1]
    grad = grad_ref[...]
    halo_rows = halo_ref.shape[0] * halo_ref.shape[1]
    rows = halo_rows + own_ref.shape[0]
    sublanes = lax.broadcasted_iota(jnp.int32, (rows, post_ref.shape[1]), 0)
    total = jnp.zeros((rows, 2 * channels), jnp.float32)
    for o in range(post_ref.shape[0]):
        hot_t = (sublanes == post_ref[o:o + 1, :]).astype(jnp.bfloat16)
        weight = w_ref[o * channels:(o + 1) * channels, :]
        spread = lax.dot_general(grad, weight, (((1,), (1,)), ((), ())), preferred_element_type=jnp.float32)
        high = spread.astype(jnp.bfloat16)
        low = (spread - high.astype(jnp.float32)).astype(jnp.bfloat16)
        total = total + jnp.dot(hot_t, jnp.concatenate([high, low], axis=1),
                                preferred_element_type=jnp.float32)
    summed = total[:, :channels] + total[:, channels:]
    halo_ref[...] = summed[:halo_rows].reshape(halo_ref.shape)
    own_ref[...] = summed[halo_rows:]


def _vmem_call(kernel, outs, *args):
    return pl.pallas_call(
        kernel,
        out_shape=outs,
        in_specs=[pl.BlockSpec(memory_space=pltpu.VMEM)] * len(args),
        out_specs=jax.tree.map(lambda _: pl.BlockSpec(memory_space=pltpu.VMEM), outs),
    )(*args)


def on_device(features, neighbours, down_map, w_conv, w_down, coarse_grad):
    voxels, channels = features.shape
    offsets = neighbours.shape[1]
    rim = 64
    absent = neighbours >= 9 * voxels
    slot_idx = neighbours // voxels
    local_idx = neighbours - slot_idx * voxels
    halo_slot = jnp.where(slot_idx < 4, slot_idx, slot_idx - 1)
    compact = jnp.where(slot_idx == 4, 8 * rim + local_idx, halo_slot * rim + local_idx)
    positions = jnp.where(absent, -1, compact).astype(jnp.int32)
    sendable = jnp.broadcast_to(features[None, :rim], (8, rim, channels))
    conv_out, halo = pl.pallas_call(
        conv_fwd_halo_kernel,
        out_shape=(jax.ShapeDtypeStruct((voxels, channels), jnp.float32),
                   jax.ShapeDtypeStruct(sendable.shape, sendable.dtype)),
        in_specs=[pl.BlockSpec(memory_space=pltpu.VMEM)] * 4,
        out_specs=(pl.BlockSpec(memory_space=pltpu.VMEM), pl.BlockSpec(memory_space=pltpu.VMEM)),
        scratch_shapes=[pltpu.SemaphoreType.DMA((8,)), pltpu.SemaphoreType.DMA((8,))],
        compiler_params=pltpu.CompilerParams(collective_id=1, has_side_effects=True),
    )(positions, features, sendable, w_conv)
    table = jnp.concatenate([halo.reshape(8 * rim, channels), features], axis=0)
    table_rows = table.shape[0]
    hidden = (features.astype(jnp.float32) + jax.nn.silu(conv_out)).astype(jnp.bfloat16)
    zero_row = jnp.zeros((1, channels), features.dtype)
    coarse_count, taps = down_map.shape
    down_local = jnp.minimum(down_map, voxels)
    hidden_pad = jnp.concatenate([hidden, zero_row], axis=0)
    coarse_rows = hidden_pad[down_local].reshape(coarse_count, taps * channels)
    coarse = jnp.dot(coarse_rows, w_down, preferred_element_type=jnp.float32).astype(jnp.bfloat16)
    coarse_back = jnp.dot(coarse_grad, w_down.T, preferred_element_type=jnp.float32)
    hidden_grad = jnp.zeros((voxels + 1, channels), jnp.float32)
    hidden_grad = hidden_grad.at[down_local.reshape(-1)].add(coarse_back.reshape(-1, channels))[
        :voxels
    ]
    down_wgrad = lax.dot_general(
        coarse_rows, coarse_grad, (((0,), (0,)), ((), ())), preferred_element_type=jnp.float32
    )
    sigmoid_y = jax.nn.sigmoid(conv_out)
    conv_grad = (hidden_grad * sigmoid_y * (1.0 + conv_out * (1.0 - sigmoid_y))).astype(
        jnp.bfloat16
    )
    conv_wgrad = _vmem_call(
        conv_wgrad_kernel, jax.ShapeDtypeStruct(w_conv.shape, jnp.float32),
        positions.T, table.T, conv_grad)
    (conv_wgrad, down_wgrad), own_part, returned = summed_everywhere(
        [conv_wgrad, down_wgrad], positions.T, conv_grad, w_conv, (8, rim, channels), voxels)
    incoming = jnp.sum(returned, axis=0)
    grad_input = hidden_grad + own_part
    grad_input = grad_input.at[:rim].add(incoming)
    return (coarse, grad_input, conv_wgrad, down_wgrad)


def solution(mesh):
    in_specs = (
        P(("region", "slab"), None),
        P(("region", "slab"), None),
        P(("region", "slab"), None),
        P(),
        P(),
        P(("region", "slab"), None),
    )
    out_specs = (P(("region", "slab"), None), P(("region", "slab"), None), P(), P())
    return jax.shard_map(
        on_device, mesh=mesh, in_specs=in_specs, out_specs=out_specs, check_vma=False
    )
```

```python
import jax
import jax.numpy as jnp
from jax import lax
from jax.experimental import pallas as pl
from jax.experimental.pallas import tpu as pltpu
from jax.sharding import PartitionSpec as P
from jax.experimental import pallas as pl
from jax.experimental.pallas import tpu as pltpu

MESH = pl.DeviceIdType.MESH
HALVINGS = 7
ORDER_A = [0, 4, 7, 1, 5, 8]
ORDER_B = [4, 7, 0, 5, 8, 1]
FULL_A = [2, 6]
FULL_B = [6, 2]


def _bit_partner(region, slab, b):
    if b < 3:
        v = (slab // (1 << b)) % 2
        return v, region, slab + (1 - 2 * v) * (1 << b)
    j = b - 3
    v = (region // (1 << j)) % 2
    return v, region + (1 - 2 * v) * (1 << j), slab


def _step(region, slab, core, ba, bb):
    va, ra, sa = _bit_partner(region, slab, ba)
    vb, rb, sb = _bit_partner(region, slab, bb)
    return va + core * (vb - va), ra + core * (rb - ra), sa + core * (sb - sa)


def allreduce_kernel(x_ref, post_ref, grad_ref, w_ref, hgrad_ref, o_ref, hsrc_ref, own_ref, hout_ref, *scratch):
    HALVES = [x_ref.shape[0] >> (k + 1) for k in range(HALVINGS)]
    recvs = scratch[:9]
    send_sem, recv_sem, free_sem = scratch[9], scratch[10], scratch[11]
    codes, present, targets, hcopies, hcount = _halo_plan(hsrc_ref, hout_ref, scratch[12], scratch[13])
    hout_ref[...] = jnp.zeros(hout_ref.shape, hout_ref.dtype)
    region = lax.axis_index("region")
    slab = lax.axis_index("slab")
    core = region % 2
    steps = [(core, region + 1 - 2 * core, slab)]
    for ba, bb in zip(ORDER_A, ORDER_B):
        steps.append(_step(region, slab, core, ba, bb))
    fulls = [_step(region, slab, core, ba, bb) for ba, bb in zip(FULL_A, FULL_B)]

    barrier = pltpu.get_barrier_semaphore()
    for _, r, s in steps + fulls:
        pl.semaphore_signal(barrier, inc=1, device_id=(r, s), device_id_type=MESH)
    _halo_signal(barrier, codes, present, targets)
    conv_scatter_body(post_ref, grad_ref, w_ref, hsrc_ref, own_ref)
    pl.semaphore_wait(barrier, len(steps) + len(fulls) + hcount)
    _halo_start(codes, present, hcopies)

    off = 0
    offs = []
    for k, (v, r, s) in enumerate(steps):
        size = HALVES[k]
        keep = pl.multiple_of(off + v * size, 8)
        send = pl.multiple_of(off + (1 - v) * size, 8)
        src = x_ref if k == 0 else o_ref
        copy = pltpu.make_async_remote_copy(
            src_ref=src.at[pl.ds(send, size)], dst_ref=recvs[k],
            send_sem=send_sem.at[k], recv_sem=recv_sem.at[k],
            device_id=(r, s), device_id_type=MESH)
        copy.start()
        copy.wait()
        pl.semaphore_signal(free_sem.at[k], inc=1, device_id=(r, s), device_id_type=MESH)
        o_ref[pl.ds(keep, size)] = src[pl.ds(keep, size)] + recvs[k][...]
        off = keep
        offs.append(keep)
    last = HALVES[-1]
    for i, (v, r, s) in enumerate(fulls):
        k = len(steps) + i
        copy = pltpu.make_async_remote_copy(
            src_ref=o_ref.at[pl.ds(off, last)], dst_ref=recvs[k],
            send_sem=send_sem.at[k], recv_sem=recv_sem.at[k],
            device_id=(r, s), device_id_type=MESH)
        copy.start()
        copy.wait()
        o_ref[pl.ds(off, last)] = o_ref[pl.ds(off, last)] + recvs[k][...]
    base = len(steps) + len(fulls)
    for k in reversed(range(len(steps))):
        v, r, s = steps[k]
        size = HALVES[k]
        j = base + (len(steps) - 1 - k)
        copy = pltpu.make_async_remote_copy(
            src_ref=o_ref.at[pl.ds(offs[k], size)], dst_ref=o_ref.at[pl.ds(offs[k], size)],
            send_sem=send_sem.at[j], recv_sem=recv_sem.at[j],
            device_id=(r, s), device_id_type=MESH)
        pl.semaphore_wait(free_sem.at[k], 1)
        copy.start()
        copy.wait()
    _halo_finish(codes, present, hcopies)
    rim = hout_ref.shape[1]
    own_ref[...] = hgrad_ref[...] + own_ref[...]
    own_ref[:rim] = own_ref[:rim] + jnp.sum(hout_ref[...], axis=0)


def allreduce(x, post, grad, w, hgrad, hshape, own_rows):
    rows = x.shape[0]
    HALVES = [rows >> (k + 1) for k in range(HALVINGS)]
    n_copies = 9 + 7
    return pl.pallas_call(
        allreduce_kernel,
        out_shape=(jax.ShapeDtypeStruct((rows, 128), jnp.float32),
                   jax.ShapeDtypeStruct(hshape, jnp.float32),
                   jax.ShapeDtypeStruct((own_rows, hshape[2]), jnp.float32),
                   jax.ShapeDtypeStruct(hshape, jnp.float32)),
        in_specs=[pl.BlockSpec(memory_space=pltpu.VMEM)] * 5,
        out_specs=tuple(pl.BlockSpec(memory_space=pltpu.VMEM) for _ in range(4)),
        scratch_shapes=[pltpu.VMEM((h, 128), jnp.float32) for h in HALVES]
        + [pltpu.VMEM((HALVES[-1], 128), jnp.float32)] * 2
        + [pltpu.SemaphoreType.DMA((n_copies,)), pltpu.SemaphoreType.DMA((n_copies,))]
        + [pltpu.SemaphoreType.REGULAR((HALVINGS,))]
        + [pltpu.SemaphoreType.DMA((8,)), pltpu.SemaphoreType.DMA((8,))],
        compiler_params=pltpu.CompilerParams(collective_id=0, has_side_effects=True),
    )(x, post, grad, w, hgrad)


def summed_everywhere(arrays, post, grad, w, hgrad, hshape, own_rows):
    flat = jnp.concatenate([a.reshape(-1) for a in arrays])
    unit = 128 * 8 << HALVINGS
    rows = -(-flat.size // unit) * unit // 128
    padded = jnp.pad(flat, (0, rows * 128 - flat.size)).reshape(rows, 128)
    total, _, own, hout = allreduce(padded, post, grad, w, hgrad, hshape, own_rows)
    total = total.reshape(-1)
    out, at = [], 0
    for a in arrays:
        out.append(total[at:at + a.size].reshape(a.shape))
        at += a.size
    return out, own, hout


def _exists(index, size):
    low = (index + size - 1) // size
    high = (2 * size - 3 - index) // (size - 1)
    return (low, 1, high)


def _halo_plan(src_ref, out_ref, send_sem, recv_sem):
    region = lax.axis_index("region")
    slab = lax.axis_index("slab")
    along_region = _exists(region, lax.axis_size("region"))
    along_slab = _exists(slab, lax.axis_size("slab"))
    codes = [c for c in range(9) if c != 4]
    slot = {c: i for i, c in enumerate(codes)}
    present, targets, copies = {}, {}, {}
    for c in codes:
        present[c] = along_region[c // 3] * along_slab[c % 3]
        targets[c] = (region + c // 3 - 1, slab + c % 3 - 1)
        copies[c] = pltpu.make_async_remote_copy(
            src_ref=src_ref.at[slot[c]], dst_ref=out_ref.at[slot[8 - c]],
            send_sem=send_sem.at[slot[c]], recv_sem=recv_sem.at[slot[8 - c]],
            device_id=targets[c], device_id_type=MESH)
    count = (along_region[0] + 1 + along_region[2]) * (along_slab[0] + 1 + along_slab[2]) - 1
    return codes, present, targets, copies, count


def _halo_signal(barrier, codes, present, targets):
    for c in codes:
        @pl.when(present[c] == 1)
        def _():
            pl.semaphore_signal(barrier, inc=1, device_id=targets[c], device_id_type=MESH)


def _halo_start(codes, present, copies):
    for c in codes:
        @pl.when(present[c] == 1)
        def _():
            copies[c].start()


def _halo_finish(codes, present, copies):
    for c in codes:
        @pl.when(present[c] == 1)
        def _():
            copies[8 - c].wait_recv()
            copies[c].wait_send()


def halo_kernel(src_ref, out_ref, send_sem, recv_sem):
    codes, present, targets, copies, count = _halo_plan(src_ref, out_ref, send_sem, recv_sem)
    out_ref[...] = jnp.zeros(out_ref.shape, out_ref.dtype)
    barrier = pltpu.get_barrier_semaphore()
    _halo_signal(barrier, codes, present, targets)
    pl.semaphore_wait(barrier, count)
    _halo_start(codes, present, copies)
    _halo_finish(codes, present, copies)


def halo_exchange(src, cid):
    return pl.pallas_call(
        halo_kernel,
        out_shape=jax.ShapeDtypeStruct(src.shape, src.dtype),
        in_specs=[pl.BlockSpec(memory_space=pltpu.VMEM)],
        out_specs=pl.BlockSpec(memory_space=pltpu.VMEM),
        scratch_shapes=[pltpu.SemaphoreType.DMA((8,)), pltpu.SemaphoreType.DMA((8,))],
        compiler_params=pltpu.CompilerParams(collective_id=cid, has_side_effects=True),
    )(src)


def extended_2(block, sides, width):
    for axis, dim in sides:
        count = lax.axis_size(axis)
        forward = [(i, i + 1) for i in range(count - 1)]
        backward = [(target, source) for source, target in forward]
        low = lax.ppermute(
            lax.slice_in_dim(block, block.shape[dim] - width, None, axis=dim), axis, forward
        )
        high = lax.ppermute(lax.slice_in_dim(block, 0, width, axis=dim), axis, backward)
        block = jnp.concatenate([low, block, high], axis=dim)
    return block


def _one_hot(pos_ref, o, rows):
    column = pos_ref[:, o:o + 1]
    lanes = lax.broadcasted_iota(jnp.int32, (column.shape[0], rows), 1)
    return (column == lanes).astype(jnp.bfloat16)


def conv_fwd_kernel(pos_ref, table_ref, w_ref, out_ref):
    channels = table_ref.shape[1]
    table = table_ref[...]
    total = jnp.zeros(out_ref.shape, jnp.float32)
    for o in range(pos_ref.shape[1]):
        picked = jnp.dot(_one_hot(pos_ref, o, table.shape[0]), table, preferred_element_type=jnp.float32)
        weight = w_ref[o * channels:(o + 1) * channels, :]
        total = total + jnp.dot(picked.astype(jnp.bfloat16), weight, preferred_element_type=jnp.float32)
    out_ref[...] = total


def conv_fwd_halo_kernel(pos_ref, own_ref, src_ref, w_ref, out_ref, hout_ref, send_sem, recv_sem):
    channels = own_ref.shape[1]
    voxels = own_ref.shape[0]
    halo_rows = hout_ref.shape[0] * hout_ref.shape[1]
    codes, present, targets, copies, count = _halo_plan(src_ref, hout_ref, send_sem, recv_sem)
    hout_ref[...] = jnp.zeros(hout_ref.shape, hout_ref.dtype)
    barrier = pltpu.get_barrier_semaphore()
    _halo_signal(barrier, codes, present, targets)
    pl.semaphore_wait(barrier, count)
    _halo_start(codes, present, copies)
    own = own_ref[...]
    own_lanes = lax.broadcasted_iota(jnp.int32, (pos_ref.shape[0], voxels), 1) + halo_rows
    total = jnp.zeros(out_ref.shape, jnp.float32)
    for o in range(pos_ref.shape[1]):
        hot = (pos_ref[:, o:o + 1] == own_lanes).astype(jnp.bfloat16)
        picked = jnp.dot(hot, own, preferred_element_type=jnp.float32)
        weight = w_ref[o * channels:(o + 1) * channels, :]
        total = total + jnp.dot(picked.astype(jnp.bfloat16), weight, preferred_element_type=jnp.float32)
    _halo_finish(codes, present, copies)
    halo = hout_ref[...].reshape(halo_rows, channels)
    for o in range(pos_ref.shape[1]):
        picked = jnp.dot(_one_hot(pos_ref, o, halo_rows), halo, preferred_element_type=jnp.float32)
        weight = w_ref[o * channels:(o + 1) * channels, :]
        total = total + jnp.dot(picked.astype(jnp.bfloat16), weight, preferred_element_type=jnp.float32)
    out_ref[...] = total


def conv_wgrad_kernel(post_ref, tablet_ref, grad_ref, wgrad_ref):
    channels = tablet_ref.shape[0]
    table_t = tablet_ref[...]
    grad = grad_ref[...]
    rows = table_t.shape[1]
    sublanes = lax.broadcasted_iota(jnp.int32, (rows, post_ref.shape[1]), 0)
    for o in range(post_ref.shape[0]):
        hot_t = (sublanes == post_ref[o:o + 1, :]).astype(jnp.bfloat16)
        picked_t = jnp.dot(table_t, hot_t, preferred_element_type=jnp.float32).astype(jnp.bfloat16)
        wgrad_ref[o * channels:(o + 1) * channels, :] = jnp.dot(
            picked_t, grad, preferred_element_type=jnp.float32)


def conv_scatter_body(post_ref, grad_ref, w_ref, halo_ref, own_ref):
    channels = grad_ref.shape[1]
    grad = grad_ref[...]
    halo_rows = halo_ref.shape[0] * halo_ref.shape[1]
    rows = halo_rows + own_ref.shape[0]
    sublanes = lax.broadcasted_iota(jnp.int32, (rows, post_ref.shape[1]), 0)
    total = jnp.zeros((rows, 2 * channels), jnp.float32)
    for o in range(post_ref.shape[0]):
        hot_t = (sublanes == post_ref[o:o + 1, :]).astype(jnp.bfloat16)
        weight = w_ref[o * channels:(o + 1) * channels, :]
        spread = lax.dot_general(grad, weight, (((1,), (1,)), ((), ())), preferred_element_type=jnp.float32)
        high = spread.astype(jnp.bfloat16)
        low = (spread - high.astype(jnp.float32)).astype(jnp.bfloat16)
        total = total + jnp.dot(hot_t, jnp.concatenate([high, low], axis=1),
                                preferred_element_type=jnp.float32)
    summed = total[:, :channels] + total[:, channels:]
    halo_ref[...] = summed[:halo_rows].reshape(halo_ref.shape)
    own_ref[...] = summed[halo_rows:]


def _vmem_call(kernel, outs, *args):
    return pl.pallas_call(
        kernel,
        out_shape=outs,
        in_specs=[pl.BlockSpec(memory_space=pltpu.VMEM)] * len(args),
        out_specs=jax.tree.map(lambda _: pl.BlockSpec(memory_space=pltpu.VMEM), outs),
    )(*args)


def on_device(features, neighbours, down_map, w_conv, w_down, coarse_grad):
    voxels, channels = features.shape
    offsets = neighbours.shape[1]
    rim = 64
    absent = neighbours >= 9 * voxels
    slot_idx = neighbours // voxels
    local_idx = neighbours - slot_idx * voxels
    halo_slot = jnp.where(slot_idx < 4, slot_idx, slot_idx - 1)
    compact = jnp.where(slot_idx == 4, 8 * rim + local_idx, halo_slot * rim + local_idx)
    positions = jnp.where(absent, -1, compact).astype(jnp.int32)
    sendable = jnp.broadcast_to(features[None, :rim], (8, rim, channels))
    conv_out, halo = pl.pallas_call(
        conv_fwd_halo_kernel,
        out_shape=(jax.ShapeDtypeStruct((voxels, channels), jnp.float32),
                   jax.ShapeDtypeStruct(sendable.shape, sendable.dtype)),
        in_specs=[pl.BlockSpec(memory_space=pltpu.VMEM)] * 4,
        out_specs=(pl.BlockSpec(memory_space=pltpu.VMEM), pl.BlockSpec(memory_space=pltpu.VMEM)),
        scratch_shapes=[pltpu.SemaphoreType.DMA((8,)), pltpu.SemaphoreType.DMA((8,))],
        compiler_params=pltpu.CompilerParams(collective_id=1, has_side_effects=True),
    )(positions, features, sendable, w_conv)
    table = jnp.concatenate([halo.reshape(8 * rim, channels), features], axis=0)
    table_rows = table.shape[0]
    hidden = (features.astype(jnp.float32) + jax.nn.silu(conv_out)).astype(jnp.bfloat16)
    zero_row = jnp.zeros((1, channels), features.dtype)
    coarse_count, taps = down_map.shape
    down_local = jnp.minimum(down_map, voxels)
    hidden_pad = jnp.concatenate([hidden, zero_row], axis=0)
    coarse_rows = hidden_pad[down_local].reshape(coarse_count, taps * channels)
    coarse = jnp.dot(coarse_rows, w_down, preferred_element_type=jnp.float32).astype(jnp.bfloat16)
    coarse_back = jnp.dot(coarse_grad, w_down.T, preferred_element_type=jnp.float32)
    hidden_grad = jnp.zeros((voxels + 1, channels), jnp.float32)
    hidden_grad = hidden_grad.at[down_local.reshape(-1)].add(coarse_back.reshape(-1, channels))[
        :voxels
    ]
    down_wgrad = lax.dot_general(
        coarse_rows, coarse_grad, (((0,), (0,)), ((), ())), preferred_element_type=jnp.float32
    )
    sigmoid_y = jax.nn.sigmoid(conv_out)
    conv_grad = (hidden_grad * sigmoid_y * (1.0 + conv_out * (1.0 - sigmoid_y))).astype(
        jnp.bfloat16
    )
    conv_wgrad = _vmem_call(
        conv_wgrad_kernel, jax.ShapeDtypeStruct(w_conv.shape, jnp.float32),
        positions.T, table.T, conv_grad)
    (conv_wgrad, down_wgrad), grad_input, _ = summed_everywhere(
        [conv_wgrad, down_wgrad], positions.T, conv_grad, w_conv, hidden_grad, (8, rim, channels), voxels)
    return (coarse, grad_input, conv_wgrad, down_wgrad)


def solution(mesh):
    in_specs = (
        P(("region", "slab"), None),
        P(("region", "slab"), None),
        P(("region", "slab"), None),
        P(),
        P(),
        P(("region", "slab"), None),
    )
    out_specs = (P(("region", "slab"), None), P(("region", "slab"), None), P(), P())
    return jax.shard_map(
        on_device, mesh=mesh, in_specs=in_specs, out_specs=out_specs, check_vma=False
    )
```

```python
import jax
import jax.numpy as jnp
from jax import lax
from jax.experimental import pallas as pl
from jax.experimental.pallas import tpu as pltpu
from jax.sharding import PartitionSpec as P
from jax.experimental import pallas as pl
from jax.experimental.pallas import tpu as pltpu

MESH = pl.DeviceIdType.MESH
HALVINGS = 7
ORDER_A = [0, 4, 7, 1, 5, 8]
ORDER_B = [4, 7, 0, 5, 8, 1]
FULL_A = [2, 6]
FULL_B = [6, 2]


def _bit_partner(region, slab, b):
    if b < 3:
        v = (slab // (1 << b)) % 2
        return v, region, slab + (1 - 2 * v) * (1 << b)
    j = b - 3
    v = (region // (1 << j)) % 2
    return v, region + (1 - 2 * v) * (1 << j), slab


def _step(region, slab, core, ba, bb):
    va, ra, sa = _bit_partner(region, slab, ba)
    vb, rb, sb = _bit_partner(region, slab, bb)
    return va + core * (vb - va), ra + core * (rb - ra), sa + core * (sb - sa)


def allreduce_kernel(x_ref, post_ref, grad_ref, w_ref, hgrad_ref, o_ref, hsrc_ref, own_ref, hout_ref, *scratch):
    HALVES = [x_ref.shape[0] >> (k + 1) for k in range(HALVINGS)]
    recvs = scratch[:9]
    send_sem, recv_sem, free_sem = scratch[9], scratch[10], scratch[11]
    codes, present, targets, hcopies, hcount = _halo_plan(hsrc_ref, hout_ref, scratch[12], scratch[13])
    hout_ref[...] = jnp.zeros(hout_ref.shape, hout_ref.dtype)
    region = lax.axis_index("region")
    slab = lax.axis_index("slab")
    core = region % 2
    steps = [(core, region + 1 - 2 * core, slab)]
    for ba, bb in zip(ORDER_A, ORDER_B):
        steps.append(_step(region, slab, core, ba, bb))
    fulls = [_step(region, slab, core, ba, bb) for ba, bb in zip(FULL_A, FULL_B)]

    barrier = pltpu.get_barrier_semaphore()
    for _, r, s in steps + fulls:
        pl.semaphore_signal(barrier, inc=1, device_id=(r, s), device_id_type=MESH)
    _halo_signal(barrier, codes, present, targets)
    conv_scatter_body(post_ref, grad_ref, w_ref, hsrc_ref, own_ref)
    pl.semaphore_wait(barrier, len(steps) + len(fulls) + hcount)
    _halo_start(codes, present, hcopies)

    off = 0
    offs = []
    for k, (v, r, s) in enumerate(steps):
        size = HALVES[k]
        keep = pl.multiple_of(off + v * size, 8)
        send = pl.multiple_of(off + (1 - v) * size, 8)
        src = x_ref if k == 0 else o_ref
        copy = pltpu.make_async_remote_copy(
            src_ref=src.at[pl.ds(send, size)], dst_ref=recvs[k],
            send_sem=send_sem.at[k], recv_sem=recv_sem.at[k],
            device_id=(r, s), device_id_type=MESH)
        copy.start()
        copy.wait()
        pl.semaphore_signal(free_sem.at[k], inc=1, device_id=(r, s), device_id_type=MESH)
        o_ref[pl.ds(keep, size)] = src[pl.ds(keep, size)] + recvs[k][...]
        off = keep
        offs.append(keep)
    last = HALVES[-1]
    for i, (v, r, s) in enumerate(fulls):
        k = len(steps) + i
        copy = pltpu.make_async_remote_copy(
            src_ref=o_ref.at[pl.ds(off, last)], dst_ref=recvs[k],
            send_sem=send_sem.at[k], recv_sem=recv_sem.at[k],
            device_id=(r, s), device_id_type=MESH)
        copy.start()
        copy.wait()
        o_ref[pl.ds(off, last)] = o_ref[pl.ds(off, last)] + recvs[k][...]
    base = len(steps) + len(fulls)
    for k in reversed(range(len(steps))):
        v, r, s = steps[k]
        size = HALVES[k]
        j = base + (len(steps) - 1 - k)
        copy = pltpu.make_async_remote_copy(
            src_ref=o_ref.at[pl.ds(offs[k], size)], dst_ref=o_ref.at[pl.ds(offs[k], size)],
            send_sem=send_sem.at[j], recv_sem=recv_sem.at[j],
            device_id=(r, s), device_id_type=MESH)
        pl.semaphore_wait(free_sem.at[k], 1)
        copy.start()
        copy.wait()
    _halo_finish(codes, present, hcopies)
    rim = hout_ref.shape[1]
    own_ref[...] = hgrad_ref[...] + own_ref[...]
    own_ref[:rim] = own_ref[:rim] + jnp.sum(hout_ref[...], axis=0)


def allreduce(x, post, grad, w, hgrad, hshape, own_rows):
    rows = x.shape[0]
    HALVES = [rows >> (k + 1) for k in range(HALVINGS)]
    n_copies = 9 + 7
    return pl.pallas_call(
        allreduce_kernel,
        out_shape=(jax.ShapeDtypeStruct((rows, 128), jnp.float32),
                   jax.ShapeDtypeStruct(hshape, jnp.float32),
                   jax.ShapeDtypeStruct((own_rows, hshape[2]), jnp.float32),
                   jax.ShapeDtypeStruct(hshape, jnp.float32)),
        in_specs=[pl.BlockSpec(memory_space=pltpu.VMEM)] * 5,
        out_specs=tuple(pl.BlockSpec(memory_space=pltpu.VMEM) for _ in range(4)),
        scratch_shapes=[pltpu.VMEM((h, 128), jnp.float32) for h in HALVES]
        + [pltpu.VMEM((HALVES[-1], 128), jnp.float32)] * 2
        + [pltpu.SemaphoreType.DMA((n_copies,)), pltpu.SemaphoreType.DMA((n_copies,))]
        + [pltpu.SemaphoreType.REGULAR((HALVINGS,))]
        + [pltpu.SemaphoreType.DMA((8,)), pltpu.SemaphoreType.DMA((8,))],
        compiler_params=pltpu.CompilerParams(collective_id=0, has_side_effects=True),
    )(x, post, grad, w, hgrad)


def summed_everywhere(arrays, post, grad, w, hgrad, hshape, own_rows):
    parts = [a.reshape(-1, 128) for a in arrays]
    unit = 8 << HALVINGS
    used = sum(p.shape[0] for p in parts)
    rows = -(-used // unit) * unit
    padded = jnp.concatenate(parts + [jnp.zeros((rows - used, 128), jnp.float32)], axis=0)
    total, _, own, hout = allreduce(padded, post, grad, w, hgrad, hshape, own_rows)
    out, at = [], 0
    for a, p in zip(arrays, parts):
        out.append(total[at:at + p.shape[0]].reshape(a.shape))
        at += p.shape[0]
    return out, own, hout

def _exists(index, size):
    low = (index + size - 1) // size
    high = (2 * size - 3 - index) // (size - 1)
    return (low, 1, high)


def _halo_plan(src_ref, out_ref, send_sem, recv_sem):
    region = lax.axis_index("region")
    slab = lax.axis_index("slab")
    along_region = _exists(region, lax.axis_size("region"))
    along_slab = _exists(slab, lax.axis_size("slab"))
    codes = [c for c in range(9) if c != 4]
    slot = {c: i for i, c in enumerate(codes)}
    present, targets, copies = {}, {}, {}
    for c in codes:
        present[c] = along_region[c // 3] * along_slab[c % 3]
        targets[c] = (region + c // 3 - 1, slab + c % 3 - 1)
        copies[c] = pltpu.make_async_remote_copy(
            src_ref=src_ref.at[slot[c]], dst_ref=out_ref.at[slot[8 - c]],
            send_sem=send_sem.at[slot[c]], recv_sem=recv_sem.at[slot[8 - c]],
            device_id=targets[c], device_id_type=MESH)
    count = (along_region[0] + 1 + along_region[2]) * (along_slab[0] + 1 + along_slab[2]) - 1
    return codes, present, targets, copies, count


def _halo_signal(barrier, codes, present, targets):
    for c in codes:
        @pl.when(present[c] == 1)
        def _():
            pl.semaphore_signal(barrier, inc=1, device_id=targets[c], device_id_type=MESH)


def _halo_start(codes, present, copies):
    for c in codes:
        @pl.when(present[c] == 1)
        def _():
            copies[c].start()


def _halo_finish(codes, present, copies):
    for c in codes:
        @pl.when(present[c] == 1)
        def _():
            copies[8 - c].wait_recv()
            copies[c].wait_send()


def halo_kernel(src_ref, out_ref, send_sem, recv_sem):
    codes, present, targets, copies, count = _halo_plan(src_ref, out_ref, send_sem, recv_sem)
    out_ref[...] = jnp.zeros(out_ref.shape, out_ref.dtype)
    barrier = pltpu.get_barrier_semaphore()
    _halo_signal(barrier, codes, present, targets)
    pl.semaphore_wait(barrier, count)
    _halo_start(codes, present, copies)
    _halo_finish(codes, present, copies)


def halo_exchange(src, cid):
    return pl.pallas_call(
        halo_kernel,
        out_shape=jax.ShapeDtypeStruct(src.shape, src.dtype),
        in_specs=[pl.BlockSpec(memory_space=pltpu.VMEM)],
        out_specs=pl.BlockSpec(memory_space=pltpu.VMEM),
        scratch_shapes=[pltpu.SemaphoreType.DMA((8,)), pltpu.SemaphoreType.DMA((8,))],
        compiler_params=pltpu.CompilerParams(collective_id=cid, has_side_effects=True),
    )(src)


def extended_2(block, sides, width):
    for axis, dim in sides:
        count = lax.axis_size(axis)
        forward = [(i, i + 1) for i in range(count - 1)]
        backward = [(target, source) for source, target in forward]
        low = lax.ppermute(
            lax.slice_in_dim(block, block.shape[dim] - width, None, axis=dim), axis, forward
        )
        high = lax.ppermute(lax.slice_in_dim(block, 0, width, axis=dim), axis, backward)
        block = jnp.concatenate([low, block, high], axis=dim)
    return block


def _one_hot(pos_ref, o, rows):
    column = pos_ref[:, o:o + 1]
    lanes = lax.broadcasted_iota(jnp.int32, (column.shape[0], rows), 1)
    return (column == lanes).astype(jnp.bfloat16)


def conv_fwd_kernel(pos_ref, table_ref, w_ref, out_ref):
    channels = table_ref.shape[1]
    table = table_ref[...]
    total = jnp.zeros(out_ref.shape, jnp.float32)
    for o in range(pos_ref.shape[1]):
        picked = jnp.dot(_one_hot(pos_ref, o, table.shape[0]), table, preferred_element_type=jnp.float32)
        weight = w_ref[o * channels:(o + 1) * channels, :]
        total = total + jnp.dot(picked.astype(jnp.bfloat16), weight, preferred_element_type=jnp.float32)
    out_ref[...] = total


def conv_fwd_halo_kernel(pos_ref, own_ref, src_ref, w_ref, out_ref, hout_ref, send_sem, recv_sem):
    channels = own_ref.shape[1]
    voxels = own_ref.shape[0]
    halo_rows = hout_ref.shape[0] * hout_ref.shape[1]
    codes, present, targets, copies, count = _halo_plan(src_ref, hout_ref, send_sem, recv_sem)
    hout_ref[...] = jnp.zeros(hout_ref.shape, hout_ref.dtype)
    barrier = pltpu.get_barrier_semaphore()
    _halo_signal(barrier, codes, present, targets)
    pl.semaphore_wait(barrier, count)
    _halo_start(codes, present, copies)
    own = own_ref[...]
    own_lanes = lax.broadcasted_iota(jnp.int32, (pos_ref.shape[0], voxels), 1) + halo_rows
    total = jnp.zeros(out_ref.shape, jnp.float32)
    for o in range(pos_ref.shape[1]):
        hot = (pos_ref[:, o:o + 1] == own_lanes).astype(jnp.bfloat16)
        picked = jnp.dot(hot, own, preferred_element_type=jnp.float32)
        weight = w_ref[o * channels:(o + 1) * channels, :]
        total = total + jnp.dot(picked.astype(jnp.bfloat16), weight, preferred_element_type=jnp.float32)
    _halo_finish(codes, present, copies)
    halo = hout_ref[...].reshape(halo_rows, channels)
    for o in range(pos_ref.shape[1]):
        picked = jnp.dot(_one_hot(pos_ref, o, halo_rows), halo, preferred_element_type=jnp.float32)
        weight = w_ref[o * channels:(o + 1) * channels, :]
        total = total + jnp.dot(picked.astype(jnp.bfloat16), weight, preferred_element_type=jnp.float32)
    out_ref[...] = total


def conv_wgrad_kernel(post_ref, tablet_ref, grad_ref, wgrad_ref):
    channels = tablet_ref.shape[0]
    table_t = tablet_ref[...]
    grad = grad_ref[...]
    rows = table_t.shape[1]
    sublanes = lax.broadcasted_iota(jnp.int32, (rows, post_ref.shape[1]), 0)
    for o in range(post_ref.shape[0]):
        hot_t = (sublanes == post_ref[o:o + 1, :]).astype(jnp.bfloat16)
        picked_t = jnp.dot(table_t, hot_t, preferred_element_type=jnp.float32).astype(jnp.bfloat16)
        wgrad_ref[o * channels:(o + 1) * channels, :] = jnp.dot(
            picked_t, grad, preferred_element_type=jnp.float32)


def conv_scatter_body(post_ref, grad_ref, w_ref, halo_ref, own_ref):
    channels = grad_ref.shape[1]
    grad = grad_ref[...]
    halo_rows = halo_ref.shape[0] * halo_ref.shape[1]
    rows = halo_rows + own_ref.shape[0]
    sublanes = lax.broadcasted_iota(jnp.int32, (rows, post_ref.shape[1]), 0)
    total = jnp.zeros((rows, 2 * channels), jnp.float32)
    for o in range(post_ref.shape[0]):
        hot_t = (sublanes == post_ref[o:o + 1, :]).astype(jnp.bfloat16)
        weight = w_ref[o * channels:(o + 1) * channels, :]
        spread = lax.dot_general(grad, weight, (((1,), (1,)), ((), ())), preferred_element_type=jnp.float32)
        high = spread.astype(jnp.bfloat16)
        low = (spread - high.astype(jnp.float32)).astype(jnp.bfloat16)
        total = total + jnp.dot(hot_t, jnp.concatenate([high, low], axis=1),
                                preferred_element_type=jnp.float32)
    summed = total[:, :channels] + total[:, channels:]
    halo_ref[...] = summed[:halo_rows].reshape(halo_ref.shape)
    own_ref[...] = summed[halo_rows:]


def _vmem_call(kernel, outs, *args):
    return pl.pallas_call(
        kernel,
        out_shape=outs,
        in_specs=[pl.BlockSpec(memory_space=pltpu.VMEM)] * len(args),
        out_specs=jax.tree.map(lambda _: pl.BlockSpec(memory_space=pltpu.VMEM), outs),
    )(*args)


def on_device(features, neighbours, down_map, w_conv, w_down, coarse_grad):
    voxels, channels = features.shape
    offsets = neighbours.shape[1]
    rim = 64
    absent = neighbours >= 9 * voxels
    slot_idx = neighbours // voxels
    local_idx = neighbours - slot_idx * voxels
    halo_slot = jnp.where(slot_idx < 4, slot_idx, slot_idx - 1)
    compact = jnp.where(slot_idx == 4, 8 * rim + local_idx, halo_slot * rim + local_idx)
    positions = jnp.where(absent, -1, compact).astype(jnp.int32)
    sendable = jnp.broadcast_to(features[None, :rim], (8, rim, channels))
    conv_out, halo = pl.pallas_call(
        conv_fwd_halo_kernel,
        out_shape=(jax.ShapeDtypeStruct((voxels, channels), jnp.float32),
                   jax.ShapeDtypeStruct(sendable.shape, sendable.dtype)),
        in_specs=[pl.BlockSpec(memory_space=pltpu.VMEM)] * 4,
        out_specs=(pl.BlockSpec(memory_space=pltpu.VMEM), pl.BlockSpec(memory_space=pltpu.VMEM)),
        scratch_shapes=[pltpu.SemaphoreType.DMA((8,)), pltpu.SemaphoreType.DMA((8,))],
        compiler_params=pltpu.CompilerParams(collective_id=1, has_side_effects=True),
    )(positions, features, sendable, w_conv)
    table = jnp.concatenate([halo.reshape(8 * rim, channels), features], axis=0)
    table_rows = table.shape[0]
    hidden = (features.astype(jnp.float32) + jax.nn.silu(conv_out)).astype(jnp.bfloat16)
    zero_row = jnp.zeros((1, channels), features.dtype)
    coarse_count, taps = down_map.shape
    down_local = jnp.minimum(down_map, voxels)
    hidden_pad = jnp.concatenate([hidden, zero_row], axis=0)
    coarse_rows = hidden_pad[down_local].reshape(coarse_count, taps * channels)
    coarse = jnp.dot(coarse_rows, w_down, preferred_element_type=jnp.float32).astype(jnp.bfloat16)
    coarse_back = jnp.dot(coarse_grad, w_down.T, preferred_element_type=jnp.float32)
    hidden_grad = jnp.zeros((voxels + 1, channels), jnp.float32)
    hidden_grad = hidden_grad.at[down_local.reshape(-1)].add(coarse_back.reshape(-1, channels))[
        :voxels
    ]
    down_wgrad = lax.dot_general(
        coarse_rows, coarse_grad, (((0,), (0,)), ((), ())), preferred_element_type=jnp.float32
    )
    sigmoid_y = jax.nn.sigmoid(conv_out)
    conv_grad = (hidden_grad * sigmoid_y * (1.0 + conv_out * (1.0 - sigmoid_y))).astype(
        jnp.bfloat16
    )
    conv_wgrad = _vmem_call(
        conv_wgrad_kernel, jax.ShapeDtypeStruct(w_conv.shape, jnp.float32),
        positions.T, table.T, conv_grad)
    (conv_wgrad, down_wgrad), grad_input, _ = summed_everywhere(
        [conv_wgrad, down_wgrad], positions.T, conv_grad, w_conv, hidden_grad, (8, rim, channels), voxels)
    return (coarse, grad_input, conv_wgrad, down_wgrad)


def solution(mesh):
    in_specs = (
        P(("region", "slab"), None),
        P(("region", "slab"), None),
        P(("region", "slab"), None),
        P(),
        P(),
        P(("region", "slab"), None),
    )
    out_specs = (P(("region", "slab"), None), P(("region", "slab"), None), P(), P())
    return jax.shard_map(
        on_device, mesh=mesh, in_specs=in_specs, out_specs=out_specs, check_vma=False
    )
```

```python
import jax
import jax.numpy as jnp
from jax import lax
from jax.experimental import pallas as pl
from jax.experimental.pallas import tpu as pltpu
from jax.sharding import PartitionSpec as P
from jax.experimental import pallas as pl
from jax.experimental.pallas import tpu as pltpu

MESH = pl.DeviceIdType.MESH
HALVINGS = 7
ORDER_A = [0, 4, 7, 1, 5, 8]
ORDER_B = [4, 7, 0, 5, 8, 1]
FULL_A = [2, 6]
FULL_B = [6, 2]


def _bit_partner(region, slab, b):
    if b < 3:
        v = (slab // (1 << b)) % 2
        return v, region, slab + (1 - 2 * v) * (1 << b)
    j = b - 3
    v = (region // (1 << j)) % 2
    return v, region + (1 - 2 * v) * (1 << j), slab


def _step(region, slab, core, ba, bb):
    va, ra, sa = _bit_partner(region, slab, ba)
    vb, rb, sb = _bit_partner(region, slab, bb)
    return va + core * (vb - va), ra + core * (rb - ra), sa + core * (sb - sa)


def allreduce_kernel(x_ref, post_ref, grad_ref, w_ref, hgrad_ref, o_ref, hsrc_ref, own_ref, hout_ref, *scratch):
    HALVES = [x_ref.shape[0] >> (k + 1) for k in range(HALVINGS)]
    recvs = scratch[:9]
    send_sem, recv_sem, free_sem = scratch[9], scratch[10], scratch[11]
    codes, present, targets, hcopies, hcount = _halo_plan(hsrc_ref, hout_ref, scratch[12], scratch[13])
    hout_ref[...] = jnp.zeros(hout_ref.shape, hout_ref.dtype)
    region = lax.axis_index("region")
    slab = lax.axis_index("slab")
    core = region % 2
    steps = [(core, region + 1 - 2 * core, slab)]
    for ba, bb in zip(ORDER_A, ORDER_B):
        steps.append(_step(region, slab, core, ba, bb))
    fulls = [_step(region, slab, core, ba, bb) for ba, bb in zip(FULL_A, FULL_B)]

    barrier = pltpu.get_barrier_semaphore()
    for _, r, s in steps + fulls:
        pl.semaphore_signal(barrier, inc=1, device_id=(r, s), device_id_type=MESH)
    _halo_signal(barrier, codes, present, targets)
    conv_scatter_body(post_ref, grad_ref, w_ref, hsrc_ref, own_ref)
    pl.semaphore_wait(barrier, len(steps) + len(fulls) + hcount)

    off = 0
    offs = []
    for k, (v, r, s) in enumerate(steps):
        size = HALVES[k]
        keep = pl.multiple_of(off + v * size, 8)
        send = pl.multiple_of(off + (1 - v) * size, 8)
        src = x_ref if k == 0 else o_ref
        copy = pltpu.make_async_remote_copy(
            src_ref=src.at[pl.ds(send, size)], dst_ref=recvs[k],
            send_sem=send_sem.at[k], recv_sem=recv_sem.at[k],
            device_id=(r, s), device_id_type=MESH)
        copy.start()
        copy.wait()
        pl.semaphore_signal(free_sem.at[k], inc=1, device_id=(r, s), device_id_type=MESH)
        o_ref[pl.ds(keep, size)] = src[pl.ds(keep, size)] + recvs[k][...]
        off = keep
        offs.append(keep)
    _halo_start(codes, present, hcopies)
    last = HALVES[-1]
    for i, (v, r, s) in enumerate(fulls):
        k = len(steps) + i
        copy = pltpu.make_async_remote_copy(
            src_ref=o_ref.at[pl.ds(off, last)], dst_ref=recvs[k],
            send_sem=send_sem.at[k], recv_sem=recv_sem.at[k],
            device_id=(r, s), device_id_type=MESH)
        copy.start()
        copy.wait()
        o_ref[pl.ds(off, last)] = o_ref[pl.ds(off, last)] + recvs[k][...]
    base = len(steps) + len(fulls)
    for k in reversed(range(len(steps))):
        v, r, s = steps[k]
        size = HALVES[k]
        j = base + (len(steps) - 1 - k)
        copy = pltpu.make_async_remote_copy(
            src_ref=o_ref.at[pl.ds(offs[k], size)], dst_ref=o_ref.at[pl.ds(offs[k], size)],
            send_sem=send_sem.at[j], recv_sem=recv_sem.at[j],
            device_id=(r, s), device_id_type=MESH)
        pl.semaphore_wait(free_sem.at[k], 1)
        copy.start()
        copy.wait()
    _halo_finish(codes, present, hcopies)
    rim = hout_ref.shape[1]
    own_ref[...] = hgrad_ref[...] + own_ref[...]
    own_ref[:rim] = own_ref[:rim] + jnp.sum(hout_ref[...], axis=0)


def allreduce(x, post, grad, w, hgrad, hshape, own_rows):
    rows = x.shape[0]
    HALVES = [rows >> (k + 1) for k in range(HALVINGS)]
    n_copies = 9 + 7
    return pl.pallas_call(
        allreduce_kernel,
        out_shape=(jax.ShapeDtypeStruct((rows, 128), jnp.float32),
                   jax.ShapeDtypeStruct(hshape, jnp.float32),
                   jax.ShapeDtypeStruct((own_rows, hshape[2]), jnp.float32),
                   jax.ShapeDtypeStruct(hshape, jnp.float32)),
        in_specs=[pl.BlockSpec(memory_space=pltpu.VMEM)] * 5,
        out_specs=tuple(pl.BlockSpec(memory_space=pltpu.VMEM) for _ in range(4)),
        scratch_shapes=[pltpu.VMEM((h, 128), jnp.float32) for h in HALVES]
        + [pltpu.VMEM((HALVES[-1], 128), jnp.float32)] * 2
        + [pltpu.SemaphoreType.DMA((n_copies,)), pltpu.SemaphoreType.DMA((n_copies,))]
        + [pltpu.SemaphoreType.REGULAR((HALVINGS,))]
        + [pltpu.SemaphoreType.DMA((8,)), pltpu.SemaphoreType.DMA((8,))],
        compiler_params=pltpu.CompilerParams(collective_id=0, has_side_effects=True),
    )(x, post, grad, w, hgrad)


def summed_everywhere(arrays, post, grad, w, hgrad, hshape, own_rows):
    flat = jnp.concatenate([a.reshape(-1) for a in arrays])
    unit = 128 * 8 << HALVINGS
    rows = -(-flat.size // unit) * unit // 128
    padded = jnp.pad(flat, (0, rows * 128 - flat.size)).reshape(rows, 128)
    total, _, own, hout = allreduce(padded, post, grad, w, hgrad, hshape, own_rows)
    total = total.reshape(-1)
    out, at = [], 0
    for a in arrays:
        out.append(total[at:at + a.size].reshape(a.shape))
        at += a.size
    return out, own, hout


def _exists(index, size):
    low = (index + size - 1) // size
    high = (2 * size - 3 - index) // (size - 1)
    return (low, 1, high)


def _halo_plan(src_ref, out_ref, send_sem, recv_sem):
    region = lax.axis_index("region")
    slab = lax.axis_index("slab")
    along_region = _exists(region, lax.axis_size("region"))
    along_slab = _exists(slab, lax.axis_size("slab"))
    codes = [c for c in range(9) if c != 4]
    slot = {c: i for i, c in enumerate(codes)}
    present, targets, copies = {}, {}, {}
    for c in codes:
        present[c] = along_region[c // 3] * along_slab[c % 3]
        targets[c] = (region + c // 3 - 1, slab + c % 3 - 1)
        copies[c] = pltpu.make_async_remote_copy(
            src_ref=src_ref.at[slot[c]], dst_ref=out_ref.at[slot[8 - c]],
            send_sem=send_sem.at[slot[c]], recv_sem=recv_sem.at[slot[8 - c]],
            device_id=targets[c], device_id_type=MESH)
    count = (along_region[0] + 1 + along_region[2]) * (along_slab[0] + 1 + along_slab[2]) - 1
    return codes, present, targets, copies, count


def _halo_signal(barrier, codes, present, targets):
    for c in codes:
        @pl.when(present[c] == 1)
        def _():
            pl.semaphore_signal(barrier, inc=1, device_id=targets[c], device_id_type=MESH)


def _halo_start(codes, present, copies):
    for c in codes:
        @pl.when(present[c] == 1)
        def _():
            copies[c].start()


def _halo_finish(codes, present, copies):
    for c in codes:
        @pl.when(present[c] == 1)
        def _():
            copies[8 - c].wait_recv()
            copies[c].wait_send()


def halo_kernel(src_ref, out_ref, send_sem, recv_sem):
    codes, present, targets, copies, count = _halo_plan(src_ref, out_ref, send_sem, recv_sem)
    out_ref[...] = jnp.zeros(out_ref.shape, out_ref.dtype)
    barrier = pltpu.get_barrier_semaphore()
    _halo_signal(barrier, codes, present, targets)
    pl.semaphore_wait(barrier, count)
    _halo_start(codes, present, copies)
    _halo_finish(codes, present, copies)


def halo_exchange(src, cid):
    return pl.pallas_call(
        halo_kernel,
        out_shape=jax.ShapeDtypeStruct(src.shape, src.dtype),
        in_specs=[pl.BlockSpec(memory_space=pltpu.VMEM)],
        out_specs=pl.BlockSpec(memory_space=pltpu.VMEM),
        scratch_shapes=[pltpu.SemaphoreType.DMA((8,)), pltpu.SemaphoreType.DMA((8,))],
        compiler_params=pltpu.CompilerParams(collective_id=cid, has_side_effects=True),
    )(src)


def extended_2(block, sides, width):
    for axis, dim in sides:
        count = lax.axis_size(axis)
        forward = [(i, i + 1) for i in range(count - 1)]
        backward = [(target, source) for source, target in forward]
        low = lax.ppermute(
            lax.slice_in_dim(block, block.shape[dim] - width, None, axis=dim), axis, forward
        )
        high = lax.ppermute(lax.slice_in_dim(block, 0, width, axis=dim), axis, backward)
        block = jnp.concatenate([low, block, high], axis=dim)
    return block


def _one_hot(pos_ref, o, rows):
    column = pos_ref[:, o:o + 1]
    lanes = lax.broadcasted_iota(jnp.int32, (column.shape[0], rows), 1)
    return (column == lanes).astype(jnp.bfloat16)


def conv_fwd_kernel(pos_ref, table_ref, w_ref, out_ref):
    channels = table_ref.shape[1]
    table = table_ref[...]
    total = jnp.zeros(out_ref.shape, jnp.float32)
    for o in range(pos_ref.shape[1]):
        picked = jnp.dot(_one_hot(pos_ref, o, table.shape[0]), table, preferred_element_type=jnp.float32)
        weight = w_ref[o * channels:(o + 1) * channels, :]
        total = total + jnp.dot(picked.astype(jnp.bfloat16), weight, preferred_element_type=jnp.float32)
    out_ref[...] = total


def conv_fwd_halo_kernel(pos_ref, own_ref, src_ref, w_ref, out_ref, hout_ref, send_sem, recv_sem):
    channels = own_ref.shape[1]
    voxels = own_ref.shape[0]
    halo_rows = hout_ref.shape[0] * hout_ref.shape[1]
    codes, present, targets, copies, count = _halo_plan(src_ref, hout_ref, send_sem, recv_sem)
    hout_ref[...] = jnp.zeros(hout_ref.shape, hout_ref.dtype)
    barrier = pltpu.get_barrier_semaphore()
    _halo_signal(barrier, codes, present, targets)
    pl.semaphore_wait(barrier, count)
    _halo_start(codes, present, copies)
    own = own_ref[...]
    own_lanes = lax.broadcasted_iota(jnp.int32, (pos_ref.shape[0], voxels), 1) + halo_rows
    total = jnp.zeros(out_ref.shape, jnp.float32)
    for o in range(pos_ref.shape[1]):
        hot = (pos_ref[:, o:o + 1] == own_lanes).astype(jnp.bfloat16)
        picked = jnp.dot(hot, own, preferred_element_type=jnp.float32)
        weight = w_ref[o * channels:(o + 1) * channels, :]
        total = total + jnp.dot(picked.astype(jnp.bfloat16), weight, preferred_element_type=jnp.float32)
    _halo_finish(codes, present, copies)
    halo = hout_ref[...].reshape(halo_rows, channels)
    for o in range(pos_ref.shape[1]):
        picked = jnp.dot(_one_hot(pos_ref, o, halo_rows), halo, preferred_element_type=jnp.float32)
        weight = w_ref[o * channels:(o + 1) * channels, :]
        total = total + jnp.dot(picked.astype(jnp.bfloat16), weight, preferred_element_type=jnp.float32)
    out_ref[...] = total


def conv_wgrad_kernel(post_ref, tablet_ref, grad_ref, wgrad_ref):
    channels = tablet_ref.shape[0]
    table_t = tablet_ref[...]
    grad = grad_ref[...]
    rows = table_t.shape[1]
    sublanes = lax.broadcasted_iota(jnp.int32, (rows, post_ref.shape[1]), 0)
    for o in range(post_ref.shape[0]):
        hot_t = (sublanes == post_ref[o:o + 1, :]).astype(jnp.bfloat16)
        picked_t = jnp.dot(table_t, hot_t, preferred_element_type=jnp.float32).astype(jnp.bfloat16)
        wgrad_ref[o * channels:(o + 1) * channels, :] = jnp.dot(
            picked_t, grad, preferred_element_type=jnp.float32)


def conv_scatter_body(post_ref, grad_ref, w_ref, halo_ref, own_ref):
    channels = grad_ref.shape[1]
    grad = grad_ref[...]
    halo_rows = halo_ref.shape[0] * halo_ref.shape[1]
    rows = halo_rows + own_ref.shape[0]
    sublanes = lax.broadcasted_iota(jnp.int32, (rows, post_ref.shape[1]), 0)
    total = jnp.zeros((rows, 2 * channels), jnp.float32)
    for o in range(post_ref.shape[0]):
        hot_t = (sublanes == post_ref[o:o + 1, :]).astype(jnp.bfloat16)
        weight = w_ref[o * channels:(o + 1) * channels, :]
        spread = lax.dot_general(grad, weight, (((1,), (1,)), ((), ())), preferred_element_type=jnp.float32)
        high = spread.astype(jnp.bfloat16)
        low = (spread - high.astype(jnp.float32)).astype(jnp.bfloat16)
        total = total + jnp.dot(hot_t, jnp.concatenate([high, low], axis=1),
                                preferred_element_type=jnp.float32)
    summed = total[:, :channels] + total[:, channels:]
    halo_ref[...] = summed[:halo_rows].reshape(halo_ref.shape)
    own_ref[...] = summed[halo_rows:]


def _vmem_call(kernel, outs, *args):
    return pl.pallas_call(
        kernel,
        out_shape=outs,
        in_specs=[pl.BlockSpec(memory_space=pltpu.VMEM)] * len(args),
        out_specs=jax.tree.map(lambda _: pl.BlockSpec(memory_space=pltpu.VMEM), outs),
    )(*args)


def on_device(features, neighbours, down_map, w_conv, w_down, coarse_grad):
    voxels, channels = features.shape
    offsets = neighbours.shape[1]
    rim = 64
    absent = neighbours >= 9 * voxels
    slot_idx = neighbours // voxels
    local_idx = neighbours - slot_idx * voxels
    halo_slot = jnp.where(slot_idx < 4, slot_idx, slot_idx - 1)
    compact = jnp.where(slot_idx == 4, 8 * rim + local_idx, halo_slot * rim + local_idx)
    positions = jnp.where(absent, -1, compact).astype(jnp.int32)
    sendable = jnp.broadcast_to(features[None, :rim], (8, rim, channels))
    conv_out, halo = pl.pallas_call(
        conv_fwd_halo_kernel,
        out_shape=(jax.ShapeDtypeStruct((voxels, channels), jnp.float32),
                   jax.ShapeDtypeStruct(sendable.shape, sendable.dtype)),
        in_specs=[pl.BlockSpec(memory_space=pltpu.VMEM)] * 4,
        out_specs=(pl.BlockSpec(memory_space=pltpu.VMEM), pl.BlockSpec(memory_space=pltpu.VMEM)),
        scratch_shapes=[pltpu.SemaphoreType.DMA((8,)), pltpu.SemaphoreType.DMA((8,))],
        compiler_params=pltpu.CompilerParams(collective_id=1, has_side_effects=True),
    )(positions, features, sendable, w_conv)
    table = jnp.concatenate([halo.reshape(8 * rim, channels), features], axis=0)
    table_rows = table.shape[0]
    hidden = (features.astype(jnp.float32) + jax.nn.silu(conv_out)).astype(jnp.bfloat16)
    zero_row = jnp.zeros((1, channels), features.dtype)
    coarse_count, taps = down_map.shape
    down_local = jnp.minimum(down_map, voxels)
    hidden_pad = jnp.concatenate([hidden, zero_row], axis=0)
    coarse_rows = hidden_pad[down_local].reshape(coarse_count, taps * channels)
    coarse = jnp.dot(coarse_rows, w_down, preferred_element_type=jnp.float32).astype(jnp.bfloat16)
    coarse_back = jnp.dot(coarse_grad, w_down.T, preferred_element_type=jnp.float32)
    hidden_grad = jnp.zeros((voxels + 1, channels), jnp.float32)
    hidden_grad = hidden_grad.at[down_local.reshape(-1)].add(coarse_back.reshape(-1, channels))[
        :voxels
    ]
    down_wgrad = lax.dot_general(
        coarse_rows, coarse_grad, (((0,), (0,)), ((), ())), preferred_element_type=jnp.float32
    )
    sigmoid_y = jax.nn.sigmoid(conv_out)
    conv_grad = (hidden_grad * sigmoid_y * (1.0 + conv_out * (1.0 - sigmoid_y))).astype(
        jnp.bfloat16
    )
    conv_wgrad = _vmem_call(
        conv_wgrad_kernel, jax.ShapeDtypeStruct(w_conv.shape, jnp.float32),
        positions.T, table.T, conv_grad)
    (conv_wgrad, down_wgrad), grad_input, _ = summed_everywhere(
        [conv_wgrad, down_wgrad], positions.T, conv_grad, w_conv, hidden_grad, (8, rim, channels), voxels)
    return (coarse, grad_input, conv_wgrad, down_wgrad)


def solution(mesh):
    in_specs = (
        P(("region", "slab"), None),
        P(("region", "slab"), None),
        P(("region", "slab"), None),
        P(),
        P(),
        P(("region", "slab"), None),
    )
    out_specs = (P(("region", "slab"), None), P(("region", "slab"), None), P(), P())
    return jax.shard_map(
        on_device, mesh=mesh, in_specs=in_specs, out_specs=out_specs, check_vma=False
    )
```
